32 devices in a mesh: slab: 2 (over x), inline: 8 (over z, y), xline: 2 (over core).
Axes of the slice: x: 2, y: 2, z: 4, core: 2. Of those that a mesh axis runs over, the one named last changes fastest.
Arguments:
- traces: bfloat16 [256, 48, 128], P(('slab', 'inline'), 'xline'), parts along dimension 0, may hold values from -15 to 15
- directions: int32 [10], replicated, may hold values from 0 to 31
- init_means: float32 [32, 20], replicated, may hold values from 0.3 to 2.5
- init_variances: float32 [32, 20], replicated, may hold values from 0.01 to 0.2
- init_weights: float32 [32], replicated, may hold values from 0.01 to 1
Outputs:
- posterior: bfloat16 [256, 32, 48, 128], P(('slab', 'inline'), None, 'xline'), parts along dimension 0
- final_means: float32 [64, 20], P('slab'), parts along dimension 0
- final_variances: float32 [64, 20], P('slab'), parts along dimension 0
- final_weights: float32 [64], P('slab'), parts along dimension 0
The draws below stay inside these ranges and needn't reach their ends.
There are 2 independent parts, one for each index of `slab`. The reference program is written for one: setup_inputs(seed, part) draws one part's arguments, and reference() takes and returns one part's arrays. A program takes and returns all parts, laid end to end along the dimension named above; an argument that names none is the same for every part. Nothing has to cross between parts.
All inputs are finite; a program needn't handle non-finite values.
Results may differ from the reference program's by a relative error of at most 0.001.
The reference program's roundings to bfloat16 on the way count: a program that leaves them out, or rounds other values in their place, can miss the bound.
Values may be sent and summed in bfloat16 or wider, within the bound.
A program may use at most 64 MiB of HBM per device.

```python
import math
import jax
import jax.numpy as jnp
import numpy as np
from jax import lax

NT = 128
ORIENTS = 10
FEATS = 20
K = 32
TAPS = 31
HALF = 15
AZIMUTHS = 8
DIPS = 4
ITERS = 2
NI = 128
NX = 48
CELLS = 786432


def draw_traces(key, part):
    position = jnp.arange(NI).astype(jnp.float32) / max(NI - 1, 1)
    drawn_values = jnp.clip(jax.random.normal(key, (NI, NX, NT), jnp.float32), -5.0, 5.0)
    amplitude = 3.0 ** position
    return jnp.clip(drawn_values * amplitude[:, None, None], -15.0, 15.0).astype(jnp.bfloat16)


def set_ends(values, key, smallest, high):
    shape = values.shape
    place = [jax.random.randint(jax.random.fold_in(key, axis), (), 0, shape[axis]) for axis in range(len(shape))]
    values = values.at[tuple(place)].set(smallest)
    longest = shape.index(max(shape))
    place[longest] = (place[longest] + 1) % shape[longest]
    return values.at[tuple(place)].set(high)


def setup_inputs(seed: int = 0, part: int = 0) -> dict:
    seeds = jax.random.split(jax.random.key(seed), 6)
    part_keys = jax.random.split(jax.random.fold_in(seeds[5], part), 6)
    return {
        "traces": draw_traces(jax.random.fold_in(jax.random.fold_in(seeds[5], part), 71), part),
        "directions": set_ends(jax.random.randint(seeds[1], (ORIENTS,), 0, AZIMUTHS * DIPS), jax.random.fold_in(seeds[1], 1), 0, (AZIMUTHS * DIPS) - 1).astype(jnp.int32),
        "init_means": jnp.clip(jax.random.uniform(seeds[2], (K, FEATS), jnp.float32, 0.3, 2.5), 0.3, 2.5),
        "init_variances": jnp.clip(jnp.exp(jax.random.uniform(seeds[3], (K, FEATS), jnp.float32, math.log(0.01), math.log(0.2))), 0.01, 0.2),
        "init_weights": jnp.clip(jnp.exp(jax.random.uniform(seeds[4], (K,), jnp.float32, math.log(0.01), math.log(1.0))), 0.01, 1.0),
    }


eps_mag = 0.01
wavenumber = math.pi / 4.0
highest = lax.Precision.HIGHEST
cross_real = np.array([[[1.0, 0.0], [1.0, 0.0]], [[0.0, 1.0], [0.0, -1.0]]], np.float32)
cross_imag = np.array([[[0.0, 1.0], [0.0, 1.0]], [[-1.0, 0.0], [1.0, 0.0]]], np.float32)

def tap_table(directions):
    azimuth = (directions % AZIMUTHS).astype(jnp.float32) * (math.pi / AZIMUTHS)
    dip_angle = (directions // AZIMUTHS + 1).astype(jnp.float32) * (math.pi / (2 * DIPS + 2))
    wave_vector = wavenumber * jnp.stack([jnp.sin(dip_angle) * jnp.cos(azimuth), jnp.sin(dip_angle) * jnp.sin(azimuth), jnp.cos(dip_angle)], axis=1)
    offsets = jnp.arange(TAPS).astype(jnp.float32) - HALF
    width_scale = HALF / 3.0
    envelope = jnp.exp(-offsets * offsets / (2.0 * width_scale * width_scale))
    envelope = envelope / jnp.sqrt(jnp.sum(envelope * envelope))
    phases = wave_vector[:, :, None] * offsets[None, None, :]
    return jnp.stack([envelope * jnp.cos(phases), envelope * jnp.sin(phases)], axis=2).astype(jnp.bfloat16)

def band_onehot(rows_in, rows_out, offset_base):
    difference = jnp.arange(rows_in).astype(jnp.int32)[:, None] - jnp.arange(rows_out).astype(jnp.int32)[None, :] + offset_base
    return (difference[:, :, None] == jnp.arange(TAPS).astype(jnp.int32)[None, None, :]).astype(jnp.float32)

def log_scores(feature_rows, centers, spreads, log_weights):
    inverse = 1.0 / spreads
    offset_term = log_weights - 0.5 * lax.optimization_barrier(jnp.sum(jnp.log(2.0 * math.pi * spreads), axis=1))
    distance = lax.optimization_barrier(jnp.sum((feature_rows[None, :, :] - centers[:, :, None]) ** 2 * inverse[:, :, None], axis=1))
    return offset_term[:, None] - 0.5 * distance

def posterior_weights(feature_rows, centers, spreads, log_weights):
    scores = log_scores(feature_rows, centers, spreads, log_weights)
    largest = lax.optimization_barrier(jnp.max(scores, axis=0, keepdims=True))
    exponent = jnp.exp(scores - largest)
    return exponent / lax.optimization_barrier(jnp.sum(exponent, axis=0, keepdims=True))

def first_pass(feature_rows, centers, spreads, log_weights):
    posterior = posterior_weights(feature_rows, centers, spreads, log_weights)
    return (posterior.astype(jnp.bfloat16), lax.optimization_barrier(jnp.sum(posterior, axis=1)), jnp.einsum('km,fm->kf', posterior, feature_rows, precision=highest))

def centred_pass(feature_rows, centers, spreads, log_weights, new_centers):
    posterior = posterior_weights(feature_rows, centers, spreads, log_weights)
    return lax.optimization_barrier(jnp.sum(posterior[:, None, :] * (feature_rows[None, :, :] - new_centers[:, :, None]) ** 2, axis=2))

def reference(traces, directions, init_means, init_variances, init_weights):
    tap_values = tap_table(directions)
    wide_taps = tap_values.astype(jnp.float32)
    time_mats = jnp.einsum('stn,orn->osrt', band_onehot(NT, NT, HALF), wide_taps[:, 2], precision=highest).astype(jnp.bfloat16)
    xline_taps = jnp.einsum('pqr,on->opqrn', cross_real, wide_taps[:, 1, 0]) + jnp.einsum('pqr,on->opqrn', cross_imag, wide_taps[:, 1, 1])
    xline_mats = jnp.einsum('xyn,opqrn->oxpqry', band_onehot(NX, NX, HALF), xline_taps, precision=highest).astype(jnp.bfloat16)
    inline_taps = tap_values[:, 0]
    flat_traces = traces.reshape(NI * NX, NT)

    def orient_features(pieces):
        time_one, xline_one, inline_one = pieces
        band = jnp.dot(flat_traces, time_one.reshape(NT, 2 * NT), preferred_element_type=jnp.float32)
        band = band.astype(jnp.bfloat16).reshape(NI, NX, 2, NT)
        across = jnp.einsum('ixpt,xpqry->iqryt', band.astype(jnp.float32), xline_one.astype(jnp.float32), precision=highest).astype(jnp.bfloat16)
        padded = jnp.pad(across.astype(jnp.float32), ((HALF, HALF), (0, 0), (0, 0), (0, 0), (0, 0)))
        real_part = jnp.zeros((NI, 2, NX, NT), jnp.float32)
        imag_part = jnp.zeros((NI, 2, NX, NT), jnp.float32)
        for shift_index in range(TAPS):
            window = padded[shift_index:shift_index + NI]
            tap_real = inline_one[0, shift_index].astype(jnp.float32)
            tap_imag = inline_one[1, shift_index].astype(jnp.float32)
            real_part = real_part + window[:, :, 0] * tap_real - window[:, :, 1] * tap_imag
            imag_part = imag_part + window[:, :, 0] * tap_imag + window[:, :, 1] * tap_real
        return jnp.sqrt(real_part * real_part + imag_part * imag_part + eps_mag)
    stacked = lax.map(orient_features, (time_mats, xline_mats, inline_taps))
    features = jnp.transpose(stacked, (1, 0, 2, 3, 4)).reshape(NI, FEATS, NX * NT)
    centers = init_means
    spreads = init_variances
    weights = init_weights
    log_weights = jnp.log(init_weights)
    posterior = None
    for iteration in range(ITERS):
        posterior, masses, firsts = lax.map(lambda feature_rows: first_pass(feature_rows, centers, spreads, log_weights), features)
        total_mass = lax.optimization_barrier(jnp.sum(masses, axis=0))
        total_first = lax.optimization_barrier(jnp.sum(firsts, axis=0))
        new_centers = (total_first + centers) / (total_mass + 1.0)[:, None]
        spread_rows = lax.map(lambda feature_rows: centred_pass(feature_rows, centers, spreads, log_weights, new_centers), features)
        new_spreads = (lax.optimization_barrier(jnp.sum(spread_rows, axis=0)) + spreads) / (total_mass + 1.0)[:, None]
        weights = (total_mass + 1.0) / (CELLS + K)
        log_weights = jnp.log(weights)
        centers = new_centers
        spreads = new_spreads
    return (posterior.reshape(NI, K, NX, NT), centers, spreads, weights)
```

```python
import functools
import math

import jax
import jax.numpy as jnp
from jax import lax
from jax.experimental import pallas as pl
from jax.experimental.pallas import tpu as pltpu
from jax.sharding import PartitionSpec as P

TAPS = 31
HALF = 15
AZIMUTHS = 8
DIPS = 4
LANES = 128

eps_mag = 0.01
wavenumber = math.pi / 4.0
width_scale = HALF / 3.0
norm = math.sqrt(
    sum(math.exp(-n * n / (width_scale * width_scale)) for n in range(-HALF, HALF + 1))
)
MESH = pl.DeviceIdType.MESH
f32 = jnp.float32
bf16 = jnp.bfloat16
VMEM = pltpu.MemorySpace.VMEM
SMEM = pltpu.MemorySpace.SMEM


def round_up(value, step):
    return -(-value // step) * step


def iotas(shape):
    return (
        lax.broadcasted_iota(jnp.int32, shape, 0),
        lax.broadcasted_iota(jnp.int32, shape, 1),
    )


def roll(value, amount):
    return value if amount == 0 else pltpu.roll(value, amount, 1)


def taps(wave, difference):
    offset = (difference - HALF).astype(f32)
    wave = jnp.concatenate([wave] * (difference.shape[1] // LANES), axis=1)
    wave = jnp.concatenate([wave] * (difference.shape[0] // 8), axis=0)
    phase = offset * wave
    envelope = jnp.exp(-offset * offset / (2.0 * width_scale * width_scale)) / norm
    hit = jnp.logical_and(difference >= 0, difference < TAPS)
    real = jnp.where(hit, envelope * jnp.cos(phase), 0.0)
    imag = jnp.where(hit, envelope * jnp.sin(phase), 0.0)
    return real, imag


def angle(value, step):
    return jnp.full((8, LANES), value.astype(f32)) * step


def time_table(dip, time_ref):
    wave = wavenumber * jnp.cos(angle(dip + 1, math.pi / (2 * DIPS + 2)))
    sub, lane = iotas((8, LANES))
    bases = taps(wave, jnp.bitwise_and(sub - lane + HALF, LANES - 1))
    for s in range(0, LANES, 16):
        pieces = []
        for start in (s, s + 8):
            near = jnp.abs(sub + start - lane) <= HALF
            pieces.append(
                jnp.concatenate([jnp.where(near, roll(base, start), 0.0) for base in bases], axis=1)
            )
        time_ref[dip, s : s + 16, :] = jnp.concatenate(pieces, axis=0).astype(bf16)


def space_tables(orient, direction, sizes, col, x_ref, i_ref):
    rows, cols, width, group = sizes
    lanes = 2 * LANES
    azimuth = angle(direction % AZIMUTHS, math.pi / AZIMUTHS)
    dip_angle = angle(direction // AZIMUTHS + 1, math.pi / (2 * DIPS + 2))
    inline_wave = wavenumber * (jnp.sin(dip_angle) * jnp.cos(azimuth))
    xline_wave = wavenumber * (jnp.sin(dip_angle) * jnp.sin(azimuth))

    sub, lane = iotas((8, lanes))
    row, step = sub % group, sub // group
    place = jnp.where(lane >= group * width, lane - lanes, lane)
    bases = taps(xline_wave, place - row * width - step - col * cols + HALF)
    mine = jnp.logical_and(lane >= row * width, lane < (row + 1) * width)
    per = 8 // group
    for part in range(2):
        for y in range(0, cols, 2 * per):
            pair = jnp.concatenate(
                [jnp.where(mine, roll(bases[part], y + dy), 0.0) for dy in (0, per)], axis=0
            )
            start = (part * cols + y) * group
            x_ref[orient, start : start + 16, :] = pair[:, : group * width].astype(bf16)

    deep = 3 * rows
    half = per * deep
    sub, lane = iotas((rows, lanes))
    imag_in = lane >= half
    within = jnp.where(imag_in, lane - half, lane)
    line = (within // 8) * group + within % group
    step = (within // group) % per
    real, imag = taps(inline_wave, line - sub - rows + HALF)
    blocks = [jnp.where(imag_in, -imag, real), jnp.where(imag_in, real, imag)]
    for dy in range(per):
        for index, block in enumerate(blocks):
            start = (dy * 2 + index) * rows
            value = jnp.where(step == dy, block, 0.0)
            i_ref[orient, start : start + rows, :] = value[:, : 2 * half].astype(bf16)


def halo_kernel(inlines, xlines, sizes, dir_ref, own_ref, out_ref, time_ref, x_ref, i_ref, *sems):
    send_sem, recv_sem, own_sem = sems
    row = lax.axis_index("inline")
    col = lax.axis_index("xline")
    cols = sizes[1]
    mine = pl.ds(pl.multiple_of(col * cols, 8), cols)

    def there(side):
        return row > 0 if side < 0 else row < inlines - 1

    barrier = pltpu.get_barrier_semaphore()
    for side in (-1, 1):
        @pl.when(there(side))
        def _(side=side):
            pl.semaphore_signal(
                barrier, inc=1, device_id={"inline": row + side}, device_id_type=MESH
            )
    for shift in range(1, xlines):
        pl.semaphore_signal(
            barrier,
            inc=1,
            device_id={"xline": lax.rem(col + shift, xlines)},
            device_id_type=MESH,
        )
    own = pltpu.make_async_copy(own_ref, out_ref.at[1, :, mine], own_sem.at[0])
    own.start()

    @pl.loop(0, DIPS)
    def _(dip):
        time_table(dip, time_ref)

    sides = (row > 0).astype(jnp.int32) + (row < inlines - 1).astype(jnp.int32)
    pl.semaphore_wait(barrier, sides + xlines - 1)

    def along(side):
        return pltpu.make_async_remote_copy(
            src_ref=own_ref,
            dst_ref=out_ref.at[1 - side, :, mine],
            send_sem=send_sem.at[1 - side, 0],
            recv_sem=recv_sem.at[1 - side, 0],
            device_id={"inline": row + side},
            device_id_type=MESH,
        )

    def across(block, shift):
        return pltpu.make_async_remote_copy(
            src_ref=own_ref if block == 1 else out_ref.at[block, :, mine],
            dst_ref=out_ref.at[block, :, mine],
            send_sem=send_sem.at[block, shift],
            recv_sem=recv_sem.at[block, shift],
            device_id={"xline": lax.rem(col + shift, xlines)},
            device_id_type=MESH,
        )

    for side in (-1, 1):
        @pl.when(there(side))
        def _(side=side):
            along(side).start()
    for shift in range(1, xlines):
        across(1, shift).start()
    for side in (-1, 1):
        @pl.when(jnp.logical_not(there(side)))
        def _(side=side):
            out_ref[1 + side] = jnp.zeros(out_ref.shape[1:], out_ref.dtype)

    orients = x_ref.shape[0]
    early = orients // 2

    @pl.loop(0, early)
    def _(orient):
        space_tables(orient, dir_ref[orient], sizes, col, x_ref, i_ref)

    for side in (-1, 1):
        @pl.when(there(side))
        def _(side=side):
            along(-side).wait_recv()
            for shift in range(1, xlines):
                across(1 + side, shift).start()

    @pl.loop(early, orients)
    def _(orient):
        space_tables(orient, dir_ref[orient], sizes, col, x_ref, i_ref)

    own.wait()
    for shift in range(1, xlines):
        across(1, shift).wait()
    for side in (-1, 1):
        @pl.when(there(side))
        def _(side=side):
            along(side).wait_send()
            for shift in range(1, xlines):
                across(1 + side, shift).wait()


def gather_halo(traces, directions):
    inlines, xlines = lax.axis_size("inline"), lax.axis_size("xline")
    rows, cols, samples = traces.shape
    orients = directions.shape[0]
    width = xlines * cols
    group = 4
    assert group * width + cols <= 2 * LANES
    per = 8 // group
    sizes = (rows, cols, width, group)
    return pl.pallas_call(
        functools.partial(halo_kernel, inlines, xlines, sizes),
        out_shape=[
            jax.ShapeDtypeStruct((3, rows, width, samples), traces.dtype),
            jax.ShapeDtypeStruct((DIPS, samples, 2 * samples), bf16),
            jax.ShapeDtypeStruct((orients, 2 * cols * group, group * width), bf16),
            jax.ShapeDtypeStruct((orients, 2 * per * rows, 2 * per * 3 * rows), bf16),
        ],
        in_specs=[pl.BlockSpec(memory_space=SMEM), pl.BlockSpec(memory_space=pl.ANY)],
        out_specs=[pl.BlockSpec(memory_space=VMEM)] * 4,
        scratch_shapes=[
            pltpu.SemaphoreType.DMA((3, xlines)),
            pltpu.SemaphoreType.DMA((3, xlines)),
            pltpu.SemaphoreType.DMA((1,)),
        ],
        compiler_params=pltpu.CompilerParams(
            collective_id=0, has_side_effects=True, vmem_limit_bytes=8 << 20
        ),
        name="halo",
    )(directions, traces)


def filter_kernel(sizes, dir_ref, halo_ref, time_ref, x_ref, i_ref, out_ref, band, cross):
    rows, cols, width, pad, orients, group = sizes
    per = 8 // group
    deep = 3 * rows
    half = per * deep
    span = group * width
    pairs = cols // per
    block = rows * width

    for y in range(cols):
        for extra in range(pad - 2 * orients):
            out_ref[y, pl.ds(2 * orients + extra, rows, stride=pad), :] = jnp.full(
                (rows, LANES), 1.0 if extra == 0 else 0.0, f32
            )

    @pl.loop(0, DIPS)
    def _(dip):
        for b in range(3):
            lines = halo_ref[b].reshape(block, LANES)
            band[dip, b * block : (b + 1) * block, :] = jnp.dot(
                lines, time_ref[dip], preferred_element_type=f32
            ).astype(bf16)

    def across(orient, dip, step):
        mixed = [
            jnp.dot(
                x_ref[orient],
                band[dip, (2 * step + h) * span : (2 * step + h + 1) * span, :],
                preferred_element_type=f32,
            )
            for h in range(2)
        ]
        for yp in range(pairs):
            slots = [[], [], [], []]
            for h in range(2):
                with_cos = mixed[h][yp * 8 : (yp + 1) * 8]
                with_sin = mixed[h][(pairs + yp) * 8 : (pairs + yp + 1) * 8]
                cu, cv = with_cos[:, :LANES], with_cos[:, LANES:]
                su, sv = with_sin[:, :LANES], with_sin[:, LANES:]
                for slot, value in zip(slots, (cu - sv, su + cv, cu + sv, su - cv)):
                    slot.append(value)
            for index, slot in enumerate(slots):
                q, r = index // 2, index % 2
                start = ((q * pairs + yp) * 2 + r) * half + step * 16
                cross[start : start + 16, :] = jnp.concatenate(slot, axis=0).astype(bf16)

    def along(orient, q, j):
        start = (q * pairs + 2 * j) * 2 * half
        operand = jnp.concatenate(
            [
                cross[start : start + 2 * half, :],
                cross[start + 2 * half : start + 4 * half, :],
            ],
            axis=1,
        )
        total = jnp.dot(i_ref[orient], operand, preferred_element_type=f32)
        for dy in range(per):
            re = total[(2 * dy) * rows : (2 * dy + 1) * rows]
            im = total[(2 * dy + 1) * rows : (2 * dy + 2) * rows]
            square = re * re + im * im + eps_mag
            size = square * lax.rsqrt(square)
            for h in range(2):
                out_ref[
                    (2 * j + h) * per + dy, pl.ds(2 * orient + q, rows, stride=pad), :
                ] = size[:, h * LANES : (h + 1) * LANES]

    @pl.loop(0, orients)
    def _(orient):
        dip = dir_ref[orient] // AZIMUTHS
        for step in range(deep // (2 * group)):
            across(orient, dip, step)
        for q in range(2):
            for j in range(pairs // 2):
                along(orient, q, j)


def filter_features(halo, tables, directions, pad):
    _, rows, width, samples = halo.shape
    orients, height, depth = tables[1].shape
    group = depth // width
    cols = height // (2 * group)
    sizes = (rows, cols, width, pad, orients, group)
    return pl.pallas_call(
        functools.partial(filter_kernel, sizes),
        out_shape=jax.ShapeDtypeStruct((cols, rows * pad, samples), f32),
        in_specs=[pl.BlockSpec(memory_space=SMEM)] + [pl.BlockSpec(memory_space=VMEM)] * 4,
        out_specs=pl.BlockSpec(memory_space=VMEM),
        scratch_shapes=[
            pltpu.VMEM((DIPS, 3 * rows * width, 2 * samples), bf16),
            pltpu.VMEM((4 * cols * 3 * rows, samples), bf16),
        ],
        compiler_params=pltpu.CompilerParams(vmem_limit_bytes=24 << 20),
        name="filters",
    )(directions, halo, *tables)


def split3(value):
    high = value.astype(bf16)
    rest = value - high.astype(f32)
    mid = rest.astype(bf16)
    low = (rest - mid.astype(f32)).astype(bf16)
    return high, mid, low


def column(row):
    return jnp.transpose(jnp.broadcast_to(row, (row.shape[1], row.shape[1])))


def padded(value, fill):
    rows, lanes = value.shape
    wide = jnp.concatenate([value, jnp.full((rows, LANES - lanes), fill, f32)], axis=1)
    full = jnp.concatenate([wide, jnp.full((LANES - rows, LANES), fill, f32)], axis=0)
    return jnp.transpose(full)


def first_params(mean_ref, var_ref, weight_ref):
    comps = mean_ref.shape[1]
    means = padded(mean_ref[...], 0.0)[:comps]
    shift_row = jnp.mean(means, axis=0, keepdims=True)
    weights = jnp.broadcast_to(padded(weight_ref[...], 1.0)[:comps, :1], (comps, LANES))
    return (means - shift_row, padded(var_ref[...], 1.0)[:comps], weights), shift_row


def next_params(folded, params, sizes):
    pad, count, cells = sizes
    means, spreads, _ = params
    comps = means.shape[0]
    total = jnp.concatenate([folded, pltpu.roll(folded, LANES // 2, 1)], axis=0)
    used = lax.broadcasted_iota(jnp.int32, (comps, LANES), 1) < count
    mass = total[:, count : count + 1]
    first = jnp.where(used, total, 0.0)
    second = jnp.where(used, pltpu.roll(total, LANES - pad, 1), 0.0)
    below = mass + 1.0
    new_means = (first + means) / below
    centred = second - 2.0 * new_means * first + new_means * new_means * mass
    new_spreads = jnp.where(used, (centred + spreads) / below, 1.0)
    return new_means, new_spreads, jnp.broadcast_to(below / (cells + comps), (comps, LANES))


def peer(shift, inlines, xlines):
    me = lax.axis_index("inline") * xlines + lax.axis_index("xline")
    other = lax.rem(me + shift, inlines * xlines)
    return {"inline": other // xlines, "xline": lax.rem(other, xlines)}


def greet(inlines, xlines):
    barrier = pltpu.get_barrier_semaphore()
    for shift in range(1, inlines * xlines):
        pl.semaphore_signal(
            barrier, inc=1, device_id=peer(shift, inlines, xlines), device_id_type=MESH
        )


def gather_sum(inlines, xlines, payload_ref, slots, send_sem, recv_sem):
    members = inlines * xlines
    me = lax.axis_index("inline") * xlines + lax.axis_index("xline")
    pl.semaphore_wait(pltpu.get_barrier_semaphore(), members - 1)

    def copy(shift):
        return pltpu.make_async_remote_copy(
            src_ref=payload_ref,
            dst_ref=slots.at[me],
            send_sem=send_sem.at[shift],
            recv_sem=recv_sem.at[shift],
            device_id=peer(shift, inlines, xlines),
            device_id_type=MESH,
        )

    for shift in range(1, members):
        copy(shift).start()
    slots[me] = payload_ref[...]
    for shift in range(1, members):
        copy(shift).wait()
    total = slots[0]
    for member in range(1, members):
        total = total + slots[member]
    return total


def gather_scratch(members, comps):
    return [
        pltpu.VMEM((members, comps // 2, LANES), f32),
        pltpu.SemaphoreType.DMA((members,)),
        pltpu.SemaphoreType.DMA((members,)),
    ]


def moment_kernel(sizes, last, *refs):
    cols, pad, count, chunk, together, cells, inlines, xlines = sizes
    if last:
        split_ref, sum_ref, mean_ref, var_ref, weight_ref, *refs = refs
        moment_ref, post_ref, table, total, wide = refs
    else:
        feat_ref, mean_ref, var_ref, weight_ref, *refs = refs
        moment_ref, split_ref, table, total, shift_ref, payload, slots, send_sem, recv_sem = refs
    step = pl.program_id(0)
    comps = mean_ref.shape[1]

    @pl.when(step == 0)
    def _():
        if not last:
            greet(inlines, xlines)
        params, shift_row = first_params(mean_ref, var_ref, weight_ref)
        if last:
            params = next_params(sum_ref[...], params, (pad, count, cells))
        else:
            shift_ref[...] = column(shift_row)[:pad]
        lane = lax.broadcasted_iota(jnp.int32, (comps, 2 * LANES), 1)
        means = jnp.concatenate([params[0], jnp.zeros((comps, LANES), f32)], axis=1)
        spreads = jnp.concatenate([params[1], jnp.ones((comps, LANES), f32)], axis=1)
        used = lane < count
        inverse = jnp.where(used, 1.0 / spreads, 0.0)
        scaled = means * inverse
        terms = jnp.where(used, jnp.log(2.0 * math.pi * spreads) + means * scaled, 0.0)
        constant = jnp.log(params[2][:, :1]) - 0.5 * jnp.sum(terms, axis=1, keepdims=True)
        row = jnp.where(used, scaled, 0.0) + jnp.where(lane == count, constant, 0.0)
        row = row + pltpu.roll(-0.5 * inverse, pad, 1)
        parts = split3(row)
        for index, part in enumerate(parts):
            part = part.astype(f32)
            tiled = part + pltpu.roll(part, 2 * pad, 1) + pltpu.roll(part, 4 * pad, 1)
            table[index * comps : (index + 1) * comps, :] = tiled.astype(bf16)
        total[...] = jnp.zeros_like(total)

    weights = table[:, : 6 * pad]
    def scores(j, first):
        span = slice(first * LANES, (first + chunk) * LANES)
        if last:
            operand = split_ref[j, :, span]
        else:
            base = pl.multiple_of((step * together + j) * pad, 8)
            values = jnp.concatenate(
                [
                    feat_ref[first + y, pl.ds(base, pad), :] - shift_ref[...]
                    for y in range(chunk)
                ],
                axis=1,
            )
            both = jnp.concatenate([values, values * values], axis=0)
            operand = jnp.concatenate(split3(both), axis=0)
            split_ref[j, :, span] = operand
        wide_score = jnp.dot(weights, operand, preferred_element_type=f32)
        score = wide_score[:comps] + (
            wide_score[comps : 2 * comps] + wide_score[2 * comps : 3 * comps]
        )
        return operand, score

    pieces = [(j, first) for j in range(together) for first in range(0, cols, chunk)]
    ahead = scores(*pieces[0])
    moment = total[...]
    for index, (j, first) in enumerate(pieces):
        operand, score = ahead
        if index + 1 < len(pieces):
            ahead = scores(*pieces[index + 1])
        exponent = jnp.exp(score - jnp.max(score, axis=0, keepdims=True))
        share = exponent * (1.0 / jnp.sum(exponent, axis=0, keepdims=True))
        high = share.astype(bf16)
        low = (share - high.astype(f32)).astype(bf16)
        moment = moment + lax.dot_general(
            jnp.concatenate([high, low], axis=0),
            operand,
            (((1,), (1,)), ((), ())),
            preferred_element_type=f32,
        )
        if last:
            for y in range(chunk):
                wide[pl.ds((j * comps) * cols + first + y, comps, stride=cols), :] = share[
                    :, y * LANES : (y + 1) * LANES
                ]
    total[...] = moment
    if last:
        for j in range(together):
            for k in range(comps):
                start = (j * comps + k) * cols
                post_ref[j, k] = wide[start : start + cols, :].astype(bf16)

    @pl.when(step == pl.num_programs(0) - 1)
    def _():
        both = total[:comps] + total[comps:]
        both = jnp.concatenate([both, jnp.zeros((comps, 2 * LANES - 6 * pad), f32)], axis=1)
        summed = (
            both
            + pltpu.roll(both, 2 * LANES - 2 * pad, 1)
            + pltpu.roll(both, 2 * LANES - 4 * pad, 1)
        )[:, :LANES]
        lane = lax.broadcasted_iota(jnp.int32, (comps, LANES), 1)
        summed = jnp.where(lane < 2 * pad, summed, 0.0)
        half = comps // 2
        folded = summed[:half] + pltpu.roll(summed[half:], LANES // 2, 1)
        if last:
            moment_ref[...] = folded
        else:
            payload[...] = folded
            moment_ref[...] = gather_sum(inlines, xlines, payload, slots, send_sem, recv_sem)


def moments(features, split, summed, init, count, rows, cells):
    last = summed is not None
    inlines, xlines = lax.axis_size("inline"), lax.axis_size("xline")
    comps = init[0].shape[1]
    cols, flat, samples = features.shape
    pad = flat // rows
    assert 4 * pad <= LANES and comps % 16 == 0
    chunk = 4
    together = 2
    folded = jax.ShapeDtypeStruct((comps // 2, LANES), f32)
    inputs = ([summed] if last else []) + list(init)
    out_shape, out_specs = [folded], [pl.BlockSpec(folded.shape, lambda j: (0, 0))]
    split_shape = (rows, 6 * pad, cols * samples)
    split_spec = pl.BlockSpec((together,) + split_shape[1:], lambda j: (j, 0, 0))
    scratch = [
        pltpu.VMEM((3 * comps, 2 * LANES), bf16),
        pltpu.VMEM((2 * comps, 6 * pad), f32),
    ]
    params = dict(vmem_limit_bytes=24 << 20)
    if last:
        out_shape.append(jax.ShapeDtypeStruct((rows, comps, cols, samples), bf16))
        out_specs.append(pl.BlockSpec((together, comps, cols, samples), lambda j: (j, 0, 0, 0)))
        scratch.append(pltpu.VMEM((together * comps * cols, samples), f32))
    else:
        out_shape.append(jax.ShapeDtypeStruct(split_shape, bf16))
        out_specs.append(split_spec)
        scratch += [pltpu.VMEM((pad, LANES), f32), pltpu.VMEM(folded.shape, f32)]
        scratch += gather_scratch(inlines * xlines, comps)
        params.update(collective_id=1, has_side_effects=True)
    sizes = (cols, pad, count, chunk, together, cells, inlines, xlines)
    return pl.pallas_call(
        functools.partial(moment_kernel, sizes, last),
        out_shape=out_shape,
        grid=(rows // together,),
        in_specs=[split_spec if last else pl.BlockSpec(memory_space=VMEM)]
        + [pl.BlockSpec(array.shape, lambda j: (0, 0)) for array in inputs],
        out_specs=out_specs,
        scratch_shapes=scratch,
        compiler_params=pltpu.CompilerParams(**params),
        name="last_pass" if last else "first_pass",
    )(split if last else features, *inputs)


def sum_kernel(inlines, xlines, moment_ref, out_ref, slots, send_sem, recv_sem):
    greet(inlines, xlines)
    out_ref[...] = gather_sum(inlines, xlines, moment_ref, slots, send_sem, recv_sem)


def sum_moments(moment):
    inlines, xlines = lax.axis_size("inline"), lax.axis_size("xline")
    return pl.pallas_call(
        functools.partial(sum_kernel, inlines, xlines),
        out_shape=jax.ShapeDtypeStruct(moment.shape, f32),
        in_specs=[pl.BlockSpec(memory_space=VMEM)],
        out_specs=pl.BlockSpec(memory_space=VMEM),
        scratch_shapes=gather_scratch(inlines * xlines, 2 * moment.shape[0]),
        compiler_params=pltpu.CompilerParams(
            collective_id=2, has_side_effects=True, vmem_limit_bytes=4 << 20
        ),
        name="sum_moments",
    )(moment)


def final_kernel(sizes, *refs):
    *sums, mean_ref, var_ref, weight_ref, mean_out, var_out, weight_out = refs
    count = sizes[1]
    params, shift_row = first_params(mean_ref, var_ref, weight_ref)
    for summed in sums:
        params = next_params(summed[...], params, sizes)
    means, spreads, weights = params
    comps = means.shape[0]
    blank = jnp.zeros((LANES - comps, LANES), f32)
    turned = [
        jnp.transpose(jnp.concatenate([value, blank], axis=0))[:, :comps]
        for value in (means + shift_row, spreads, weights)
    ]
    mean_out[...] = turned[0][:count]
    var_out[...] = turned[1][:count]
    weight_out[...] = turned[2][:1]


def finish(sums, init, sizes):
    count, comps = init[0].shape
    inputs = sums + list(init)
    return pl.pallas_call(
        functools.partial(final_kernel, sizes),
        out_shape=[
            jax.ShapeDtypeStruct((count, comps), f32),
            jax.ShapeDtypeStruct((count, comps), f32),
            jax.ShapeDtypeStruct((1, comps), f32),
        ],
        in_specs=[pl.BlockSpec(memory_space=VMEM)] * len(inputs),
        out_specs=[pl.BlockSpec(memory_space=VMEM)] * 3,
        compiler_params=pltpu.CompilerParams(vmem_limit_bytes=4 << 20),
        name="finish",
    )(*inputs)


def per_device(traces, directions, init_means, init_variances, init_weights):
    rows, cols, samples = traces.shape
    assert samples == LANES and rows >= HALF and rows % 8 == 0 and cols % 4 == 0
    count = 2 * directions.shape[0]
    pad = round_up(count + 1, 8)
    comps = init_weights.shape[0]
    cells = lax.axis_size("inline") * rows * lax.axis_size("xline") * cols * samples
    init = (init_means.T, init_variances.T, init_weights.reshape(1, comps))
    halo, *tables = gather_halo(traces, directions)
    features = filter_features(halo, tables, directions, pad)
    summed, split = moments(features, None, None, init, count, rows, cells)
    moment, posterior = moments(features, split, summed, init, count, rows, cells)
    sums = [summed, sum_moments(moment)]
    means, spreads, weights = finish(sums, init, (pad, count, cells))
    return posterior, means.T, spreads.T, weights.reshape(comps)


def solution(mesh):
    in_specs = (P(("slab", "inline"), "xline", None), P(), P(), P(), P())
    out_specs = (
        P(("slab", "inline"), None, "xline", None),
        P("slab", None),
        P("slab", None),
        P("slab"),
    )
    return jax.shard_map(
        per_device, mesh=mesh, in_specs=in_specs, out_specs=out_specs, check_vma=False
    )
```

```python
import functools
import math

import jax
import jax.numpy as jnp
from jax import lax
from jax.experimental import pallas as pl
from jax.experimental.pallas import tpu as pltpu
from jax.sharding import PartitionSpec as P

TAPS = 31
HALF = 15
AZIMUTHS = 8
DIPS = 4
LANES = 128

eps_mag = 0.01
wavenumber = math.pi / 4.0
width_scale = HALF / 3.0
norm = math.sqrt(
    sum(math.exp(-n * n / (width_scale * width_scale)) for n in range(-HALF, HALF + 1))
)
MESH = pl.DeviceIdType.MESH
LOG2E = math.log2(math.e)
f32 = jnp.float32
bf16 = jnp.bfloat16
VMEM = pltpu.MemorySpace.VMEM
SMEM = pltpu.MemorySpace.SMEM


def round_up(value, step):
    return -(-value // step) * step


def iotas(shape):
    return (
        lax.broadcasted_iota(jnp.int32, shape, 0),
        lax.broadcasted_iota(jnp.int32, shape, 1),
    )


def roll(value, amount):
    return value if amount == 0 else pltpu.roll(value, amount, 1)


def taps(wave, difference):
    offset = (difference - HALF).astype(f32)
    wave = jnp.concatenate([wave] * (difference.shape[1] // LANES), axis=1)
    wave = jnp.concatenate([wave] * (difference.shape[0] // 8), axis=0)
    phase = offset * wave
    envelope = jnp.exp(-offset * offset / (2.0 * width_scale * width_scale)) / norm
    hit = jnp.logical_and(difference >= 0, difference < TAPS)
    real = jnp.where(hit, envelope * jnp.cos(phase), 0.0)
    imag = jnp.where(hit, envelope * jnp.sin(phase), 0.0)
    return real, imag


def angle(value, step):
    return jnp.full((8, LANES), value.astype(f32)) * step


def time_table(dip, time_ref):
    wave = wavenumber * jnp.cos(angle(dip + 1, math.pi / (2 * DIPS + 2)))
    sub, lane = iotas((8, LANES))
    bases = taps(wave, jnp.bitwise_and(sub - lane + HALF, LANES - 1))
    for s in range(0, LANES, 16):
        pieces = []
        for start in (s, s + 8):
            near = jnp.abs(sub + start - lane) <= HALF
            pieces.append(
                jnp.concatenate([jnp.where(near, roll(base, start), 0.0) for base in bases], axis=1)
            )
        time_ref[dip, s : s + 16, :] = jnp.concatenate(pieces, axis=0).astype(bf16)


def space_tables(orient, direction, sizes, col, x_ref, i_ref):
    rows, cols, width, group = sizes
    lanes = 2 * LANES
    azimuth = angle(direction % AZIMUTHS, math.pi / AZIMUTHS)
    dip_angle = angle(direction // AZIMUTHS + 1, math.pi / (2 * DIPS + 2))
    inline_wave = wavenumber * (jnp.sin(dip_angle) * jnp.cos(azimuth))
    xline_wave = wavenumber * (jnp.sin(dip_angle) * jnp.sin(azimuth))

    sub, lane = iotas((8, lanes))
    row, step = sub % group, sub // group
    place = jnp.where(lane >= group * width, lane - lanes, lane)
    bases = taps(xline_wave, place - row * width - step - col * cols + HALF)
    mine = jnp.logical_and(lane >= row * width, lane < (row + 1) * width)
    per = 8 // group
    for part in range(2):
        for y in range(0, cols, 2 * per):
            pair = jnp.concatenate(
                [jnp.where(mine, roll(bases[part], y + dy), 0.0) for dy in (0, per)], axis=0
            )
            start = (part * cols + y) * group
            x_ref[orient, start : start + 16, :] = pair[:, : group * width].astype(bf16)

    deep = 3 * rows
    half = per * deep
    sub, lane = iotas((rows, lanes))
    imag_in = lane >= half
    within = jnp.where(imag_in, lane - half, lane)
    line = (within // 8) * group + within % group
    step = (within // group) % per
    real, imag = taps(inline_wave, line - sub - rows + HALF)
    blocks = [jnp.where(imag_in, -imag, real), jnp.where(imag_in, real, imag)]
    for dy in range(per):
        for index, block in enumerate(blocks):
            start = (dy * 2 + index) * rows
            value = jnp.where(step == dy, block, 0.0)
            i_ref[orient, start : start + rows, :] = value[:, : 2 * half].astype(bf16)


def halo_kernel(inlines, xlines, sizes, dir_ref, own_ref, out_ref, time_ref, x_ref, i_ref, *sems):
    send_sem, recv_sem, own_sem = sems
    row = lax.axis_index("inline")
    col = lax.axis_index("xline")
    cols = sizes[1]
    mine = pl.ds(pl.multiple_of(col * cols, 8), cols)

    def there(side):
        return row > 0 if side < 0 else row < inlines - 1

    barrier = pltpu.get_barrier_semaphore()
    for side in (-1, 1):
        @pl.when(there(side))
        def _(side=side):
            pl.semaphore_signal(
                barrier, inc=1, device_id={"inline": row + side}, device_id_type=MESH
            )
    for shift in range(1, xlines):
        pl.semaphore_signal(
            barrier,
            inc=1,
            device_id={"xline": lax.rem(col + shift, xlines)},
            device_id_type=MESH,
        )
    own = pltpu.make_async_copy(own_ref, out_ref.at[1, :, mine], own_sem.at[0])
    own.start()

    @pl.loop(0, DIPS)
    def _(dip):
        time_table(dip, time_ref)

    sides = (row > 0).astype(jnp.int32) + (row < inlines - 1).astype(jnp.int32)
    pl.semaphore_wait(barrier, sides + xlines - 1)

    def along(side):
        return pltpu.make_async_remote_copy(
            src_ref=own_ref,
            dst_ref=out_ref.at[1 - side, :, mine],
            send_sem=send_sem.at[1 - side, 0],
            recv_sem=recv_sem.at[1 - side, 0],
            device_id={"inline": row + side},
            device_id_type=MESH,
        )

    def across(block, shift):
        return pltpu.make_async_remote_copy(
            src_ref=own_ref if block == 1 else out_ref.at[block, :, mine],
            dst_ref=out_ref.at[block, :, mine],
            send_sem=send_sem.at[block, shift],
            recv_sem=recv_sem.at[block, shift],
            device_id={"xline": lax.rem(col + shift, xlines)},
            device_id_type=MESH,
        )

    for side in (-1, 1):
        @pl.when(there(side))
        def _(side=side):
            along(side).start()
    for shift in range(1, xlines):
        across(1, shift).start()
    for side in (-1, 1):
        @pl.when(jnp.logical_not(there(side)))
        def _(side=side):
            out_ref[1 + side] = jnp.zeros(out_ref.shape[1:], out_ref.dtype)

    orients = x_ref.shape[0]
    early = orients // 2

    @pl.loop(0, early)
    def _(orient):
        space_tables(orient, dir_ref[orient], sizes, col, x_ref, i_ref)

    for side in (-1, 1):
        @pl.when(there(side))
        def _(side=side):
            along(-side).wait_recv()
            for shift in range(1, xlines):
                across(1 + side, shift).start()

    @pl.loop(early, orients)
    def _(orient):
        space_tables(orient, dir_ref[orient], sizes, col, x_ref, i_ref)

    own.wait()
    for shift in range(1, xlines):
        across(1, shift).wait()
    for side in (-1, 1):
        @pl.when(there(side))
        def _(side=side):
            along(side).wait_send()
            for shift in range(1, xlines):
                across(1 + side, shift).wait()


def gather_halo(traces, directions):
    inlines, xlines = lax.axis_size("inline"), lax.axis_size("xline")
    rows, cols, samples = traces.shape
    orients = directions.shape[0]
    width = xlines * cols
    group = 4
    assert group * width + cols <= 2 * LANES
    per = 8 // group
    sizes = (rows, cols, width, group)
    return pl.pallas_call(
        functools.partial(halo_kernel, inlines, xlines, sizes),
        out_shape=[
            jax.ShapeDtypeStruct((3, rows, width, samples), traces.dtype),
            jax.ShapeDtypeStruct((DIPS, samples, 2 * samples), bf16),
            jax.ShapeDtypeStruct((orients, 2 * cols * group, group * width), bf16),
            jax.ShapeDtypeStruct((orients, 2 * per * rows, 2 * per * 3 * rows), bf16),
        ],
        in_specs=[pl.BlockSpec(memory_space=SMEM), pl.BlockSpec(memory_space=pl.ANY)],
        out_specs=[pl.BlockSpec(memory_space=VMEM)] * 4,
        scratch_shapes=[
            pltpu.SemaphoreType.DMA((3, xlines)),
            pltpu.SemaphoreType.DMA((3, xlines)),
            pltpu.SemaphoreType.DMA((1,)),
        ],
        compiler_params=pltpu.CompilerParams(
            collective_id=0, has_side_effects=True, vmem_limit_bytes=8 << 20
        ),
        name="halo",
    )(directions, traces)


def filter_kernel(sizes, dir_ref, halo_ref, time_ref, x_ref, i_ref, out_ref, band, cross):
    rows, cols, width, pad, orients, group = sizes
    per = 8 // group
    deep = 3 * rows
    half = per * deep
    span = group * width
    pairs = cols // per
    block = rows * width

    for y in range(cols):
        for extra in range(pad - 2 * orients):
            out_ref[y, pl.ds(2 * orients + extra, rows, stride=pad), :] = jnp.full(
                (rows, LANES), 1.0 if extra == 0 else 0.0, f32
            )

    @pl.loop(0, DIPS)
    def _(dip):
        for b in range(3):
            lines = halo_ref[b].reshape(block, LANES)
            band[dip, b * block : (b + 1) * block, :] = jnp.dot(
                lines, time_ref[dip], preferred_element_type=f32
            ).astype(bf16)

    def across(orient, dip, step):
        mixed = [
            jnp.dot(
                x_ref[orient],
                band[dip, (2 * step + h) * span : (2 * step + h + 1) * span, :],
                preferred_element_type=f32,
            )
            for h in range(2)
        ]
        for yp in range(pairs):
            slots = [[], [], [], []]
            for h in range(2):
                with_cos = mixed[h][yp * 8 : (yp + 1) * 8]
                with_sin = mixed[h][(pairs + yp) * 8 : (pairs + yp + 1) * 8]
                cu, cv = with_cos[:, :LANES], with_cos[:, LANES:]
                su, sv = with_sin[:, :LANES], with_sin[:, LANES:]
                for slot, value in zip(slots, (cu - sv, su + cv, cu + sv, su - cv)):
                    slot.append(value)
            for index, slot in enumerate(slots):
                q, r = index // 2, index % 2
                start = ((q * pairs + yp) * 2 + r) * half + step * 16
                cross[start : start + 16, :] = jnp.concatenate(slot, axis=0).astype(bf16)

    def along(orient, q, j):
        start = (q * pairs + 2 * j) * 2 * half
        operand = jnp.concatenate(
            [
                cross[start : start + 2 * half, :],
                cross[start + 2 * half : start + 4 * half, :],
            ],
            axis=1,
        )
        total = jnp.dot(i_ref[orient], operand, preferred_element_type=f32)
        for dy in range(per):
            re = total[(2 * dy) * rows : (2 * dy + 1) * rows]
            im = total[(2 * dy + 1) * rows : (2 * dy + 2) * rows]
            square = re * re + im * im + eps_mag
            size = square * lax.rsqrt(square)
            for h in range(2):
                out_ref[
                    (2 * j + h) * per + dy, pl.ds(2 * orient + q, rows, stride=pad), :
                ] = size[:, h * LANES : (h + 1) * LANES]

    @pl.loop(0, orients)
    def _(orient):
        dip = dir_ref[orient] // AZIMUTHS
        for step in range(deep // (2 * group)):
            across(orient, dip, step)
        for q in range(2):
            for j in range(pairs // 2):
                along(orient, q, j)


def filter_features(halo, tables, directions, pad):
    _, rows, width, samples = halo.shape
    orients, height, depth = tables[1].shape
    group = depth // width
    cols = height // (2 * group)
    sizes = (rows, cols, width, pad, orients, group)
    return pl.pallas_call(
        functools.partial(filter_kernel, sizes),
        out_shape=jax.ShapeDtypeStruct((cols, rows * pad, samples), f32),
        in_specs=[pl.BlockSpec(memory_space=SMEM)] + [pl.BlockSpec(memory_space=VMEM)] * 4,
        out_specs=pl.BlockSpec(memory_space=VMEM),
        scratch_shapes=[
            pltpu.VMEM((DIPS, 3 * rows * width, 2 * samples), bf16),
            pltpu.VMEM((4 * cols * 3 * rows, samples), bf16),
        ],
        compiler_params=pltpu.CompilerParams(vmem_limit_bytes=24 << 20),
        name="filters",
    )(directions, halo, *tables)


def split3(value):
    high = value.astype(bf16)
    rest = value - high.astype(f32)
    mid = rest.astype(bf16)
    low = (rest - mid.astype(f32)).astype(bf16)
    return high, mid, low


def column(row):
    return jnp.transpose(jnp.broadcast_to(row, (row.shape[1], row.shape[1])))


def padded(value, fill):
    rows, lanes = value.shape
    wide = jnp.concatenate([value, jnp.full((rows, LANES - lanes), fill, f32)], axis=1)
    full = jnp.concatenate([wide, jnp.full((LANES - rows, LANES), fill, f32)], axis=0)
    return jnp.transpose(full)


def first_params(mean_ref, var_ref, weight_ref):
    comps = mean_ref.shape[1]
    means = padded(mean_ref[...], 0.0)[:comps]
    shift_row = jnp.mean(means, axis=0, keepdims=True)
    weights = jnp.broadcast_to(padded(weight_ref[...], 1.0)[:comps, :1], (comps, LANES))
    return (means - shift_row, padded(var_ref[...], 1.0)[:comps], weights), shift_row


def next_params(folded, params, sizes):
    pad, count, cells = sizes
    means, spreads, _ = params
    comps = means.shape[0]
    total = jnp.concatenate([folded, pltpu.roll(folded, LANES // 2, 1)], axis=0)
    used = lax.broadcasted_iota(jnp.int32, (comps, LANES), 1) < count
    mass = total[:, count : count + 1]
    first = jnp.where(used, total, 0.0)
    second = jnp.where(used, pltpu.roll(total, LANES - pad, 1), 0.0)
    below = mass + 1.0
    new_means = (first + means) / below
    centred = second - 2.0 * new_means * first + new_means * new_means * mass
    new_spreads = jnp.where(used, (centred + spreads) / below, 1.0)
    return new_means, new_spreads, jnp.broadcast_to(below / (cells + comps), (comps, LANES))


def peer(shift, inlines, xlines):
    me = lax.axis_index("inline") * xlines + lax.axis_index("xline")
    other = lax.rem(me + shift, inlines * xlines)
    return {"inline": other // xlines, "xline": lax.rem(other, xlines)}


def greet(inlines, xlines):
    barrier = pltpu.get_barrier_semaphore()
    for shift in range(1, inlines * xlines):
        pl.semaphore_signal(
            barrier, inc=1, device_id=peer(shift, inlines, xlines), device_id_type=MESH
        )


def gather_sum(inlines, xlines, payload_ref, slots, send_sem, recv_sem):
    members = inlines * xlines
    me = lax.axis_index("inline") * xlines + lax.axis_index("xline")
    pl.semaphore_wait(pltpu.get_barrier_semaphore(), members - 1)

    def copy(shift):
        return pltpu.make_async_remote_copy(
            src_ref=payload_ref,
            dst_ref=slots.at[me],
            send_sem=send_sem.at[shift],
            recv_sem=recv_sem.at[shift],
            device_id=peer(shift, inlines, xlines),
            device_id_type=MESH,
        )

    for shift in range(1, members):
        copy(shift).start()
    slots[me] = payload_ref[...]
    for shift in range(1, members):
        copy(shift).wait()
    total = slots[0]
    for member in range(1, members):
        total = total + slots[member]
    return total


def gather_scratch(members, comps):
    return [
        pltpu.VMEM((members, comps // 2, LANES), f32),
        pltpu.SemaphoreType.DMA((members,)),
        pltpu.SemaphoreType.DMA((members,)),
    ]


def moment_kernel(sizes, last, *refs):
    cols, pad, count, chunk, together, cells, inlines, xlines = sizes
    if last:
        split_ref, sum_ref, mean_ref, var_ref, weight_ref, *refs = refs
        moment_ref, post_ref, table, total, wide = refs
    else:
        feat_ref, mean_ref, var_ref, weight_ref, *refs = refs
        moment_ref, split_ref, table, total, shift_ref, payload, slots, send_sem, recv_sem = refs
    step = pl.program_id(0)
    comps = mean_ref.shape[1]

    @pl.when(step == 0)
    def _():
        if not last:
            greet(inlines, xlines)
        params, shift_row = first_params(mean_ref, var_ref, weight_ref)
        if last:
            params = next_params(sum_ref[...], params, (pad, count, cells))
        else:
            shift_ref[...] = column(shift_row)[:pad]
        lane = lax.broadcasted_iota(jnp.int32, (comps, 2 * LANES), 1)
        means = jnp.concatenate([params[0], jnp.zeros((comps, LANES), f32)], axis=1)
        spreads = jnp.concatenate([params[1], jnp.ones((comps, LANES), f32)], axis=1)
        used = lane < count
        inverse = jnp.where(used, 1.0 / spreads, 0.0)
        scaled = means * inverse
        terms = jnp.where(used, jnp.log(2.0 * math.pi * spreads) + means * scaled, 0.0)
        constant = jnp.log(params[2][:, :1]) - 0.5 * jnp.sum(terms, axis=1, keepdims=True)
        row = jnp.where(used, scaled, 0.0) + jnp.where(lane == count, constant, 0.0)
        row = row + pltpu.roll(-0.5 * inverse, pad, 1)
        parts = split3(row * LOG2E)
        for index, part in enumerate(parts):
            part = part.astype(f32)
            tiled = part + pltpu.roll(part, 2 * pad, 1) + pltpu.roll(part, 4 * pad, 1)
            table[index * comps : (index + 1) * comps, :] = tiled.astype(bf16)
        total[...] = jnp.zeros_like(total)

    weights = table[:, : 6 * pad]
    def scores(j, first):
        span = slice(first * LANES, (first + chunk) * LANES)
        if last:
            operand = split_ref[j, :, span]
        else:
            base = pl.multiple_of((step * together + j) * pad, 8)
            values = jnp.concatenate(
                [
                    feat_ref[first + y, pl.ds(base, pad), :] - shift_ref[...]
                    for y in range(chunk)
                ],
                axis=1,
            )
            both = jnp.concatenate([values, values * values], axis=0)
            operand = jnp.concatenate(split3(both), axis=0)
            split_ref[j, :, span] = operand
        wide_score = jnp.dot(weights, operand, preferred_element_type=f32)
        score = wide_score[:comps] + (
            wide_score[comps : 2 * comps] + wide_score[2 * comps : 3 * comps]
        )
        return operand, score

    pieces = [(j, first) for j in range(together) for first in range(0, cols, chunk)]
    ahead = scores(*pieces[0])
    moment = total[...]
    for index, (j, first) in enumerate(pieces):
        operand, score = ahead
        if index + 1 < len(pieces):
            ahead = scores(*pieces[index + 1])
        exponent = jnp.exp2(score - jnp.max(score, axis=0, keepdims=True))
        share = exponent * (1.0 / jnp.sum(exponent, axis=0, keepdims=True))
        high = share.astype(bf16)
        low = (share - high.astype(f32)).astype(bf16)
        moment = moment + lax.dot_general(
            jnp.concatenate([high, low], axis=0),
            operand[: 4 * pad],
            (((1,), (1,)), ((), ())),
            preferred_element_type=f32,
        )
        if last:
            for y in range(chunk):
                wide[pl.ds((j * comps) * cols + first + y, comps, stride=cols), :] = share[
                    :, y * LANES : (y + 1) * LANES
                ]
    total[...] = moment
    if last:
        for j in range(together):
            for k in range(comps):
                start = (j * comps + k) * cols
                post_ref[j, k] = wide[start : start + cols, :].astype(bf16)

    @pl.when(step == pl.num_programs(0) - 1)
    def _():
        both = total[:comps] + total[comps:]
        both = jnp.concatenate([both, jnp.zeros((comps, LANES - 4 * pad), f32)], axis=1)
        summed = both + pltpu.roll(both, LANES - 2 * pad, 1)
        lane = lax.broadcasted_iota(jnp.int32, (comps, LANES), 1)
        summed = jnp.where(lane < 2 * pad, summed, 0.0)
        half = comps // 2
        folded = summed[:half] + pltpu.roll(summed[half:], LANES // 2, 1)
        if last:
            moment_ref[...] = folded
        else:
            payload[...] = folded
            moment_ref[...] = gather_sum(inlines, xlines, payload, slots, send_sem, recv_sem)


def moments(features, split, summed, init, count, rows, cells):
    last = summed is not None
    inlines, xlines = lax.axis_size("inline"), lax.axis_size("xline")
    comps = init[0].shape[1]
    cols, flat, samples = features.shape
    pad = flat // rows
    assert 4 * pad <= LANES and comps % 16 == 0
    chunk = 4
    together = 4
    folded = jax.ShapeDtypeStruct((comps // 2, LANES), f32)
    inputs = ([summed] if last else []) + list(init)
    out_shape, out_specs = [folded], [pl.BlockSpec(folded.shape, lambda j: (0, 0))]
    split_shape = (rows, 6 * pad, cols * samples)
    split_spec = pl.BlockSpec((together,) + split_shape[1:], lambda j: (j, 0, 0))
    scratch = [
        pltpu.VMEM((3 * comps, 2 * LANES), bf16),
        pltpu.VMEM((2 * comps, 4 * pad), f32),
    ]
    params = dict(vmem_limit_bytes=24 << 20)
    if last:
        out_shape.append(jax.ShapeDtypeStruct((rows, comps, cols, samples), bf16))
        out_specs.append(pl.BlockSpec((together, comps, cols, samples), lambda j: (j, 0, 0, 0)))
        scratch.append(pltpu.VMEM((together * comps * cols, samples), f32))
    else:
        out_shape.append(jax.ShapeDtypeStruct(split_shape, bf16))
        out_specs.append(split_spec)
        scratch += [pltpu.VMEM((pad, LANES), f32), pltpu.VMEM(folded.shape, f32)]
        scratch += gather_scratch(inlines * xlines, comps)
        params.update(collective_id=1, has_side_effects=True)
    sizes = (cols, pad, count, chunk, together, cells, inlines, xlines)
    return pl.pallas_call(
        functools.partial(moment_kernel, sizes, last),
        out_shape=out_shape,
        grid=(rows // together,),
        in_specs=[split_spec if last else pl.BlockSpec(memory_space=VMEM)]
        + [pl.BlockSpec(array.shape, lambda j: (0, 0)) for array in inputs],
        out_specs=out_specs,
        scratch_shapes=scratch,
        compiler_params=pltpu.CompilerParams(**params),
        name="last_pass" if last else "first_pass",
    )(split if last else features, *inputs)


def sum_kernel(inlines, xlines, moment_ref, out_ref, slots, send_sem, recv_sem):
    greet(inlines, xlines)
    out_ref[...] = gather_sum(inlines, xlines, moment_ref, slots, send_sem, recv_sem)


def sum_moments(moment):
    inlines, xlines = lax.axis_size("inline"), lax.axis_size("xline")
    return pl.pallas_call(
        functools.partial(sum_kernel, inlines, xlines),
        out_shape=jax.ShapeDtypeStruct(moment.shape, f32),
        in_specs=[pl.BlockSpec(memory_space=VMEM)],
        out_specs=pl.BlockSpec(memory_space=VMEM),
        scratch_shapes=gather_scratch(inlines * xlines, 2 * moment.shape[0]),
        compiler_params=pltpu.CompilerParams(
            collective_id=2, has_side_effects=True, vmem_limit_bytes=4 << 20
        ),
        name="sum_moments",
    )(moment)


def final_kernel(sizes, *refs):
    *sums, mean_ref, var_ref, weight_ref, mean_out, var_out, weight_out = refs
    count = sizes[1]
    params, shift_row = first_params(mean_ref, var_ref, weight_ref)
    for summed in sums:
        params = next_params(summed[...], params, sizes)
    means, spreads, weights = params
    comps = means.shape[0]
    blank = jnp.zeros((LANES - comps, LANES), f32)
    turned = [
        jnp.transpose(jnp.concatenate([value, blank], axis=0))[:, :comps]
        for value in (means + shift_row, spreads, weights)
    ]
    mean_out[...] = turned[0][:count]
    var_out[...] = turned[1][:count]
    weight_out[...] = turned[2][:1]


def finish(sums, init, sizes):
    count, comps = init[0].shape
    inputs = sums + list(init)
    return pl.pallas_call(
        functools.partial(final_kernel, sizes),
        out_shape=[
            jax.ShapeDtypeStruct((count, comps), f32),
            jax.ShapeDtypeStruct((count, comps), f32),
            jax.ShapeDtypeStruct((1, comps), f32),
        ],
        in_specs=[pl.BlockSpec(memory_space=VMEM)] * len(inputs),
        out_specs=[pl.BlockSpec(memory_space=VMEM)] * 3,
        compiler_params=pltpu.CompilerParams(vmem_limit_bytes=4 << 20),
        name="finish",
    )(*inputs)


def per_device(traces, directions, init_means, init_variances, init_weights):
    rows, cols, samples = traces.shape
    assert samples == LANES and rows >= HALF and rows % 8 == 0 and cols % 4 == 0
    count = 2 * directions.shape[0]
    pad = round_up(count + 1, 8)
    comps = init_weights.shape[0]
    cells = lax.axis_size("inline") * rows * lax.axis_size("xline") * cols * samples
    init = (init_means.T, init_variances.T, init_weights.reshape(1, comps))
    halo, *tables = gather_halo(traces, directions)
    features = filter_features(halo, tables, directions, pad)
    summed, split = moments(features, None, None, init, count, rows, cells)
    moment, posterior = moments(features, split, summed, init, count, rows, cells)
    sums = [summed, sum_moments(moment)]
    means, spreads, weights = finish(sums, init, (pad, count, cells))
    return posterior, means.T, spreads.T, weights.reshape(comps)


def solution(mesh):
    in_specs = (P(("slab", "inline"), "xline", None), P(), P(), P(), P())
    out_specs = (
        P(("slab", "inline"), None, "xline", None),
        P("slab", None),
        P("slab", None),
        P("slab"),
    )
    return jax.shard_map(
        per_device, mesh=mesh, in_specs=in_specs, out_specs=out_specs, check_vma=False
    )
```

```python
import functools
import math

import jax
import jax.numpy as jnp
from jax import lax
from jax.experimental import pallas as pl
from jax.experimental.pallas import tpu as pltpu
from jax.sharding import PartitionSpec as P

TAPS = 31
HALF = 15
AZIMUTHS = 8
DIPS = 4
LANES = 128

eps_mag = 0.01
wavenumber = math.pi / 4.0
width_scale = HALF / 3.0
norm = math.sqrt(
    sum(math.exp(-n * n / (width_scale * width_scale)) for n in range(-HALF, HALF + 1))
)
MESH = pl.DeviceIdType.MESH
LOG2E = math.log2(math.e)
f32 = jnp.float32
bf16 = jnp.bfloat16
VMEM = pltpu.MemorySpace.VMEM
SMEM = pltpu.MemorySpace.SMEM
HBM = pltpu.MemorySpace.HBM


def round_up(value, step):
    return -(-value // step) * step


def iotas(shape):
    return (
        lax.broadcasted_iota(jnp.int32, shape, 0),
        lax.broadcasted_iota(jnp.int32, shape, 1),
    )


def roll(value, amount):
    return value if amount == 0 else pltpu.roll(value, amount, 1)


def taps(wave, difference):
    offset = (difference - HALF).astype(f32)
    wave = jnp.concatenate([wave] * (difference.shape[1] // LANES), axis=1)
    wave = jnp.concatenate([wave] * (difference.shape[0] // 8), axis=0)
    phase = offset * wave
    envelope = jnp.exp(-offset * offset / (2.0 * width_scale * width_scale)) / norm
    hit = jnp.logical_and(difference >= 0, difference < TAPS)
    real = jnp.where(hit, envelope * jnp.cos(phase), 0.0)
    imag = jnp.where(hit, envelope * jnp.sin(phase), 0.0)
    return real, imag


def angle(value, step):
    return jnp.full((8, LANES), value.astype(f32)) * step


def time_table(dip, time_ref):
    wave = wavenumber * jnp.cos(angle(dip + 1, math.pi / (2 * DIPS + 2)))
    sub, lane = iotas((8, LANES))
    bases = taps(wave, jnp.bitwise_and(sub - lane + HALF, LANES - 1))
    for s in range(0, LANES, 16):
        pieces = []
        for start in (s, s + 8):
            near = jnp.abs(sub + start - lane) <= HALF
            pieces.append(
                jnp.concatenate([jnp.where(near, roll(base, start), 0.0) for base in bases], axis=1)
            )
        time_ref[dip, s : s + 16, :] = jnp.concatenate(pieces, axis=0).astype(bf16)


def space_tables(orient, direction, sizes, col, x_ref, i_ref):
    rows, cols, width, group = sizes
    lanes = 2 * LANES
    azimuth = angle(direction % AZIMUTHS, math.pi / AZIMUTHS)
    dip_angle = angle(direction // AZIMUTHS + 1, math.pi / (2 * DIPS + 2))
    inline_wave = wavenumber * (jnp.sin(dip_angle) * jnp.cos(azimuth))
    xline_wave = wavenumber * (jnp.sin(dip_angle) * jnp.sin(azimuth))

    sub, lane = iotas((8, lanes))
    row, step = sub % group, sub // group
    place = jnp.where(lane >= group * width, lane - lanes, lane)
    bases = taps(xline_wave, place - row * width - step - col * cols + HALF)
    mine = jnp.logical_and(lane >= row * width, lane < (row + 1) * width)
    per = 8 // group
    for part in range(2):
        for y in range(0, cols, 2 * per):
            pair = jnp.concatenate(
                [jnp.where(mine, roll(bases[part], y + dy), 0.0) for dy in (0, per)], axis=0
            )
            start = (part * cols + y) * group
            x_ref[orient, start : start + 16, :] = pair[:, : group * width].astype(bf16)

    deep = 3 * rows
    half = per * deep
    sub, lane = iotas((rows, lanes))
    imag_in = lane >= half
    within = jnp.where(imag_in, lane - half, lane)
    line = (within // 8) * group + within % group
    step = (within // group) % per
    real, imag = taps(inline_wave, line - sub - rows + HALF)
    blocks = [jnp.where(imag_in, -imag, real), jnp.where(imag_in, real, imag)]
    for dy in range(per):
        for index, block in enumerate(blocks):
            start = (dy * 2 + index) * rows
            value = jnp.where(step == dy, block, 0.0)
            i_ref[orient, start : start + rows, :] = value[:, : 2 * half].astype(bf16)


def feature_kernel(inlines, xlines, sizes, *refs):
    rows, cols, width, pad, orients, group = sizes
    dir_in, own_ref, out_ref, dir_ref, halo, time_ref, x_ref, i_ref, band, cross, *sems = refs
    send_sem, recv_sem, local_sem = sems
    per = 8 // group
    deep = 3 * rows
    half = per * deep
    span = group * width
    pairs = cols // per
    block = rows * width
    steps = deep // (2 * group)
    row = lax.axis_index("inline")
    col = lax.axis_index("xline")
    mine = pl.ds(pl.multiple_of(col * cols, 8), cols)

    def there(side):
        return row > 0 if side < 0 else row < inlines - 1

    barrier = pltpu.get_barrier_semaphore()
    for side in (-1, 1):
        @pl.when(there(side))
        def _(side=side):
            pl.semaphore_signal(
                barrier, inc=1, device_id={"inline": row + side}, device_id_type=MESH
            )
    for shift in range(1, xlines):
        pl.semaphore_signal(
            barrier,
            inc=1,
            device_id={"xline": lax.rem(col + shift, xlines)},
            device_id_type=MESH,
        )
    own = pltpu.make_async_copy(own_ref, halo.at[1, :, mine], local_sem.at[0])
    own.start()
    named = pltpu.make_async_copy(dir_in, dir_ref, local_sem.at[1])
    named.start()
    sides = (row > 0).astype(jnp.int32) + (row < inlines - 1).astype(jnp.int32)
    pl.semaphore_wait(barrier, sides + xlines - 1)

    def along_line(side):
        return pltpu.make_async_remote_copy(
            src_ref=own_ref,
            dst_ref=halo.at[1 - side, :, mine],
            send_sem=send_sem.at[1 - side, 0],
            recv_sem=recv_sem.at[1 - side, 0],
            device_id={"inline": row + side},
            device_id_type=MESH,
        )

    def to_partner(part, shift):
        return pltpu.make_async_remote_copy(
            src_ref=own_ref if part == 1 else halo.at[part, :, mine],
            dst_ref=halo.at[part, :, mine],
            send_sem=send_sem.at[part, shift],
            recv_sem=recv_sem.at[part, shift],
            device_id={"xline": lax.rem(col + shift, xlines)},
            device_id_type=MESH,
        )

    for side in (-1, 1):
        @pl.when(there(side))
        def _(side=side):
            along_line(side).start()
    for shift in range(1, xlines):
        to_partner(1, shift).start()

    for side in (-1, 1):
        @pl.when(jnp.logical_not(there(side)))
        def _(side=side):
            halo[1 + side] = jnp.zeros(halo.shape[1:], halo.dtype)

    @pl.loop(0, DIPS)
    def _(dip):
        time_table(dip, time_ref)

    named.wait()

    @pl.loop(0, orients)
    def _(orient):
        space_tables(
            orient, dir_ref[orient], (rows, cols, width, group), col, x_ref, i_ref
        )

    def make_band(part):
        @pl.loop(0, DIPS)
        def _(dip):
            band[dip, part * block : (part + 1) * block, :] = jnp.dot(
                halo[part].reshape(block, LANES), time_ref[dip], preferred_element_type=f32
            ).astype(bf16)

    def across(orient, dip, step):
        mixed = [
            jnp.dot(
                x_ref[orient],
                band[dip, (2 * step + h) * span : (2 * step + h + 1) * span, :],
                preferred_element_type=f32,
            )
            for h in range(2)
        ]
        for yp in range(pairs):
            slots = [[], [], [], []]
            for h in range(2):
                with_cos = mixed[h][yp * 8 : (yp + 1) * 8]
                with_sin = mixed[h][(pairs + yp) * 8 : (pairs + yp + 1) * 8]
                cu, cv = with_cos[:, :LANES], with_cos[:, LANES:]
                su, sv = with_sin[:, :LANES], with_sin[:, LANES:]
                for slot, value in zip(slots, (cu - sv, su + cv, cu + sv, su - cv)):
                    slot.append(value)
            for index, slot in enumerate(slots):
                q, r = index // 2, index % 2
                start = ((q * pairs + yp) * 2 + r) * half + step * 16
                cross[orient, start : start + 16, :] = jnp.concatenate(slot, axis=0).astype(bf16)

    def along(orient, q, j):
        start = (q * pairs + 2 * j) * 2 * half
        operand = jnp.concatenate(
            [
                cross[orient, start : start + 2 * half, :],
                cross[orient, start + 2 * half : start + 4 * half, :],
            ],
            axis=1,
        )
        total = jnp.dot(i_ref[orient], operand, preferred_element_type=f32)
        for dy in range(per):
            re = total[(2 * dy) * rows : (2 * dy + 1) * rows]
            im = total[(2 * dy + 1) * rows : (2 * dy + 2) * rows]
            square = re * re + im * im + eps_mag
            size = square * lax.rsqrt(square)
            for h in range(2):
                out_ref[
                    (2 * j + h) * per + dy, pl.ds(2 * orient + q, rows, stride=pad), :
                ] = size[:, h * LANES : (h + 1) * LANES]

    inner = range(steps // 3, 2 * steps // 3)
    outer = [step for step in range(steps) if step not in inner]

    def dip_of(orient):
        return dir_ref[orient] // AZIMUTHS

    def own_rows(first, last):
        @pl.loop(first, last)
        def _(orient):
            for step in inner:
                across(orient, dip_of(orient), step)

    own.wait()
    for shift in range(1, xlines):
        to_partner(1, shift).wait_recv()
    make_band(1)
    own_rows(0, orients // 2)
    for side in (-1, 1):
        @pl.when(there(side))
        def _(side=side):
            along_line(-side).wait_recv()
            for shift in range(1, xlines):
                to_partner(1 + side, shift).start()
    own_rows(orients // 2, orients)
    for y in range(cols):
        for extra in range(pad - 2 * orients):
            out_ref[y, pl.ds(2 * orients + extra, rows, stride=pad), :] = jnp.full(
                (rows, LANES), 1.0 if extra == 0 else 0.0, f32
            )
    for shift in range(1, xlines):
        to_partner(1, shift).wait_send()
    for side in (-1, 1):
        @pl.when(there(side))
        def _(side=side):
            along_line(side).wait_send()
            for shift in range(1, xlines):
                to_partner(1 + side, shift).wait()
    make_band(0)
    make_band(2)

    for step in outer:
        across(0, dip_of(0), step)

    pieces = [(q, j) for q in range(2) for j in range(pairs // 2)]
    share = -(-len(pieces) // len(outer))

    @pl.loop(1, orients)
    def _(orient):
        dip = dip_of(orient)
        for index, step in enumerate(outer):
            across(orient, dip, step)
            for q, j in pieces[index * share : (index + 1) * share]:
                along(orient - 1, q, j)

    for q, j in pieces:
        along(orients - 1, q, j)


def make_features(traces, directions, pad):
    inlines, xlines = lax.axis_size("inline"), lax.axis_size("xline")
    rows, cols, samples = traces.shape
    orients = directions.shape[0]
    width = xlines * cols
    group = 4
    assert group * width + cols <= 2 * LANES
    per = 8 // group
    sizes = (rows, cols, width, pad, orients, group)
    return pl.pallas_call(
        functools.partial(feature_kernel, inlines, xlines, sizes),
        out_shape=jax.ShapeDtypeStruct((cols, rows * pad, samples), f32),
        in_specs=[pl.BlockSpec(memory_space=HBM)] * 2,
        out_specs=pl.BlockSpec(memory_space=VMEM),
        scratch_shapes=[
            pltpu.SMEM((orients,), jnp.int32),
            pltpu.VMEM((3, rows, width, samples), bf16),
            pltpu.VMEM((DIPS, samples, 2 * samples), bf16),
            pltpu.VMEM((orients, 2 * cols * group, group * width), bf16),
            pltpu.VMEM((orients, 2 * per * rows, 2 * per * 3 * rows), bf16),
            pltpu.VMEM((DIPS, 3 * rows * width, 2 * samples), bf16),
            pltpu.VMEM((orients, 4 * cols * 3 * rows, samples), bf16),
            pltpu.SemaphoreType.DMA((3, xlines)),
            pltpu.SemaphoreType.DMA((3, xlines)),
            pltpu.SemaphoreType.DMA((2,)),
        ],
        compiler_params=pltpu.CompilerParams(
            collective_id=0, has_side_effects=True, vmem_limit_bytes=40 << 20
        ),
        name="features",
    )(
        pltpu.with_memory_space_constraint(directions, HBM),
        pltpu.with_memory_space_constraint(traces, HBM),
    )


def split3(value):
    high = value.astype(bf16)
    rest = value - high.astype(f32)
    mid = rest.astype(bf16)
    low = (rest - mid.astype(f32)).astype(bf16)
    return high, mid, low


def column(row):
    return jnp.transpose(jnp.broadcast_to(row, (row.shape[1], row.shape[1])))


def padded(value, fill):
    rows, lanes = value.shape
    wide = jnp.concatenate([value, jnp.full((rows, LANES - lanes), fill, f32)], axis=1)
    full = jnp.concatenate([wide, jnp.full((LANES - rows, LANES), fill, f32)], axis=0)
    return jnp.transpose(full)


def first_params(mean_ref, var_ref, weight_ref):
    comps = mean_ref.shape[1]
    means = padded(mean_ref[...], 0.0)[:comps]
    shift_row = jnp.mean(means, axis=0, keepdims=True)
    weights = jnp.broadcast_to(padded(weight_ref[...], 1.0)[:comps, :1], (comps, LANES))
    return (means - shift_row, padded(var_ref[...], 1.0)[:comps], weights), shift_row


def next_params(folded, params, sizes):
    pad, count, cells = sizes
    means, spreads, _ = params
    comps = means.shape[0]
    total = jnp.concatenate([folded, pltpu.roll(folded, LANES // 2, 1)], axis=0)
    used = lax.broadcasted_iota(jnp.int32, (comps, LANES), 1) < count
    mass = total[:, count : count + 1]
    first = jnp.where(used, total, 0.0)
    second = jnp.where(used, pltpu.roll(total, LANES - pad, 1), 0.0)
    below = mass + 1.0
    new_means = (first + means) / below
    centred = second - 2.0 * new_means * first + new_means * new_means * mass
    new_spreads = jnp.where(used, (centred + spreads) / below, 1.0)
    return new_means, new_spreads, jnp.broadcast_to(below / (cells + comps), (comps, LANES))


def peer(shift, inlines, xlines):
    me = lax.axis_index("inline") * xlines + lax.axis_index("xline")
    other = lax.rem(me + shift, inlines * xlines)
    return {"inline": other // xlines, "xline": lax.rem(other, xlines)}


def greet(inlines, xlines):
    barrier = pltpu.get_barrier_semaphore()
    for shift in range(1, inlines * xlines):
        pl.semaphore_signal(
            barrier, inc=1, device_id=peer(shift, inlines, xlines), device_id_type=MESH
        )


def gather_sum(inlines, xlines, payload_ref, slots, send_sem, recv_sem):
    members = inlines * xlines
    me = lax.axis_index("inline") * xlines + lax.axis_index("xline")
    pl.semaphore_wait(pltpu.get_barrier_semaphore(), members - 1)

    def copy(shift):
        return pltpu.make_async_remote_copy(
            src_ref=payload_ref,
            dst_ref=slots.at[me],
            send_sem=send_sem.at[shift],
            recv_sem=recv_sem.at[shift],
            device_id=peer(shift, inlines, xlines),
            device_id_type=MESH,
        )

    for shift in range(1, members):
        copy(shift).start()
    slots[me] = payload_ref[...]
    for shift in range(1, members):
        copy(shift).wait()
    total = slots[0]
    for member in range(1, members):
        total = total + slots[member]
    return total


def gather_scratch(members, comps):
    return [
        pltpu.VMEM((members, comps // 2, LANES), f32),
        pltpu.SemaphoreType.DMA((members,)),
        pltpu.SemaphoreType.DMA((members,)),
    ]


def moment_kernel(sizes, last, *refs):
    cols, pad, count, chunk, together, cells, inlines, xlines = sizes
    if last:
        split_ref, sum_ref, mean_ref, var_ref, weight_ref, *refs = refs
        moment_ref, post_ref, table, total, wide = refs
    else:
        feat_ref, mean_ref, var_ref, weight_ref, *refs = refs
        moment_ref, split_ref, table, total, shift_ref, payload, slots, send_sem, recv_sem = refs
    step = pl.program_id(0)
    comps = mean_ref.shape[1]

    @pl.when(step == 0)
    def _():
        if not last:
            greet(inlines, xlines)
        params, shift_row = first_params(mean_ref, var_ref, weight_ref)
        if last:
            params = next_params(sum_ref[...], params, (pad, count, cells))
        else:
            shift_ref[...] = column(shift_row)[:pad]
        lane = lax.broadcasted_iota(jnp.int32, (comps, 2 * LANES), 1)
        means = jnp.concatenate([params[0], jnp.zeros((comps, LANES), f32)], axis=1)
        spreads = jnp.concatenate([params[1], jnp.ones((comps, LANES), f32)], axis=1)
        used = lane < count
        inverse = jnp.where(used, 1.0 / spreads, 0.0)
        scaled = means * inverse
        terms = jnp.where(used, jnp.log(2.0 * math.pi * spreads) + means * scaled, 0.0)
        constant = jnp.log(params[2][:, :1]) - 0.5 * jnp.sum(terms, axis=1, keepdims=True)
        row = jnp.where(used, scaled, 0.0) + jnp.where(lane == count, constant, 0.0)
        row = row + pltpu.roll(-0.5 * inverse, pad, 1)
        parts = split3(row * LOG2E)
        for index, part in enumerate(parts):
            part = part.astype(f32)
            tiled = part + pltpu.roll(part, 2 * pad, 1) + pltpu.roll(part, 4 * pad, 1)
            table[index * comps : (index + 1) * comps, :] = tiled.astype(bf16)
        total[...] = jnp.zeros_like(total)

    weights = table[:, : 6 * pad]
    def scores(j, first):
        span = slice(first * LANES, (first + chunk) * LANES)
        if last:
            operand = split_ref[j, :, span]
        else:
            base = pl.multiple_of((step * together + j) * pad, 8)
            values = jnp.concatenate(
                [
                    feat_ref[first + y, pl.ds(base, pad), :] - shift_ref[...]
                    for y in range(chunk)
                ],
                axis=1,
            )
            both = jnp.concatenate([values, values * values], axis=0)
            operand = jnp.concatenate(split3(both), axis=0)
            split_ref[j, :, span] = operand
        wide_score = jnp.dot(weights, operand, preferred_element_type=f32)
        score = wide_score[:comps] + (
            wide_score[comps : 2 * comps] + wide_score[2 * comps : 3 * comps]
        )
        return operand, score

    pieces = [(j, first) for j in range(together) for first in range(0, cols, chunk)]
    ahead = scores(*pieces[0])
    moment = total[...]
    for index, (j, first) in enumerate(pieces):
        operand, score = ahead
        if index + 1 < len(pieces):
            ahead = scores(*pieces[index + 1])
        exponent = jnp.exp2(score - jnp.max(score, axis=0, keepdims=True))
        share = exponent * (1.0 / jnp.sum(exponent, axis=0, keepdims=True))
        high = share.astype(bf16)
        low = (share - high.astype(f32)).astype(bf16)
        moment = moment + lax.dot_general(
            jnp.concatenate([high, low], axis=0),
            operand[: 4 * pad],
            (((1,), (1,)), ((), ())),
            preferred_element_type=f32,
        )
        if last:
            for y in range(chunk):
                wide[pl.ds((j * comps) * cols + first + y, comps, stride=cols), :] = share[
                    :, y * LANES : (y + 1) * LANES
                ]
    total[...] = moment
    if last:
        for j in range(together):
            for k in range(comps):
                start = (j * comps + k) * cols
                post_ref[j, k] = wide[start : start + cols, :].astype(bf16)

    @pl.when(step == pl.num_programs(0) - 1)
    def _():
        both = total[:comps] + total[comps:]
        both = jnp.concatenate([both, jnp.zeros((comps, LANES - 4 * pad), f32)], axis=1)
        summed = both + pltpu.roll(both, LANES - 2 * pad, 1)
        lane = lax.broadcasted_iota(jnp.int32, (comps, LANES), 1)
        summed = jnp.where(lane < 2 * pad, summed, 0.0)
        half = comps // 2
        folded = summed[:half] + pltpu.roll(summed[half:], LANES // 2, 1)
        if last:
            moment_ref[...] = folded
        else:
            payload[...] = folded
            moment_ref[...] = gather_sum(inlines, xlines, payload, slots, send_sem, recv_sem)


def moments(features, split, summed, init, count, rows, cells):
    last = summed is not None
    inlines, xlines = lax.axis_size("inline"), lax.axis_size("xline")
    comps = init[0].shape[1]
    cols, flat, samples = features.shape
    pad = flat // rows
    assert 4 * pad <= LANES and comps % 16 == 0
    chunk = 4
    together = 4
    folded = jax.ShapeDtypeStruct((comps // 2, LANES), f32)
    inputs = ([summed] if last else []) + list(init)
    out_shape, out_specs = [folded], [pl.BlockSpec(folded.shape, lambda j: (0, 0))]
    split_shape = (rows, 6 * pad, cols * samples)
    split_spec = pl.BlockSpec((together,) + split_shape[1:], lambda j: (j, 0, 0))
    scratch = [
        pltpu.VMEM((3 * comps, 2 * LANES), bf16),
        pltpu.VMEM((2 * comps, 4 * pad), f32),
    ]
    params = dict(vmem_limit_bytes=24 << 20)
    if last:
        out_shape.append(jax.ShapeDtypeStruct((rows, comps, cols, samples), bf16))
        out_specs.append(pl.BlockSpec((together, comps, cols, samples), lambda j: (j, 0, 0, 0)))
        scratch.append(pltpu.VMEM((together * comps * cols, samples), f32))
    else:
        out_shape.append(jax.ShapeDtypeStruct(split_shape, bf16))
        out_specs.append(split_spec)
        scratch += [pltpu.VMEM((pad, LANES), f32), pltpu.VMEM(folded.shape, f32)]
        scratch += gather_scratch(inlines * xlines, comps)
        params.update(collective_id=1, has_side_effects=True)
    sizes = (cols, pad, count, chunk, together, cells, inlines, xlines)
    return pl.pallas_call(
        functools.partial(moment_kernel, sizes, last),
        out_shape=out_shape,
        grid=(rows // together,),
        in_specs=[split_spec if last else pl.BlockSpec(memory_space=VMEM)]
        + [pl.BlockSpec(array.shape, lambda j: (0, 0)) for array in inputs],
        out_specs=out_specs,
        scratch_shapes=scratch,
        compiler_params=pltpu.CompilerParams(**params),
        name="last_pass" if last else "first_pass",
    )(split if last else features, *inputs)


def sum_kernel(inlines, xlines, moment_ref, out_ref, slots, send_sem, recv_sem):
    greet(inlines, xlines)
    out_ref[...] = gather_sum(inlines, xlines, moment_ref, slots, send_sem, recv_sem)


def sum_moments(moment):
    inlines, xlines = lax.axis_size("inline"), lax.axis_size("xline")
    return pl.pallas_call(
        functools.partial(sum_kernel, inlines, xlines),
        out_shape=jax.ShapeDtypeStruct(moment.shape, f32),
        in_specs=[pl.BlockSpec(memory_space=VMEM)],
        out_specs=pl.BlockSpec(memory_space=VMEM),
        scratch_shapes=gather_scratch(inlines * xlines, 2 * moment.shape[0]),
        compiler_params=pltpu.CompilerParams(
            collective_id=2, has_side_effects=True, vmem_limit_bytes=4 << 20
        ),
        name="sum_moments",
    )(moment)


def final_kernel(sizes, *refs):
    *sums, mean_ref, var_ref, weight_ref, mean_out, var_out, weight_out = refs
    count = sizes[1]
    params, shift_row = first_params(mean_ref, var_ref, weight_ref)
    for summed in sums:
        params = next_params(summed[...], params, sizes)
    means, spreads, weights = params
    comps = means.shape[0]
    blank = jnp.zeros((LANES - comps, LANES), f32)
    turned = [
        jnp.transpose(jnp.concatenate([value, blank], axis=0))[:, :comps]
        for value in (means + shift_row, spreads, weights)
    ]
    mean_out[...] = turned[0][:count]
    var_out[...] = turned[1][:count]
    weight_out[...] = turned[2][:1]


def finish(sums, init, sizes):
    count, comps = init[0].shape
    inputs = sums + list(init)
    return pl.pallas_call(
        functools.partial(final_kernel, sizes),
        out_shape=[
            jax.ShapeDtypeStruct((count, comps), f32),
            jax.ShapeDtypeStruct((count, comps), f32),
            jax.ShapeDtypeStruct((1, comps), f32),
        ],
        in_specs=[pl.BlockSpec(memory_space=VMEM)] * len(inputs),
        out_specs=[pl.BlockSpec(memory_space=VMEM)] * 3,
        compiler_params=pltpu.CompilerParams(vmem_limit_bytes=4 << 20),
        name="finish",
    )(*inputs)


def per_device(traces, directions, init_means, init_variances, init_weights):
    rows, cols, samples = traces.shape
    assert samples == LANES and rows >= HALF and rows % 8 == 0 and cols % 4 == 0
    count = 2 * directions.shape[0]
    pad = round_up(count + 1, 8)
    comps = init_weights.shape[0]
    cells = lax.axis_size("inline") * rows * lax.axis_size("xline") * cols * samples
    init = (init_means.T, init_variances.T, init_weights.reshape(1, comps))
    features = make_features(traces, directions, pad)
    summed, split = moments(features, None, None, init, count, rows, cells)
    moment, posterior = moments(features, split, summed, init, count, rows, cells)
    sums = [summed, sum_moments(moment)]
    means, spreads, weights = finish(sums, init, (pad, count, cells))
    return posterior, means.T, spreads.T, weights.reshape(comps)


def solution(mesh):
    in_specs = (P(("slab", "inline"), "xline", None), P(), P(), P(), P())
    out_specs = (
        P(("slab", "inline"), None, "xline", None),
        P("slab", None),
        P("slab", None),
        P("slab"),
    )
    return jax.shard_map(
        per_device, mesh=mesh, in_specs=in_specs, out_specs=out_specs, check_vma=False
    )
```

```python
import functools
import math

import jax
import jax.numpy as jnp
from jax import lax
from jax.experimental import pallas as pl
from jax.experimental.pallas import tpu as pltpu
from jax.sharding import PartitionSpec as P

TAPS = 31
HALF = 15
AZIMUTHS = 8
DIPS = 4
LANES = 128

eps_mag = 0.01
wavenumber = math.pi / 4.0
width_scale = HALF / 3.0
norm = math.sqrt(
    sum(math.exp(-n * n / (width_scale * width_scale)) for n in range(-HALF, HALF + 1))
)
MESH = pl.DeviceIdType.MESH
LOG2E = math.log2(math.e)
f32 = jnp.float32
bf16 = jnp.bfloat16
VMEM = pltpu.MemorySpace.VMEM
SMEM = pltpu.MemorySpace.SMEM
HBM = pltpu.MemorySpace.HBM


def round_up(value, step):
    return -(-value // step) * step


def iotas(shape):
    return (
        lax.broadcasted_iota(jnp.int32, shape, 0),
        lax.broadcasted_iota(jnp.int32, shape, 1),
    )


def roll(value, amount):
    return value if amount == 0 else pltpu.roll(value, amount, 1)


def taps(wave, difference):
    offset = (difference - HALF).astype(f32)
    wave = jnp.concatenate([wave] * (difference.shape[1] // LANES), axis=1)
    wave = jnp.concatenate([wave] * (difference.shape[0] // 8), axis=0)
    phase = offset * wave
    envelope = jnp.exp(-offset * offset / (2.0 * width_scale * width_scale)) / norm
    hit = jnp.logical_and(difference >= 0, difference < TAPS)
    real = jnp.where(hit, envelope * jnp.cos(phase), 0.0)
    imag = jnp.where(hit, envelope * jnp.sin(phase), 0.0)
    return real, imag


def angle(value, step):
    return jnp.full((8, LANES), value.astype(f32)) * step


def time_table(dip, time_ref):
    wave = wavenumber * jnp.cos(angle(dip + 1, math.pi / (2 * DIPS + 2)))
    sub, lane = iotas((8, LANES))
    bases = taps(wave, jnp.bitwise_and(sub - lane + HALF, LANES - 1))
    for s in range(0, LANES, 16):
        pieces = []
        for start in (s, s + 8):
            near = jnp.abs(sub + start - lane) <= HALF
            pieces.append(
                jnp.concatenate([jnp.where(near, roll(base, start), 0.0) for base in bases], axis=1)
            )
        time_ref[dip, s : s + 16, :] = jnp.concatenate(pieces, axis=0).astype(bf16)


def space_tables(orient, direction, sizes, col, x_ref, i_ref):
    rows, cols, width, group = sizes
    lanes = 2 * LANES
    azimuth = angle(direction % AZIMUTHS, math.pi / AZIMUTHS)
    dip_angle = angle(direction // AZIMUTHS + 1, math.pi / (2 * DIPS + 2))
    inline_wave = wavenumber * (jnp.sin(dip_angle) * jnp.cos(azimuth))
    xline_wave = wavenumber * (jnp.sin(dip_angle) * jnp.sin(azimuth))

    sub, lane = iotas((8, lanes))
    row, step = sub % group, sub // group
    place = jnp.where(lane >= group * width, lane - lanes, lane)
    bases = taps(xline_wave, place - row * width - step - col * cols + HALF)
    mine = jnp.logical_and(lane >= row * width, lane < (row + 1) * width)
    per = 8 // group
    for part in range(2):
        for y in range(0, cols, 2 * per):
            pair = jnp.concatenate(
                [jnp.where(mine, roll(bases[part], y + dy), 0.0) for dy in (0, per)], axis=0
            )
            start = (part * cols + y) * group
            x_ref[orient, start : start + 16, :] = pair[:, : group * width].astype(bf16)

    deep = 3 * rows
    half = per * deep
    sub, lane = iotas((rows, lanes))
    imag_in = lane >= half
    within = jnp.where(imag_in, lane - half, lane)
    line = (within // 8) * group + within % group
    step = (within // group) % per
    real, imag = taps(inline_wave, line - sub - rows + HALF)
    blocks = [jnp.where(imag_in, -imag, real), jnp.where(imag_in, real, imag)]
    for dy in range(per):
        for index, block in enumerate(blocks):
            start = (dy * 2 + index) * rows
            value = jnp.where(step == dy, block, 0.0)
            i_ref[orient, start : start + rows, :] = value[:, : 2 * half].astype(bf16)


def feature_kernel(inlines, xlines, sizes, *refs):
    rows, cols, width, pad, orients, group = sizes
    dir_in, own_ref, out_ref, dir_ref, halo, time_ref, x_ref, i_ref, band, cross, *sems = refs
    send_sem, recv_sem, local_sem = sems
    per = 8 // group
    deep = 3 * rows
    half = per * deep
    span = group * width
    pairs = cols // per
    block = rows * width
    steps = deep // (2 * group)
    row = lax.axis_index("inline")
    col = lax.axis_index("xline")
    mine = pl.ds(pl.multiple_of(col * cols, 8), cols)

    def there(side):
        return row > 0 if side < 0 else row < inlines - 1

    barrier = pltpu.get_barrier_semaphore()
    for side in (-1, 1):
        @pl.when(there(side))
        def _(side=side):
            pl.semaphore_signal(
                barrier, inc=1, device_id={"inline": row + side}, device_id_type=MESH
            )
    for shift in range(1, xlines):
        pl.semaphore_signal(
            barrier,
            inc=1,
            device_id={"xline": lax.rem(col + shift, xlines)},
            device_id_type=MESH,
        )
    own = pltpu.make_async_copy(own_ref, halo.at[1, :, mine], local_sem.at[0])
    own.start()
    named = pltpu.make_async_copy(dir_in, dir_ref, local_sem.at[1])
    named.start()
    sides = (row > 0).astype(jnp.int32) + (row < inlines - 1).astype(jnp.int32)
    pl.semaphore_wait(barrier, sides + xlines - 1)

    def along_line(side):
        return pltpu.make_async_remote_copy(
            src_ref=own_ref,
            dst_ref=halo.at[1 - side, :, mine],
            send_sem=send_sem.at[1 - side, 0],
            recv_sem=recv_sem.at[1 - side, 0],
            device_id={"inline": row + side},
            device_id_type=MESH,
        )

    def to_partner(part, shift):
        return pltpu.make_async_remote_copy(
            src_ref=own_ref if part == 1 else halo.at[part, :, mine],
            dst_ref=halo.at[part, :, mine],
            send_sem=send_sem.at[part, shift],
            recv_sem=recv_sem.at[part, shift],
            device_id={"xline": lax.rem(col + shift, xlines)},
            device_id_type=MESH,
        )

    for side in (-1, 1):
        @pl.when(there(side))
        def _(side=side):
            along_line(side).start()
    for shift in range(1, xlines):
        to_partner(1, shift).start()

    for side in (-1, 1):
        @pl.when(jnp.logical_not(there(side)))
        def _(side=side):
            halo[1 + side] = jnp.zeros(halo.shape[1:], halo.dtype)

    @pl.loop(0, DIPS)
    def _(dip):
        time_table(dip, time_ref)

    named.wait()

    @pl.loop(0, orients)
    def _(orient):
        space_tables(
            orient, dir_ref[orient], (rows, cols, width, group), col, x_ref, i_ref
        )

    def make_band(part):
        @pl.loop(0, DIPS)
        def _(dip):
            band[dip, part * block : (part + 1) * block, :] = jnp.dot(
                halo[part].reshape(block, LANES), time_ref[dip], preferred_element_type=f32
            ).astype(bf16)

    def across(orient, dip, step):
        mixed = [
            jnp.dot(
                x_ref[orient],
                band[dip, (2 * step + h) * span : (2 * step + h + 1) * span, :],
                preferred_element_type=f32,
            )
            for h in range(2)
        ]
        for yp in range(pairs):
            slots = [[], [], [], []]
            for h in range(2):
                with_cos = mixed[h][yp * 8 : (yp + 1) * 8]
                with_sin = mixed[h][(pairs + yp) * 8 : (pairs + yp + 1) * 8]
                cu, cv = with_cos[:, :LANES], with_cos[:, LANES:]
                su, sv = with_sin[:, :LANES], with_sin[:, LANES:]
                for slot, value in zip(slots, (cu - sv, su + cv, cu + sv, su - cv)):
                    slot.append(value)
            for index, slot in enumerate(slots):
                q, r = index // 2, index % 2
                start = ((q * pairs + yp) * 2 + r) * half + step * 16
                cross[orient, start : start + 16, :] = jnp.concatenate(slot, axis=0).astype(bf16)

    def along(orient, q, j):
        start = (q * pairs + 2 * j) * 2 * half
        operand = jnp.concatenate(
            [
                cross[orient, start : start + 2 * half, :],
                cross[orient, start + 2 * half : start + 4 * half, :],
            ],
            axis=1,
        )
        total = jnp.dot(i_ref[orient], operand, preferred_element_type=f32)
        for dy in range(per):
            re = total[(2 * dy) * rows : (2 * dy + 1) * rows]
            im = total[(2 * dy + 1) * rows : (2 * dy + 2) * rows]
            square = re * re + im * im + eps_mag
            size = square * lax.rsqrt(square)
            for h in range(2):
                out_ref[
                    (2 * j + h) * per + dy, pl.ds(2 * orient + q, rows, stride=pad), :
                ] = size[:, h * LANES : (h + 1) * LANES]

    inner = range(steps // 3, 2 * steps // 3)
    outer = [step for step in range(steps) if step not in inner]

    def dip_of(orient):
        return dir_ref[orient] // AZIMUTHS

    def own_rows(first, last):
        @pl.loop(first, last)
        def _(orient):
            for step in inner:
                across(orient, dip_of(orient), step)

    own.wait()
    for shift in range(1, xlines):
        to_partner(1, shift).wait_recv()
    make_band(1)
    own_rows(0, orients // 2)
    for side in (-1, 1):
        @pl.when(there(side))
        def _(side=side):
            along_line(-side).wait_recv()
            for shift in range(1, xlines):
                to_partner(1 + side, shift).start()
    own_rows(orients // 2, orients)
    for y in range(cols):
        for extra in range(pad - 2 * orients):
            out_ref[y, pl.ds(2 * orients + extra, rows, stride=pad), :] = jnp.full(
                (rows, LANES), 1.0 if extra == 0 else 0.0, f32
            )
    for shift in range(1, xlines):
        to_partner(1, shift).wait_send()
    for side in (-1, 1):
        @pl.when(there(side))
        def _(side=side):
            along_line(side).wait_send()
            for shift in range(1, xlines):
                to_partner(1 + side, shift).wait()
    make_band(0)
    make_band(2)

    for step in outer:
        across(0, dip_of(0), step)

    pieces = [(q, j) for q in range(2) for j in range(pairs // 2)]
    share = -(-len(pieces) // len(outer))

    @pl.loop(1, orients)
    def _(orient):
        dip = dip_of(orient)
        for index, step in enumerate(outer):
            across(orient, dip, step)
            for q, j in pieces[index * share : (index + 1) * share]:
                along(orient - 1, q, j)

    for q, j in pieces:
        along(orients - 1, q, j)


def make_features(traces, directions, pad):
    inlines, xlines = lax.axis_size("inline"), lax.axis_size("xline")
    rows, cols, samples = traces.shape
    orients = directions.shape[0]
    width = xlines * cols
    group = 4
    assert group * width + cols <= 2 * LANES
    per = 8 // group
    sizes = (rows, cols, width, pad, orients, group)
    return pl.pallas_call(
        functools.partial(feature_kernel, inlines, xlines, sizes),
        out_shape=jax.ShapeDtypeStruct((cols, rows * pad, samples), f32),
        in_specs=[pl.BlockSpec(memory_space=HBM)] * 2,
        out_specs=pl.BlockSpec(memory_space=VMEM),
        scratch_shapes=[
            pltpu.SMEM((orients,), jnp.int32),
            pltpu.VMEM((3, rows, width, samples), bf16),
            pltpu.VMEM((DIPS, samples, 2 * samples), bf16),
            pltpu.VMEM((orients, 2 * cols * group, group * width), bf16),
            pltpu.VMEM((orients, 2 * per * rows, 2 * per * 3 * rows), bf16),
            pltpu.VMEM((DIPS, 3 * rows * width, 2 * samples), bf16),
            pltpu.VMEM((orients, 4 * cols * 3 * rows, samples), bf16),
            pltpu.SemaphoreType.DMA((3, xlines)),
            pltpu.SemaphoreType.DMA((3, xlines)),
            pltpu.SemaphoreType.DMA((2,)),
        ],
        compiler_params=pltpu.CompilerParams(
            collective_id=0, has_side_effects=True, vmem_limit_bytes=40 << 20
        ),
        name="features",
    )(
        pltpu.with_memory_space_constraint(directions, HBM),
        pltpu.with_memory_space_constraint(traces, HBM),
    )


def split3(value):
    high = value.astype(bf16)
    rest = value - high.astype(f32)
    mid = rest.astype(bf16)
    low = (rest - mid.astype(f32)).astype(bf16)
    return high, mid, low


def column(row):
    return jnp.transpose(jnp.broadcast_to(row, (row.shape[1], row.shape[1])))


def padded(value, fill):
    rows, lanes = value.shape
    wide = jnp.concatenate([value, jnp.full((rows, LANES - lanes), fill, f32)], axis=1)
    full = jnp.concatenate([wide, jnp.full((LANES - rows, LANES), fill, f32)], axis=0)
    return jnp.transpose(full)


def first_params(mean_ref, var_ref, weight_ref):
    comps = mean_ref.shape[1]
    means = padded(mean_ref[...], 0.0)[:comps]
    shift_row = jnp.mean(means, axis=0, keepdims=True)
    weights = jnp.broadcast_to(padded(weight_ref[...], 1.0)[:comps, :1], (comps, LANES))
    return (means - shift_row, padded(var_ref[...], 1.0)[:comps], weights), shift_row


def next_params(folded, params, sizes):
    pad, count, cells = sizes
    means, spreads, _ = params
    comps = means.shape[0]
    total = jnp.concatenate([folded, pltpu.roll(folded, LANES // 2, 1)], axis=0)
    used = lax.broadcasted_iota(jnp.int32, (comps, LANES), 1) < count
    mass = total[:, count : count + 1]
    first = jnp.where(used, total, 0.0)
    second = jnp.where(used, pltpu.roll(total, LANES - pad, 1), 0.0)
    below = mass + 1.0
    new_means = (first + means) / below
    centred = second - 2.0 * new_means * first + new_means * new_means * mass
    new_spreads = jnp.where(used, (centred + spreads) / below, 1.0)
    return new_means, new_spreads, jnp.broadcast_to(below / (cells + comps), (comps, LANES))


def peers(inlines, xlines):
    row = lax.axis_index("inline")
    col = lax.axis_index("xline")

    def turned(index, shift, size):
        moved = index + shift
        return jnp.where(moved >= size, moved - size, moved) if shift else index

    return [
        {"inline": turned(row, down, inlines), "xline": turned(col, side, xlines)}
        for down in range(inlines)
        for side in range(xlines)
        if down or side
    ]


def gather_sum(others, me, payload, slots, send_sem, recv_sem):
    def copy(index):
        return pltpu.make_async_remote_copy(
            src_ref=payload,
            dst_ref=slots.at[me],
            send_sem=send_sem.at[index],
            recv_sem=recv_sem.at[index],
            device_id=others[index],
            device_id_type=MESH,
        )

    for index in range(len(others)):
        copy(index).start()
    slots[me] = payload[...]
    for index in range(len(others)):
        copy(index).wait()
    total = slots[0]
    for member in range(1, len(others) + 1):
        total = total + slots[member]
    return total


def em_kernel(sizes, *refs):
    cols, pad, count, chunk, together, cells, inlines, xlines = sizes
    feat_ref, mean_ref, var_ref, weight_ref, sum_ref, last_ref, post_ref, *refs = refs
    split_ref, table, total, shift_ref, wide, payload, slots, send_sem, recv_sem = refs
    comps = mean_ref.shape[1]
    rows = post_ref.shape[0]
    me = lax.axis_index("inline") * xlines + lax.axis_index("xline")
    others = peers(inlines, xlines)
    barrier = pltpu.get_barrier_semaphore()
    for other in others:
        pl.semaphore_signal(barrier, inc=1, device_id=other, device_id_type=MESH)

    def prepare(params):
        lane = lax.broadcasted_iota(jnp.int32, (comps, 2 * LANES), 1)
        means = jnp.concatenate([params[0], jnp.zeros((comps, LANES), f32)], axis=1)
        spreads = jnp.concatenate([params[1], jnp.ones((comps, LANES), f32)], axis=1)
        used = lane < count
        inverse = jnp.where(used, 1.0 / spreads, 0.0)
        scaled = means * inverse
        terms = jnp.where(used, jnp.log(2.0 * math.pi * spreads) + means * scaled, 0.0)
        constant = jnp.log(params[2][:, :1]) - 0.5 * jnp.sum(terms, axis=1, keepdims=True)
        row = jnp.where(used, scaled, 0.0) + jnp.where(lane == count, constant, 0.0)
        row = row + pltpu.roll(-0.5 * inverse, pad, 1)
        parts = split3(row * LOG2E)
        for index, part in enumerate(parts):
            part = part.astype(f32)
            tiled = part + pltpu.roll(part, 2 * pad, 1) + pltpu.roll(part, 4 * pad, 1)
            table[index * comps : (index + 1) * comps, :] = tiled.astype(bf16)
        total[...] = jnp.zeros_like(total)

    def sweep(step, last):
        weights = table[:, : 6 * pad]

        def scores(j, first):
            span = slice(first * LANES, (first + chunk) * LANES)
            line = step * together + j
            if last:
                operand = split_ref[line, :, span]
            else:
                base = pl.multiple_of(line * pad, 8)
                values = jnp.concatenate(
                    [
                        feat_ref[first + y, pl.ds(base, pad), :] - shift_ref[...]
                        for y in range(chunk)
                    ],
                    axis=1,
                )
                both = jnp.concatenate([values, values * values], axis=0)
                operand = jnp.concatenate(split3(both), axis=0)
                split_ref[line, :, span] = operand
            wide_score = jnp.dot(weights, operand, preferred_element_type=f32)
            score = wide_score[:comps] + (
                wide_score[comps : 2 * comps] + wide_score[2 * comps : 3 * comps]
            )
            return operand, score

        pieces = [(j, first) for j in range(together) for first in range(0, cols, chunk)]
        ahead = scores(*pieces[0])
        moment = total[...]
        for index, (j, first) in enumerate(pieces):
            operand, score = ahead
            if index + 1 < len(pieces):
                ahead = scores(*pieces[index + 1])
            exponent = jnp.exp2(score - jnp.max(score, axis=0, keepdims=True))
            share = exponent * (1.0 / jnp.sum(exponent, axis=0, keepdims=True))
            high = share.astype(bf16)
            low = (share - high.astype(f32)).astype(bf16)
            moment = moment + lax.dot_general(
                jnp.concatenate([high, low], axis=0),
                operand[: 4 * pad],
                (((1,), (1,)), ((), ())),
                preferred_element_type=f32,
            )
            if last:
                for y in range(chunk):
                    wide[pl.ds((j * comps) * cols + first + y, comps, stride=cols), :] = share[
                        :, y * LANES : (y + 1) * LANES
                    ]
        total[...] = moment
        if last:
            for j in range(together):
                for k in range(comps):
                    start = (j * comps + k) * cols
                    post_ref[step * together + j, k] = wide[start : start + cols, :].astype(bf16)

    def fold():
        both = total[:comps] + total[comps:]
        both = jnp.concatenate([both, jnp.zeros((comps, LANES - 4 * pad), f32)], axis=1)
        summed = both + pltpu.roll(both, LANES - 2 * pad, 1)
        lane = lax.broadcasted_iota(jnp.int32, (comps, LANES), 1)
        summed = jnp.where(lane < 2 * pad, summed, 0.0)
        half = comps // 2
        return summed[:half] + pltpu.roll(summed[half:], LANES // 2, 1)

    params, shift_row = first_params(mean_ref, var_ref, weight_ref)
    shift_ref[...] = column(shift_row)[:pad]
    prepare(params)
    pl.loop(0, rows // together)(lambda step: sweep(step, False))
    payload[0] = fold()
    pl.semaphore_wait(barrier, len(others))
    sum_ref[...] = gather_sum(
        others, me, payload.at[0], slots.at[0], send_sem.at[0], recv_sem.at[0]
    )
    prepare(next_params(sum_ref[...], params, (pad, count, cells)))
    pl.loop(0, rows // together)(lambda step: sweep(step, True))
    payload[1] = fold()
    last_ref[...] = gather_sum(
        others, me, payload.at[1], slots.at[1], send_sem.at[1], recv_sem.at[1]
    )


def mixture(features, init, count, rows, cells):
    inlines, xlines = lax.axis_size("inline"), lax.axis_size("xline")
    members = inlines * xlines
    comps = init[0].shape[1]
    cols, flat, samples = features.shape
    pad = flat // rows
    assert 4 * pad <= LANES and comps % 16 == 0
    chunk = 4
    together = 4
    assert rows % together == 0 and cols % chunk == 0
    folded = (comps // 2, LANES)
    sizes = (cols, pad, count, chunk, together, cells, inlines, xlines)
    return pl.pallas_call(
        functools.partial(em_kernel, sizes),
        out_shape=[
            jax.ShapeDtypeStruct(folded, f32),
            jax.ShapeDtypeStruct(folded, f32),
            jax.ShapeDtypeStruct((rows, comps, cols, samples), bf16),
        ],
        in_specs=[pl.BlockSpec(memory_space=VMEM)] * 4,
        out_specs=[pl.BlockSpec(memory_space=VMEM)] * 3,
        scratch_shapes=[
            pltpu.VMEM((rows, 6 * pad, cols * samples), bf16),
            pltpu.VMEM((3 * comps, 2 * LANES), bf16),
            pltpu.VMEM((2 * comps, 4 * pad), f32),
            pltpu.VMEM((pad, LANES), f32),
            pltpu.VMEM((together * comps * cols, samples), f32),
            pltpu.VMEM((2,) + folded, f32),
            pltpu.VMEM((2, members) + folded, f32),
            pltpu.SemaphoreType.DMA((2, members - 1)),
            pltpu.SemaphoreType.DMA((2, members - 1)),
        ],
        compiler_params=pltpu.CompilerParams(
            collective_id=1, has_side_effects=True, vmem_limit_bytes=36 << 20
        ),
        name="mixture",
    )(features, *init)


def final_kernel(sizes, *refs):
    *sums, post_in, mean_ref, var_ref, weight_ref = refs[:-5]
    mean_out, var_out, weight_out, post_out, sems = refs[-5:]
    count = sizes[1]
    parts = sems.shape[0]
    depth = post_in.shape[0] // parts

    def copy(part):
        span = pl.ds(part * depth, depth)
        return pltpu.make_async_copy(post_in.at[span], post_out.at[span], sems.at[part])

    for part in range(parts):
        copy(part).start()
    params, shift_row = first_params(mean_ref, var_ref, weight_ref)
    for summed in sums:
        params = next_params(summed[...], params, sizes)
    means, spreads, weights = params
    comps = means.shape[0]
    blank = jnp.zeros((LANES - comps, LANES), f32)
    turned = [
        jnp.transpose(jnp.concatenate([value, blank], axis=0))[:, :comps]
        for value in (means + shift_row, spreads, weights)
    ]
    mean_out[...] = turned[0][:count]
    var_out[...] = turned[1][:count]
    weight_out[...] = turned[2][:1]
    for part in range(parts):
        copy(part).wait()


def finish(sums, posterior, init, sizes):
    count, comps = init[0].shape
    inputs = sums + [posterior] + list(init)
    return pl.pallas_call(
        functools.partial(final_kernel, sizes),
        out_shape=[
            jax.ShapeDtypeStruct((count, comps), f32),
            jax.ShapeDtypeStruct((count, comps), f32),
            jax.ShapeDtypeStruct((1, comps), f32),
            jax.ShapeDtypeStruct(posterior.shape, posterior.dtype),
        ],
        in_specs=[pl.BlockSpec(memory_space=VMEM)] * len(inputs),
        out_specs=[pl.BlockSpec(memory_space=VMEM)] * 3 + [pl.BlockSpec(memory_space=HBM)],
        scratch_shapes=[pltpu.SemaphoreType.DMA((math.gcd(8, posterior.shape[0]),))],
        compiler_params=pltpu.CompilerParams(vmem_limit_bytes=4 << 20),
        name="finish",
    )(*inputs)


def per_device(traces, directions, init_means, init_variances, init_weights):
    rows, cols, samples = traces.shape
    assert samples == LANES and rows >= HALF and rows % 8 == 0 and cols % 4 == 0
    count = 2 * directions.shape[0]
    pad = round_up(count + 1, 8)
    comps = init_weights.shape[0]
    cells = lax.axis_size("inline") * rows * lax.axis_size("xline") * cols * samples
    init = (init_means.T, init_variances.T, init_weights.reshape(1, comps))
    features = make_features(traces, directions, pad)
    *sums, posterior = mixture(features, init, count, rows, cells)
    means, spreads, weights, posterior = finish(sums, posterior, init, (pad, count, cells))
    return posterior, means.T, spreads.T, weights.reshape(comps)


def solution(mesh):
    in_specs = (P(("slab", "inline"), "xline", None), P(), P(), P(), P())
    out_specs = (
        P(("slab", "inline"), None, "xline", None),
        P("slab", None),
        P("slab", None),
        P("slab"),
    )
    return jax.shard_map(
        per_device, mesh=mesh, in_specs=in_specs, out_specs=out_specs, check_vma=False
    )
```

```python
import functools
import math

import jax
import jax.numpy as jnp
from jax import lax
from jax.experimental import pallas as pl
from jax.experimental.pallas import tpu as pltpu
from jax.sharding import PartitionSpec as P

TAPS = 31
HALF = 15
AZIMUTHS = 8
DIPS = 4
LANES = 128

eps_mag = 0.01
wavenumber = math.pi / 4.0
width_scale = HALF / 3.0
norm = math.sqrt(
    sum(math.exp(-n * n / (width_scale * width_scale)) for n in range(-HALF, HALF + 1))
)
MESH = pl.DeviceIdType.MESH
LOG2E = math.log2(math.e)
f32 = jnp.float32
bf16 = jnp.bfloat16
VMEM = pltpu.MemorySpace.VMEM
SMEM = pltpu.MemorySpace.SMEM
HBM = pltpu.MemorySpace.HBM


def round_up(value, step):
    return -(-value // step) * step


def iotas(shape):
    return (
        lax.broadcasted_iota(jnp.int32, shape, 0),
        lax.broadcasted_iota(jnp.int32, shape, 1),
    )


def roll(value, amount):
    return value if amount == 0 else pltpu.roll(value, amount, 1)


def taps(wave, difference):
    offset = (difference - HALF).astype(f32)
    phase = offset * jnp.concatenate([wave] * (difference.shape[1] // LANES), axis=1)
    envelope = jnp.exp(-offset * offset / (2.0 * width_scale * width_scale)) / norm
    hit = jnp.logical_and(difference >= 0, difference < TAPS)
    real = jnp.where(hit, envelope * jnp.cos(phase), 0.0)
    imag = jnp.where(hit, envelope * jnp.sin(phase), 0.0)
    return real, imag


def time_table(dip, time_ref):
    dip_angle = jnp.full((8, LANES), (dip + 1).astype(f32)) * (math.pi / (2 * DIPS + 2))
    wave = wavenumber * jnp.cos(dip_angle)
    sub, lane = iotas((8, LANES))
    bases = taps(wave, jnp.bitwise_and(sub - lane + HALF, LANES - 1))
    for s in range(0, LANES, 16):
        pieces = []
        for start in (s, s + 8):
            near = jnp.abs(sub + start - lane) <= HALF
            pieces.append(
                jnp.concatenate([jnp.where(near, roll(base, start), 0.0) for base in bases], axis=1)
            )
        time_ref[dip, s : s + 16, :] = jnp.concatenate(pieces, axis=0).astype(bf16)


def space_taps(orients, dir_ref, sizes, col, xtap_ref, itap_ref):
    rows, cols, width, group = sizes
    lanes = 2 * LANES
    per = 8 // group
    height = xtap_ref.shape[1]
    sub, lane = iotas((height, LANES))
    azimuth, dip = jnp.zeros((height, LANES), f32), jnp.zeros((height, LANES), f32)
    for orient in range(orients):
        direction = dir_ref[orient]
        here = sub == orient
        azimuth = jnp.where(here, (direction % AZIMUTHS).astype(f32), azimuth)
        dip = jnp.where(here, (direction // AZIMUTHS + 1).astype(f32), dip)
    azimuth = azimuth * (math.pi / AZIMUTHS)
    dip_angle = dip * (math.pi / (2 * DIPS + 2))
    inline_wave = wavenumber * (jnp.sin(dip_angle) * jnp.cos(azimuth))
    xline_wave = wavenumber * (jnp.sin(dip_angle) * jnp.sin(azimuth))
    for index, part in enumerate(
        taps(inline_wave, jnp.where(lane % per == 0, lane // per, -1))
    ):
        itap_ref[index] = part
    lane = lax.broadcasted_iota(jnp.int32, (height, lanes), 1)
    place = jnp.where(lane >= group * width, lane - lanes, lane)
    for index, part in enumerate(taps(xline_wave, place - col * cols + HALF)):
        xtap_ref[index] = part


def space_tables(orient, sizes, xtap_ref, itap_ref, x_ref, i_ref):
    rows, cols, width, group = sizes
    lanes = 2 * LANES
    per = 8 // group
    sub, lane = iotas((8, lanes))
    row, step = sub // per, sub % per
    mine = jnp.logical_and(lane >= row * width, lane < (row + 1) * width)
    for part in range(2):
        line = jnp.broadcast_to(xtap_ref[part, pl.ds(orient, 1), :], (8, lanes))
        both = line
        for dy in range(1, per):
            both = jnp.where(step == dy, roll(line, dy), both)
        base = both
        for r in range(1, group):
            base = jnp.where(row == r, roll(both, r * width), base)
        for y in range(0, cols, 2 * per):
            pair = jnp.concatenate(
                [jnp.where(mine, roll(base, y + dy), 0.0) for dy in (0, per)], axis=0
            )
            start = (part * cols + y) * group
            x_ref[orient, start : start + 16, :] = pair[:, : group * width].astype(bf16)

    half = per * 3 * rows
    blank = jnp.zeros((rows, LANES), f32)
    real, imag = [
        pltpu.roll(
            jnp.broadcast_to(itap_ref[part, pl.ds(orient, 1), :], (rows, LANES)),
            per * (rows - HALF),
            1,
            stride=per,
            stride_axis=0,
        )
        for part in range(2)
    ]
    for dy in range(per):
        wide = [jnp.concatenate([roll(part, dy), blank], axis=1) for part in (real, imag)]
        for index, value in enumerate(
            (wide[0] - roll(wide[1], half), wide[1] + roll(wide[0], half))
        ):
            start = (dy * 2 + index) * rows
            i_ref[orient, start : start + rows, :] = value[:, : 2 * half].astype(bf16)


def feature_kernel(inlines, xlines, sizes, *refs):
    rows, cols, width, pad, orients, group = sizes
    dir_in, own_ref, out_ref, dir_ref, halo, time_ref, xtap_ref, itap_ref, *refs = refs
    x_ref, i_ref, band, cross, *sems = refs
    send_sem, recv_sem, local_sem = sems
    per = 8 // group
    deep = 3 * rows
    half = per * deep
    span = group * width
    pairs = cols // per
    block = rows * width
    steps = deep // (2 * group)
    row = lax.axis_index("inline")
    col = lax.axis_index("xline")
    mine = pl.ds(pl.multiple_of(col * cols, 8), cols)

    def there(side):
        return row > 0 if side < 0 else row < inlines - 1

    barrier = pltpu.get_barrier_semaphore()
    for side in (-1, 1):
        @pl.when(there(side))
        def _(side=side):
            pl.semaphore_signal(
                barrier, inc=1, device_id={"inline": row + side}, device_id_type=MESH
            )
    for shift in range(1, xlines):
        pl.semaphore_signal(
            barrier,
            inc=1,
            device_id={"xline": lax.rem(col + shift, xlines)},
            device_id_type=MESH,
        )
    own = pltpu.make_async_copy(own_ref, halo.at[1, :, mine], local_sem.at[0])
    own.start()
    named = pltpu.make_async_copy(dir_in, dir_ref, local_sem.at[1])
    named.start()
    sides = (row > 0).astype(jnp.int32) + (row < inlines - 1).astype(jnp.int32)
    pl.semaphore_wait(barrier, sides + xlines - 1)

    def along_line(side):
        return pltpu.make_async_remote_copy(
            src_ref=own_ref,
            dst_ref=halo.at[1 - side, :, mine],
            send_sem=send_sem.at[1 - side, 0],
            recv_sem=recv_sem.at[1 - side, 0],
            device_id={"inline": row + side},
            device_id_type=MESH,
        )

    def to_partner(part, shift):
        return pltpu.make_async_remote_copy(
            src_ref=own_ref if part == 1 else halo.at[part, :, mine],
            dst_ref=halo.at[part, :, mine],
            send_sem=send_sem.at[part, shift],
            recv_sem=recv_sem.at[part, shift],
            device_id={"xline": lax.rem(col + shift, xlines)},
            device_id_type=MESH,
        )

    for side in (-1, 1):
        @pl.when(there(side))
        def _(side=side):
            along_line(side).start()
    for shift in range(1, xlines):
        to_partner(1, shift).start()

    for side in (-1, 1):
        @pl.when(jnp.logical_not(there(side)))
        def _(side=side):
            halo[1 + side] = jnp.zeros(halo.shape[1:], halo.dtype)

    @pl.loop(0, DIPS)
    def _(dip):
        time_table(dip, time_ref)

    named.wait()

    shape = (rows, cols, width, group)
    space_taps(orients, dir_ref, shape, col, xtap_ref, itap_ref)

    @pl.loop(0, orients)
    def _(orient):
        space_tables(orient, shape, xtap_ref, itap_ref, x_ref, i_ref)

    def make_band(part):
        @pl.loop(0, DIPS, step=2)
        def _(first):
            for dip in (first, first + 1):
                band[dip, part * block : (part + 1) * block, :] = jnp.dot(
                    halo[part].reshape(block, LANES), time_ref[dip], preferred_element_type=f32
                ).astype(bf16)

    def across(orient, dip, step):
        mixed = [
            jnp.dot(
                x_ref[orient],
                band[dip, (2 * step + h) * span : (2 * step + h + 1) * span, :],
                preferred_element_type=f32,
            )
            for h in range(2)
        ]
        for yp in range(pairs):
            slots = [[], [], [], []]
            for h in range(2):
                with_cos = mixed[h][yp * 8 : (yp + 1) * 8]
                with_sin = mixed[h][(pairs + yp) * 8 : (pairs + yp + 1) * 8]
                cu, cv = with_cos[:, :LANES], with_cos[:, LANES:]
                su, sv = with_sin[:, :LANES], with_sin[:, LANES:]
                for slot, value in zip(slots, (cu - sv, su + cv, cu + sv, su - cv)):
                    slot.append(value)
            for index, slot in enumerate(slots):
                q, r = index // 2, index % 2
                start = ((q * pairs + yp) * 2 + r) * half + step * 16
                cross[orient, start : start + 16, :] = jnp.concatenate(slot, axis=0).astype(bf16)

    def along(orient, q, j):
        start = (q * pairs + 2 * j) * 2 * half
        operand = jnp.concatenate(
            [
                cross[orient, start : start + 2 * half, :],
                cross[orient, start + 2 * half : start + 4 * half, :],
            ],
            axis=1,
        )
        total = jnp.dot(i_ref[orient], operand, preferred_element_type=f32)
        for dy in range(per):
            re = total[(2 * dy) * rows : (2 * dy + 1) * rows]
            im = total[(2 * dy + 1) * rows : (2 * dy + 2) * rows]
            square = re * re + im * im + eps_mag
            size = square * lax.rsqrt(square)
            for h in range(2):
                out_ref[
                    (2 * j + h) * per + dy, pl.ds(2 * orient + q, rows, stride=pad), :
                ] = size[:, h * LANES : (h + 1) * LANES]

    inner = range(steps // 3, 2 * steps // 3)
    outer = [step for step in range(steps) if step not in inner]

    def dip_of(orient):
        return dir_ref[orient] // AZIMUTHS

    def own_rows(first, last, stride):
        @pl.loop(first, last, step=stride)
        def _(start):
            for orient in [start + index for index in range(stride)]:
                for step in inner:
                    across(orient, dip_of(orient), step)

    own.wait()
    for shift in range(1, xlines):
        to_partner(1, shift).wait_recv()
    make_band(1)
    pair = 2 if orients % 2 == 0 else 1
    early = round_up(orients // 2, pair)
    own_rows(0, early, pair)
    for side in (-1, 1):
        @pl.when(there(side))
        def _(side=side):
            along_line(-side).wait_recv()
            for shift in range(1, xlines):
                to_partner(1 + side, shift).start()
    own_rows(early, orients, pair)
    for y in range(cols):
        for extra in range(pad - 2 * orients):
            out_ref[y, pl.ds(2 * orients + extra, rows, stride=pad), :] = jnp.full(
                (rows, LANES), 1.0 if extra == 0 else 0.0, f32
            )
    for shift in range(1, xlines):
        to_partner(1, shift).wait_send()
    for side in (-1, 1):
        @pl.when(there(side))
        def _(side=side):
            along_line(side).wait_send()
            for shift in range(1, xlines):
                to_partner(1 + side, shift).wait()
    make_band(0)
    make_band(2)

    for step in outer:
        across(0, dip_of(0), step)

    pieces = [(q, j) for q in range(2) for j in range(pairs // 2)]
    share = -(-len(pieces) // len(outer))

    @pl.loop(1, orients)
    def _(orient):
        dip = dip_of(orient)
        for index, step in enumerate(outer):
            across(orient, dip, step)
            for q, j in pieces[index * share : (index + 1) * share]:
                along(orient - 1, q, j)

    for q, j in pieces:
        along(orients - 1, q, j)


def make_features(traces, directions, pad):
    inlines, xlines = lax.axis_size("inline"), lax.axis_size("xline")
    rows, cols, samples = traces.shape
    orients = directions.shape[0]
    width = xlines * cols
    group = 4
    assert group * width + cols <= 2 * LANES
    per = 8 // group
    sizes = (rows, cols, width, pad, orients, group)
    return pl.pallas_call(
        functools.partial(feature_kernel, inlines, xlines, sizes),
        out_shape=jax.ShapeDtypeStruct((cols, rows * pad, samples), f32),
        in_specs=[pl.BlockSpec(memory_space=HBM)] * 2,
        out_specs=pl.BlockSpec(memory_space=VMEM),
        scratch_shapes=[
            pltpu.SMEM((orients,), jnp.int32),
            pltpu.VMEM((3, rows, width, samples), bf16),
            pltpu.VMEM((DIPS, samples, 2 * samples), bf16),
            pltpu.VMEM((2, round_up(orients, 8), 2 * LANES), f32),
            pltpu.VMEM((2, round_up(orients, 8), LANES), f32),
            pltpu.VMEM((orients, 2 * cols * group, group * width), bf16),
            pltpu.VMEM((orients, 2 * per * rows, 2 * per * 3 * rows), bf16),
            pltpu.VMEM((DIPS, 3 * rows * width, 2 * samples), bf16),
            pltpu.VMEM((orients, 4 * cols * 3 * rows, samples), bf16),
            pltpu.SemaphoreType.DMA((3, xlines)),
            pltpu.SemaphoreType.DMA((3, xlines)),
            pltpu.SemaphoreType.DMA((2,)),
        ],
        compiler_params=pltpu.CompilerParams(
            collective_id=0, has_side_effects=True, vmem_limit_bytes=40 << 20
        ),
        name="features",
    )(
        pltpu.with_memory_space_constraint(directions, HBM),
        pltpu.with_memory_space_constraint(traces, HBM),
    )


def split3(value):
    high = value.astype(bf16)
    rest = value - high.astype(f32)
    mid = rest.astype(bf16)
    low = (rest - mid.astype(f32)).astype(bf16)
    return high, mid, low


def column(row):
    return jnp.transpose(jnp.broadcast_to(row, (row.shape[1], row.shape[1])))


def padded(value, fill):
    rows, lanes = value.shape
    wide = jnp.concatenate([value, jnp.full((rows, LANES - lanes), fill, f32)], axis=1)
    full = jnp.concatenate([wide, jnp.full((LANES - rows, LANES), fill, f32)], axis=0)
    return jnp.transpose(full)


def first_params(mean_ref, var_ref, weight_ref):
    comps = mean_ref.shape[1]
    means = padded(mean_ref[...], 0.0)[:comps]
    shift_row = jnp.mean(means, axis=0, keepdims=True)
    weights = jnp.broadcast_to(padded(weight_ref[...], 1.0)[:comps, :1], (comps, LANES))
    return (means - shift_row, padded(var_ref[...], 1.0)[:comps], weights), shift_row


def packing(comps, count):
    wide = 2 * count + 1
    groups = LANES // wide
    return wide, -(-comps // groups)


def packed(summed, count, pad):
    comps = summed.shape[0]
    wide, height = packing(comps, count)
    lane = lax.broadcasted_iota(jnp.int32, summed.shape, 1)
    close = jnp.where(lane <= count, summed, pltpu.roll(summed, LANES - (pad - count - 1), 1))
    close = jnp.where(lane < wide, close, 0.0)
    out = close[:height]
    for first in range(height, comps, height):
        part = close[first : min(first + height, comps)]
        if part.shape[0] < height:
            blank = jnp.zeros((height - part.shape[0], LANES), f32)
            part = jnp.concatenate([part, blank], axis=0)
        out = out + pltpu.roll(part, (first // height) * wide, 1)
    return out


def unpacked(folded, comps, count, pad):
    wide, height = packing(comps, count)
    parts = []
    for first in range(0, comps, height):
        shift = (first // height) * wide
        part = pltpu.roll(folded, LANES - shift, 1) if shift else folded
        parts.append(part[: min(height, comps - first)])
    close = jnp.concatenate(parts, axis=0)
    lane = lax.broadcasted_iota(jnp.int32, close.shape, 1)
    return jnp.where(lane <= count, close, pltpu.roll(close, pad - count - 1, 1))


def next_params(folded, params, sizes):
    pad, count, cells = sizes
    means, spreads, _ = params
    comps = means.shape[0]
    total = unpacked(folded, comps, count, pad)
    used = lax.broadcasted_iota(jnp.int32, (comps, LANES), 1) < count
    mass = total[:, count : count + 1]
    first = jnp.where(used, total, 0.0)
    second = jnp.where(used, pltpu.roll(total, LANES - pad, 1), 0.0)
    below = mass + 1.0
    new_means = (first + means) / below
    centred = second - 2.0 * new_means * first + new_means * new_means * mass
    new_spreads = jnp.where(used, (centred + spreads) / below, 1.0)
    return new_means, new_spreads, jnp.broadcast_to(below / (cells + comps), (comps, LANES))


def peers(inlines, xlines):
    row = lax.axis_index("inline")
    col = lax.axis_index("xline")

    def turned(index, shift, size):
        moved = index + shift
        return jnp.where(moved >= size, moved - size, moved) if shift else index

    return [
        {"inline": turned(row, down, inlines), "xline": turned(col, side, xlines)}
        for down in range(inlines)
        for side in range(xlines)
        if down or side
    ]


def gather_sum(others, me, payload, slots, send_sem, recv_sem):
    def copy(index):
        return pltpu.make_async_remote_copy(
            src_ref=payload,
            dst_ref=slots.at[me],
            send_sem=send_sem.at[index],
            recv_sem=recv_sem.at[index],
            device_id=others[index],
            device_id_type=MESH,
        )

    for index in range(len(others)):
        copy(index).start()
    slots[me] = payload[...]
    for index in range(len(others)):
        copy(index).wait()
    total = slots[0]
    for member in range(1, len(others) + 1):
        total = total + slots[member]
    return total


def em_kernel(sizes, *refs):
    cols, pad, count, chunk, together, cells, inlines, xlines = sizes
    feat_ref, mean_ref, var_ref, weight_ref, sum_ref, last_ref, post_ref, *refs = refs
    split_ref, table, total, shift_ref, wide, payload, slots, send_sem, recv_sem = refs
    comps = mean_ref.shape[1]
    rows = post_ref.shape[0]
    me = lax.axis_index("inline") * xlines + lax.axis_index("xline")
    others = peers(inlines, xlines)
    barrier = pltpu.get_barrier_semaphore()
    for other in others:
        pl.semaphore_signal(barrier, inc=1, device_id=other, device_id_type=MESH)

    def prepare(params):
        lane = lax.broadcasted_iota(jnp.int32, (comps, 2 * LANES), 1)
        means = jnp.concatenate([params[0], jnp.zeros((comps, LANES), f32)], axis=1)
        spreads = jnp.concatenate([params[1], jnp.ones((comps, LANES), f32)], axis=1)
        used = lane < count
        inverse = jnp.where(used, 1.0 / spreads, 0.0)
        scaled = means * inverse
        terms = jnp.where(used, jnp.log(2.0 * math.pi * spreads) + means * scaled, 0.0)
        constant = jnp.log(params[2][:, :1]) - 0.5 * jnp.sum(terms, axis=1, keepdims=True)
        row = jnp.where(used, scaled, 0.0) + jnp.where(lane == count, constant, 0.0)
        row = row + pltpu.roll(-0.5 * inverse, pad, 1)
        parts = split3(row * LOG2E)
        for index, part in enumerate(parts):
            part = part.astype(f32)
            tiled = part + pltpu.roll(part, 2 * pad, 1) + pltpu.roll(part, 4 * pad, 1)
            table[index * comps : (index + 1) * comps, :] = tiled.astype(bf16)
        total[...] = jnp.zeros_like(total)

    def sweep(step, last):
        weights = table[:, : 6 * pad]

        def scores(j, first):
            span = slice(first * LANES, (first + chunk) * LANES)
            line = step * together + j
            if last:
                operand = split_ref[line, :, span]
            else:
                base = pl.multiple_of(line * pad, 8)
                values = jnp.concatenate(
                    [
                        feat_ref[first + y, pl.ds(base, pad), :] - shift_ref[...]
                        for y in range(chunk)
                    ],
                    axis=1,
                )
                both = jnp.concatenate([values, values * values], axis=0)
                operand = jnp.concatenate(split3(both), axis=0)
                split_ref[line, :, span] = operand
            wide_score = jnp.dot(weights, operand, preferred_element_type=f32)
            score = wide_score[:comps] + (
                wide_score[comps : 2 * comps] + wide_score[2 * comps : 3 * comps]
            )
            return operand, score

        pieces = [(j, first) for j in range(together) for first in range(0, cols, chunk)]
        ahead = scores(*pieces[0])
        moment = total[...]
        for index, (j, first) in enumerate(pieces):
            operand, score = ahead
            if index + 1 < len(pieces):
                ahead = scores(*pieces[index + 1])
            exponent = jnp.exp2(score - jnp.max(score, axis=0, keepdims=True))
            share = exponent * (1.0 / jnp.sum(exponent, axis=0, keepdims=True))
            high = share.astype(bf16)
            low = (share - high.astype(f32)).astype(bf16)
            moment = moment + lax.dot_general(
                jnp.concatenate([high, low], axis=0),
                operand[: 4 * pad],
                (((1,), (1,)), ((), ())),
                preferred_element_type=f32,
            )
            if last:
                for y in range(chunk):
                    wide[pl.ds((j * comps) * cols + first + y, comps, stride=cols), :] = share[
                        :, y * LANES : (y + 1) * LANES
                    ]
        total[...] = moment
        if last:
            for j in range(together):
                for k in range(comps):
                    start = (j * comps + k) * cols
                    post_ref[step * together + j, k] = wide[start : start + cols, :].astype(bf16)

    def fold():
        both = total[:comps] + total[comps:]
        both = jnp.concatenate([both, jnp.zeros((comps, LANES - 4 * pad), f32)], axis=1)
        summed = both + pltpu.roll(both, LANES - 2 * pad, 1)
        return packed(summed, count, pad)

    params, shift_row = first_params(mean_ref, var_ref, weight_ref)
    shift_ref[...] = column(shift_row)[:pad]
    prepare(params)
    pl.loop(0, rows // together)(lambda step: sweep(step, False))
    payload[0] = fold()
    pl.semaphore_wait(barrier, len(others))
    sum_ref[...] = gather_sum(
        others, me, payload.at[0], slots.at[0], send_sem.at[0], recv_sem.at[0]
    )
    prepare(next_params(sum_ref[...], params, (pad, count, cells)))
    pl.loop(0, rows // together)(lambda step: sweep(step, True))
    payload[1] = fold()
    last_ref[...] = gather_sum(
        others, me, payload.at[1], slots.at[1], send_sem.at[1], recv_sem.at[1]
    )


def mixture(features, init, count, rows, cells):
    inlines, xlines = lax.axis_size("inline"), lax.axis_size("xline")
    members = inlines * xlines
    comps = init[0].shape[1]
    cols, flat, samples = features.shape
    pad = flat // rows
    assert 4 * pad <= LANES and comps % 16 == 0
    chunk = 4
    together = 4
    assert rows % together == 0 and cols % chunk == 0
    folded = (packing(comps, count)[1], LANES)
    sizes = (cols, pad, count, chunk, together, cells, inlines, xlines)
    return pl.pallas_call(
        functools.partial(em_kernel, sizes),
        out_shape=[
            jax.ShapeDtypeStruct(folded, f32),
            jax.ShapeDtypeStruct(folded, f32),
            jax.ShapeDtypeStruct((rows, comps, cols, samples), bf16),
        ],
        in_specs=[pl.BlockSpec(memory_space=VMEM)] * 4,
        out_specs=[pl.BlockSpec(memory_space=VMEM)] * 3,
        scratch_shapes=[
            pltpu.VMEM((rows, 6 * pad, cols * samples), bf16),
            pltpu.VMEM((3 * comps, 2 * LANES), bf16),
            pltpu.VMEM((2 * comps, 4 * pad), f32),
            pltpu.VMEM((pad, LANES), f32),
            pltpu.VMEM((together * comps * cols, samples), f32),
            pltpu.VMEM((2,) + folded, f32),
            pltpu.VMEM((2, members) + folded, f32),
            pltpu.SemaphoreType.DMA((2, members - 1)),
            pltpu.SemaphoreType.DMA((2, members - 1)),
        ],
        compiler_params=pltpu.CompilerParams(
            collective_id=1, has_side_effects=True, vmem_limit_bytes=36 << 20
        ),
        name="mixture",
    )(features, *init)


def final_kernel(sizes, *refs):
    *sums, post_in, mean_ref, var_ref, weight_ref = refs[:-5]
    mean_out, var_out, weight_out, post_out, sems = refs[-5:]
    count = sizes[1]
    parts = sems.shape[0]
    depth = post_in.shape[0] // parts

    def copy(part):
        span = pl.ds(part * depth, depth)
        return pltpu.make_async_copy(post_in.at[span], post_out.at[span], sems.at[part])

    for part in range(parts):
        copy(part).start()
    params, shift_row = first_params(mean_ref, var_ref, weight_ref)
    for summed in sums:
        params = next_params(summed[...], params, sizes)
    means, spreads, weights = params
    comps = means.shape[0]
    blank = jnp.zeros((LANES - comps, LANES), f32)
    turned = [
        jnp.transpose(jnp.concatenate([value, blank], axis=0))[:, :comps]
        for value in (means + shift_row, spreads, weights)
    ]
    mean_out[...] = turned[0][:count]
    var_out[...] = turned[1][:count]
    weight_out[...] = turned[2][:1]
    for part in range(parts):
        copy(part).wait()


def finish(sums, posterior, init, sizes):
    count, comps = init[0].shape
    inputs = sums + [posterior] + list(init)
    return pl.pallas_call(
        functools.partial(final_kernel, sizes),
        out_shape=[
            jax.ShapeDtypeStruct((count, comps), f32),
            jax.ShapeDtypeStruct((count, comps), f32),
            jax.ShapeDtypeStruct((1, comps), f32),
            jax.ShapeDtypeStruct(posterior.shape, posterior.dtype),
        ],
        in_specs=[pl.BlockSpec(memory_space=VMEM)] * len(inputs),
        out_specs=[pl.BlockSpec(memory_space=VMEM)] * 3 + [pl.BlockSpec(memory_space=HBM)],
        scratch_shapes=[pltpu.SemaphoreType.DMA((math.gcd(8, posterior.shape[0]),))],
        compiler_params=pltpu.CompilerParams(vmem_limit_bytes=4 << 20),
        name="finish",
    )(*inputs)


def per_device(traces, directions, init_means, init_variances, init_weights):
    rows, cols, samples = traces.shape
    assert samples == LANES and rows >= HALF and rows % 8 == 0 and cols % 4 == 0
    count = 2 * directions.shape[0]
    pad = round_up(count + 1, 8)
    comps = init_weights.shape[0]
    cells = lax.axis_size("inline") * rows * lax.axis_size("xline") * cols * samples
    init = (init_means.T, init_variances.T, init_weights.reshape(1, comps))
    features = make_features(traces, directions, pad)
    *sums, posterior = mixture(features, init, count, rows, cells)
    means, spreads, weights, posterior = finish(sums, posterior, init, (pad, count, cells))
    return posterior, means.T, spreads.T, weights.reshape(comps)


def solution(mesh):
    in_specs = (P(("slab", "inline"), "xline", None), P(), P(), P(), P())
    out_specs = (
        P(("slab", "inline"), None, "xline", None),
        P("slab", None),
        P("slab", None),
        P("slab"),
    )
    return jax.shard_map(
        per_device, mesh=mesh, in_specs=in_specs, out_specs=out_specs, check_vma=False
    )
```

```python
import functools
import math

import jax
import jax.numpy as jnp
from jax import lax
from jax.experimental import pallas as pl
from jax.experimental.pallas import tpu as pltpu
from jax.sharding import PartitionSpec as P

TAPS = 31
HALF = 15
AZIMUTHS = 8
DIPS = 4
LANES = 128

eps_mag = 0.01
wavenumber = math.pi / 4.0
width_scale = HALF / 3.0
norm = math.sqrt(
    sum(math.exp(-n * n / (width_scale * width_scale)) for n in range(-HALF, HALF + 1))
)
MESH = pl.DeviceIdType.MESH
LOG2E = math.log2(math.e)
f32 = jnp.float32
bf16 = jnp.bfloat16
VMEM = pltpu.MemorySpace.VMEM
SMEM = pltpu.MemorySpace.SMEM
HBM = pltpu.MemorySpace.HBM


def round_up(value, step):
    return -(-value // step) * step


def iotas(shape):
    return (
        lax.broadcasted_iota(jnp.int32, shape, 0),
        lax.broadcasted_iota(jnp.int32, shape, 1),
    )


def roll(value, amount):
    return value if amount == 0 else pltpu.roll(value, amount, 1)


def taps(wave, difference):
    offset = (difference - HALF).astype(f32)
    phase = offset * jnp.concatenate([wave] * (difference.shape[1] // LANES), axis=1)
    envelope = jnp.exp(-offset * offset / (2.0 * width_scale * width_scale)) / norm
    hit = jnp.logical_and(difference >= 0, difference < TAPS)
    real = jnp.where(hit, envelope * jnp.cos(phase), 0.0)
    imag = jnp.where(hit, envelope * jnp.sin(phase), 0.0)
    return real, imag


def time_table(dip, time_ref):
    dip_angle = jnp.full((8, LANES), (dip + 1).astype(f32)) * (math.pi / (2 * DIPS + 2))
    wave = wavenumber * jnp.cos(dip_angle)
    sub, lane = iotas((8, LANES))
    bases = taps(wave, jnp.bitwise_and(sub - lane + HALF, LANES - 1))
    for s in range(0, LANES, 16):
        pieces = []
        for start in (s, s + 8):
            near = jnp.abs(sub + start - lane) <= HALF
            pieces.append(
                jnp.concatenate([jnp.where(near, roll(base, start), 0.0) for base in bases], axis=1)
            )
        time_ref[dip, s : s + 16, :] = jnp.concatenate(pieces, axis=0).astype(bf16)


def space_taps(orients, dir_ref, sizes, col, xtap_ref, itap_ref):
    rows, cols, width, group = sizes
    lanes = 2 * LANES
    per = 8 // group
    height = xtap_ref.shape[1]
    sub, lane = iotas((height, LANES))
    azimuth, dip = jnp.zeros((height, LANES), f32), jnp.zeros((height, LANES), f32)
    for orient in range(orients):
        direction = dir_ref[orient]
        here = sub == orient
        azimuth = jnp.where(here, (direction % AZIMUTHS).astype(f32), azimuth)
        dip = jnp.where(here, (direction // AZIMUTHS + 1).astype(f32), dip)
    azimuth = azimuth * (math.pi / AZIMUTHS)
    dip_angle = dip * (math.pi / (2 * DIPS + 2))
    inline_wave = wavenumber * (jnp.sin(dip_angle) * jnp.cos(azimuth))
    xline_wave = wavenumber * (jnp.sin(dip_angle) * jnp.sin(azimuth))
    for index, part in enumerate(
        taps(inline_wave, jnp.where(lane % per == 0, lane // per, -1))
    ):
        itap_ref[index] = part
    lane = lax.broadcasted_iota(jnp.int32, (height, lanes), 1)
    place = jnp.where(lane >= group * width, lane - lanes, lane)
    for index, part in enumerate(taps(xline_wave, place - col * cols + HALF)):
        xtap_ref[index] = part


def space_tables(orient, sizes, xtap_ref, itap_ref, x_ref, i_ref):
    rows, cols, width, group = sizes
    lanes = 2 * LANES
    per = 8 // group
    sub, lane = iotas((8, lanes))
    row, step = sub // per, sub % per
    mine = jnp.logical_and(lane >= row * width, lane < (row + 1) * width)
    for part in range(2):
        line = jnp.broadcast_to(xtap_ref[part, pl.ds(orient, 1), :], (8, lanes))
        both = line
        for dy in range(1, per):
            both = jnp.where(step == dy, roll(line, dy), both)
        base = both
        for r in range(1, group):
            base = jnp.where(row == r, roll(both, r * width), base)
        for y in range(0, cols, 2 * per):
            pair = jnp.concatenate(
                [jnp.where(mine, roll(base, y + dy), 0.0) for dy in (0, per)], axis=0
            )
            start = (part * cols + y) * group
            x_ref[orient, start : start + 16, :] = pair[:, : group * width].astype(bf16)

    half = per * 3 * rows
    blank = jnp.zeros((rows, LANES), f32)
    real, imag = [
        pltpu.roll(
            jnp.broadcast_to(itap_ref[part, pl.ds(orient, 1), :], (rows, LANES)),
            per * (rows - HALF),
            1,
            stride=per,
            stride_axis=0,
        )
        for part in range(2)
    ]
    for dy in range(per):
        wide = [jnp.concatenate([roll(part, dy), blank], axis=1) for part in (real, imag)]
        for index, value in enumerate(
            (wide[0] - roll(wide[1], half), wide[1] + roll(wide[0], half))
        ):
            start = (dy * 2 + index) * rows
            i_ref[orient, start : start + rows, :] = value[:, : 2 * half].astype(bf16)


def feature_kernel(inlines, xlines, sizes, *refs):
    rows, cols, width, pad, orients, group = sizes
    dir_in, own_ref, out_ref, dir_ref, halo, time_ref, xtap_ref, itap_ref, *refs = refs
    x_ref, i_ref, band, cross, *sems = refs
    send_sem, recv_sem, local_sem = sems
    per = 8 // group
    deep = 3 * rows
    half = per * deep
    span = group * width
    pairs = cols // per
    block = rows * width
    steps = deep // (2 * group)
    row = lax.axis_index("inline")
    col = lax.axis_index("xline")
    mine = pl.ds(pl.multiple_of(col * cols, 8), cols)

    def there(side):
        return row > 0 if side < 0 else row < inlines - 1

    barrier = pltpu.get_barrier_semaphore()
    for side in (-1, 1):
        @pl.when(there(side))
        def _(side=side):
            pl.semaphore_signal(
                barrier, inc=1, device_id={"inline": row + side}, device_id_type=MESH
            )
    for shift in range(1, xlines):
        pl.semaphore_signal(
            barrier,
            inc=1,
            device_id={"xline": lax.rem(col + shift, xlines)},
            device_id_type=MESH,
        )
    own = pltpu.make_async_copy(own_ref, halo.at[1, :, mine], local_sem.at[0])
    own.start()
    named = pltpu.make_async_copy(dir_in, dir_ref, local_sem.at[1])
    named.start()
    sides = (row > 0).astype(jnp.int32) + (row < inlines - 1).astype(jnp.int32)
    pl.semaphore_wait(barrier, sides + xlines - 1)

    def along_line(side):
        return pltpu.make_async_remote_copy(
            src_ref=own_ref,
            dst_ref=halo.at[1 - side, :, mine],
            send_sem=send_sem.at[1 - side, 0],
            recv_sem=recv_sem.at[1 - side, 0],
            device_id={"inline": row + side},
            device_id_type=MESH,
        )

    def to_partner(part, shift):
        return pltpu.make_async_remote_copy(
            src_ref=own_ref if part == 1 else halo.at[part, :, mine],
            dst_ref=halo.at[part, :, mine],
            send_sem=send_sem.at[part, shift],
            recv_sem=recv_sem.at[part, shift],
            device_id={"xline": lax.rem(col + shift, xlines)},
            device_id_type=MESH,
        )

    for side in (-1, 1):
        @pl.when(there(side))
        def _(side=side):
            along_line(side).start()
    for shift in range(1, xlines):
        to_partner(1, shift).start()

    for side in (-1, 1):
        @pl.when(jnp.logical_not(there(side)))
        def _(side=side):
            halo[1 + side] = jnp.zeros(halo.shape[1:], halo.dtype)

    @pl.loop(0, DIPS)
    def _(dip):
        time_table(dip, time_ref)

    named.wait()

    shape = (rows, cols, width, group)
    space_taps(orients, dir_ref, shape, col, xtap_ref, itap_ref)

    @pl.loop(0, orients)
    def _(orient):
        space_tables(orient, shape, xtap_ref, itap_ref, x_ref, i_ref)

    def make_band(part):
        @pl.loop(0, DIPS, step=2)
        def _(first):
            for dip in (first, first + 1):
                band[dip, part * block : (part + 1) * block, :] = jnp.dot(
                    halo[part].reshape(block, LANES), time_ref[dip], preferred_element_type=f32
                ).astype(bf16)

    def across(orient, dip, step):
        mixed = [
            jnp.dot(
                x_ref[orient],
                band[dip, (2 * step + h) * span : (2 * step + h + 1) * span, :],
                preferred_element_type=f32,
            )
            for h in range(2)
        ]
        for yp in range(pairs):
            slots = [[], [], [], []]
            for h in range(2):
                with_cos = mixed[h][yp * 8 : (yp + 1) * 8]
                with_sin = mixed[h][(pairs + yp) * 8 : (pairs + yp + 1) * 8]
                cu, cv = with_cos[:, :LANES], with_cos[:, LANES:]
                su, sv = with_sin[:, :LANES], with_sin[:, LANES:]
                for slot, value in zip(slots, (cu - sv, su + cv, cu + sv, su - cv)):
                    slot.append(value)
            for index, slot in enumerate(slots):
                q, r = index // 2, index % 2
                start = ((q * pairs + yp) * 2 + r) * half + step * 16
                cross[orient, start : start + 16, :] = jnp.concatenate(slot, axis=0).astype(bf16)

    def along(orient, q, j):
        start = (q * pairs + 2 * j) * 2 * half
        operand = jnp.concatenate(
            [
                cross[orient, start : start + 2 * half, :],
                cross[orient, start + 2 * half : start + 4 * half, :],
            ],
            axis=1,
        )
        total = jnp.dot(i_ref[orient], operand, preferred_element_type=f32)
        for dy in range(per):
            re = total[(2 * dy) * rows : (2 * dy + 1) * rows]
            im = total[(2 * dy + 1) * rows : (2 * dy + 2) * rows]
            square = re * re + im * im + eps_mag
            size = square * lax.rsqrt(square)
            for h in range(2):
                out_ref[
                    (2 * j + h) * per + dy, pl.ds(2 * orient + q, rows, stride=pad), :
                ] = size[:, h * LANES : (h + 1) * LANES]

    inner = range(steps // 3, 2 * steps // 3)
    outer = [step for step in range(steps) if step not in inner]

    def dip_of(orient):
        return dir_ref[orient] // AZIMUTHS

    def own_rows(first, last, stride):
        @pl.loop(first, last, step=stride)
        def _(start):
            for orient in [start + index for index in range(stride)]:
                for step in inner:
                    across(orient, dip_of(orient), step)

    own.wait()
    for shift in range(1, xlines):
        to_partner(1, shift).wait_recv()
    make_band(1)
    pair = 2 if orients % 2 == 0 else 1
    early = round_up(orients // 2, pair)
    own_rows(0, early, pair)
    for side in (-1, 1):
        @pl.when(there(side))
        def _(side=side):
            along_line(-side).wait_recv()
            for shift in range(1, xlines):
                to_partner(1 + side, shift).start()
    own_rows(early, orients, pair)
    for y in range(cols):
        for extra in range(pad - 2 * orients):
            out_ref[y, pl.ds(2 * orients + extra, rows, stride=pad), :] = jnp.full(
                (rows, LANES), 1.0 if extra == 0 else 0.0, f32
            )
    for shift in range(1, xlines):
        to_partner(1, shift).wait_send()
    for side in (-1, 1):
        @pl.when(there(side))
        def _(side=side):
            along_line(side).wait_send()
            for shift in range(1, xlines):
                to_partner(1 + side, shift).wait()
    make_band(0)
    make_band(2)

    for step in outer:
        across(0, dip_of(0), step)

    pieces = [(q, j) for q in range(2) for j in range(pairs // 2)]
    share = -(-len(pieces) // len(outer))

    stride = math.gcd(orients - 1, 3)

    @pl.loop(1, orients, step=stride)
    def _(first):
        for orient in [first + index for index in range(stride)]:
            dip = dip_of(orient)
            for index, step in enumerate(outer):
                across(orient, dip, step)
                for q, j in pieces[index * share : (index + 1) * share]:
                    along(orient - 1, q, j)

    for q, j in pieces:
        along(orients - 1, q, j)


def make_features(traces, directions, pad):
    inlines, xlines = lax.axis_size("inline"), lax.axis_size("xline")
    rows, cols, samples = traces.shape
    orients = directions.shape[0]
    width = xlines * cols
    group = 4
    assert group * width + cols <= 2 * LANES
    per = 8 // group
    sizes = (rows, cols, width, pad, orients, group)
    return pl.pallas_call(
        functools.partial(feature_kernel, inlines, xlines, sizes),
        out_shape=jax.ShapeDtypeStruct((cols, rows * pad, samples), f32),
        in_specs=[pl.BlockSpec(memory_space=HBM)] * 2,
        out_specs=pl.BlockSpec(memory_space=VMEM),
        scratch_shapes=[
            pltpu.SMEM((orients,), jnp.int32),
            pltpu.VMEM((3, rows, width, samples), bf16),
            pltpu.VMEM((DIPS, samples, 2 * samples), bf16),
            pltpu.VMEM((2, round_up(orients, 8), 2 * LANES), f32),
            pltpu.VMEM((2, round_up(orients, 8), LANES), f32),
            pltpu.VMEM((orients, 2 * cols * group, group * width), bf16),
            pltpu.VMEM((orients, 2 * per * rows, 2 * per * 3 * rows), bf16),
            pltpu.VMEM((DIPS, 3 * rows * width, 2 * samples), bf16),
            pltpu.VMEM((orients, 4 * cols * 3 * rows, samples), bf16),
            pltpu.SemaphoreType.DMA((3, xlines)),
            pltpu.SemaphoreType.DMA((3, xlines)),
            pltpu.SemaphoreType.DMA((2,)),
        ],
        compiler_params=pltpu.CompilerParams(
            collective_id=0, has_side_effects=True, vmem_limit_bytes=40 << 20
        ),
        name="features",
    )(
        pltpu.with_memory_space_constraint(directions, HBM),
        pltpu.with_memory_space_constraint(traces, HBM),
    )


def split3(value):
    high = value.astype(bf16)
    rest = value - high.astype(f32)
    mid = rest.astype(bf16)
    low = (rest - mid.astype(f32)).astype(bf16)
    return high, mid, low


def column(row):
    return jnp.transpose(jnp.broadcast_to(row, (row.shape[1], row.shape[1])))


def padded(value, fill):
    rows, lanes = value.shape
    wide = jnp.concatenate([value, jnp.full((rows, LANES - lanes), fill, f32)], axis=1)
    full = jnp.concatenate([wide, jnp.full((LANES - rows, LANES), fill, f32)], axis=0)
    return jnp.transpose(full)


def first_params(mean_ref, var_ref, weight_ref):
    comps = mean_ref.shape[1]
    means = padded(mean_ref[...], 0.0)[:comps]
    shift_row = jnp.mean(means, axis=0, keepdims=True)
    weights = jnp.broadcast_to(padded(weight_ref[...], 1.0)[:comps, :1], (comps, LANES))
    return (means - shift_row, padded(var_ref[...], 1.0)[:comps], weights), shift_row


def packing(comps, count):
    wide = 2 * count + 1
    groups = LANES // wide
    return wide, -(-comps // groups)


def packed(summed, count, pad):
    comps = summed.shape[0]
    wide, height = packing(comps, count)
    lane = lax.broadcasted_iota(jnp.int32, summed.shape, 1)
    close = jnp.where(lane <= count, summed, pltpu.roll(summed, LANES - (pad - count - 1), 1))
    close = jnp.where(lane < wide, close, 0.0)
    out = close[:height]
    for first in range(height, comps, height):
        part = close[first : min(first + height, comps)]
        if part.shape[0] < height:
            blank = jnp.zeros((height - part.shape[0], LANES), f32)
            part = jnp.concatenate([part, blank], axis=0)
        out = out + pltpu.roll(part, (first // height) * wide, 1)
    return out


def unpacked(folded, comps, count, pad):
    wide, height = packing(comps, count)
    parts = []
    for first in range(0, comps, height):
        shift = (first // height) * wide
        part = pltpu.roll(folded, LANES - shift, 1) if shift else folded
        parts.append(part[: min(height, comps - first)])
    close = jnp.concatenate(parts, axis=0)
    lane = lax.broadcasted_iota(jnp.int32, close.shape, 1)
    return jnp.where(lane <= count, close, pltpu.roll(close, pad - count - 1, 1))


def next_params(folded, params, sizes):
    pad, count, cells = sizes
    means, spreads, _ = params
    comps = means.shape[0]
    total = unpacked(folded, comps, count, pad)
    used = lax.broadcasted_iota(jnp.int32, (comps, LANES), 1) < count
    mass = total[:, count : count + 1]
    first = jnp.where(used, total, 0.0)
    second = jnp.where(used, pltpu.roll(total, LANES - pad, 1), 0.0)
    below = mass + 1.0
    new_means = (first + means) / below
    centred = second - 2.0 * new_means * first + new_means * new_means * mass
    new_spreads = jnp.where(used, (centred + spreads) / below, 1.0)
    return new_means, new_spreads, jnp.broadcast_to(below / (cells + comps), (comps, LANES))


def peers(inlines, xlines):
    row = lax.axis_index("inline")
    col = lax.axis_index("xline")

    def turned(index, shift, size):
        moved = index + shift
        return jnp.where(moved >= size, moved - size, moved) if shift else index

    return [
        {"inline": turned(row, down, inlines), "xline": turned(col, side, xlines)}
        for down in range(inlines)
        for side in range(xlines)
        if down or side
    ]


def gather_sum(others, me, payload, slots, send_sem, recv_sem):
    def copy(index):
        return pltpu.make_async_remote_copy(
            src_ref=payload,
            dst_ref=slots.at[me],
            send_sem=send_sem.at[index],
            recv_sem=recv_sem.at[index],
            device_id=others[index],
            device_id_type=MESH,
        )

    for index in range(len(others)):
        copy(index).start()
    slots[me] = payload[...]
    for index in range(len(others)):
        copy(index).wait()
    total = slots[0]
    for member in range(1, len(others) + 1):
        total = total + slots[member]
    return total


def em_kernel(sizes, *refs):
    cols, pad, count, chunk, together, cells, inlines, xlines = sizes
    feat_ref, mean_ref, var_ref, weight_ref, sum_ref, last_ref, post_ref, *refs = refs
    split_ref, table, total, shift_ref, wide, payload, slots, send_sem, recv_sem = refs
    comps = mean_ref.shape[1]
    rows = post_ref.shape[0]
    me = lax.axis_index("inline") * xlines + lax.axis_index("xline")
    others = peers(inlines, xlines)
    barrier = pltpu.get_barrier_semaphore()
    for other in others:
        pl.semaphore_signal(barrier, inc=1, device_id=other, device_id_type=MESH)

    def prepare(params):
        lane = lax.broadcasted_iota(jnp.int32, (comps, 2 * LANES), 1)
        means = jnp.concatenate([params[0], jnp.zeros((comps, LANES), f32)], axis=1)
        spreads = jnp.concatenate([params[1], jnp.ones((comps, LANES), f32)], axis=1)
        used = lane < count
        inverse = jnp.where(used, 1.0 / spreads, 0.0)
        scaled = means * inverse
        terms = jnp.where(used, jnp.log(2.0 * math.pi * spreads) + means * scaled, 0.0)
        constant = jnp.log(params[2][:, :1]) - 0.5 * jnp.sum(terms, axis=1, keepdims=True)
        row = jnp.where(used, scaled, 0.0) + jnp.where(lane == count, constant, 0.0)
        row = row + pltpu.roll(-0.5 * inverse, pad, 1)
        parts = split3(row * LOG2E)
        for index, part in enumerate(parts):
            part = part.astype(f32)
            tiled = part + pltpu.roll(part, 2 * pad, 1) + pltpu.roll(part, 4 * pad, 1)
            table[index * comps : (index + 1) * comps, :] = tiled.astype(bf16)
        total[...] = jnp.zeros_like(total)

    def sweep(step, last):
        weights = table[:, : 6 * pad]

        def scores(j, first):
            span = slice(first * LANES, (first + chunk) * LANES)
            line = step * together + j
            if last:
                operand = split_ref[line, :, span]
            else:
                base = pl.multiple_of(line * pad, 8)
                values = jnp.concatenate(
                    [
                        feat_ref[first + y, pl.ds(base, pad), :] - shift_ref[...]
                        for y in range(chunk)
                    ],
                    axis=1,
                )
                both = jnp.concatenate([values, values * values], axis=0)
                operand = jnp.concatenate(split3(both), axis=0)
                split_ref[line, :, span] = operand
            wide_score = jnp.dot(weights, operand, preferred_element_type=f32)
            score = wide_score[:comps] + (
                wide_score[comps : 2 * comps] + wide_score[2 * comps : 3 * comps]
            )
            return operand, score

        pieces = [(j, first) for j in range(together) for first in range(0, cols, chunk)]
        ahead = scores(*pieces[0])
        moment = total[...]
        for index, (j, first) in enumerate(pieces):
            operand, score = ahead
            if index + 1 < len(pieces):
                ahead = scores(*pieces[index + 1])
            exponent = jnp.exp2(score - jnp.max(score, axis=0, keepdims=True))
            share = exponent * (1.0 / jnp.sum(exponent, axis=0, keepdims=True))
            high = share.astype(bf16)
            low = (share - high.astype(f32)).astype(bf16)
            moment = moment + lax.dot_general(
                jnp.concatenate([high, low], axis=0),
                operand[: 4 * pad],
                (((1,), (1,)), ((), ())),
                preferred_element_type=f32,
            )
            if last:
                for y in range(chunk):
                    wide[pl.ds((j * comps) * cols + first + y, comps, stride=cols), :] = share[
                        :, y * LANES : (y + 1) * LANES
                    ]
        total[...] = moment
        if last:
            for j in range(together):
                for k in range(comps):
                    start = (j * comps + k) * cols
                    post_ref[step * together + j, k] = wide[start : start + cols, :].astype(bf16)

    def fold():
        both = total[:comps] + total[comps:]
        both = jnp.concatenate([both, jnp.zeros((comps, LANES - 4 * pad), f32)], axis=1)
        summed = both + pltpu.roll(both, LANES - 2 * pad, 1)
        return packed(summed, count, pad)

    params, shift_row = first_params(mean_ref, var_ref, weight_ref)
    shift_ref[...] = column(shift_row)[:pad]
    prepare(params)
    pl.loop(0, rows // together)(lambda step: sweep(step, False))
    payload[0] = fold()
    pl.semaphore_wait(barrier, len(others))
    sum_ref[...] = gather_sum(
        others, me, payload.at[0], slots.at[0], send_sem.at[0], recv_sem.at[0]
    )
    prepare(next_params(sum_ref[...], params, (pad, count, cells)))
    pl.loop(0, rows // together)(lambda step: sweep(step, True))
    payload[1] = fold()
    last_ref[...] = gather_sum(
        others, me, payload.at[1], slots.at[1], send_sem.at[1], recv_sem.at[1]
    )


def mixture(features, init, count, rows, cells):
    inlines, xlines = lax.axis_size("inline"), lax.axis_size("xline")
    members = inlines * xlines
    comps = init[0].shape[1]
    cols, flat, samples = features.shape
    pad = flat // rows
    assert 4 * pad <= LANES and comps % 16 == 0
    chunk = 4
    together = math.gcd(rows, 8)
    assert rows % together == 0 and cols % chunk == 0
    folded = (packing(comps, count)[1], LANES)
    sizes = (cols, pad, count, chunk, together, cells, inlines, xlines)
    return pl.pallas_call(
        functools.partial(em_kernel, sizes),
        out_shape=[
            jax.ShapeDtypeStruct(folded, f32),
            jax.ShapeDtypeStruct(folded, f32),
            jax.ShapeDtypeStruct((rows, comps, cols, samples), bf16),
        ],
        in_specs=[pl.BlockSpec(memory_space=VMEM)] * 4,
        out_specs=[pl.BlockSpec(memory_space=VMEM)] * 3,
        scratch_shapes=[
            pltpu.VMEM((rows, 6 * pad, cols * samples), bf16),
            pltpu.VMEM((3 * comps, 2 * LANES), bf16),
            pltpu.VMEM((2 * comps, 4 * pad), f32),
            pltpu.VMEM((pad, LANES), f32),
            pltpu.VMEM((together * comps * cols, samples), f32),
            pltpu.VMEM((2,) + folded, f32),
            pltpu.VMEM((2, members) + folded, f32),
            pltpu.SemaphoreType.DMA((2, members - 1)),
            pltpu.SemaphoreType.DMA((2, members - 1)),
        ],
        compiler_params=pltpu.CompilerParams(
            collective_id=1, has_side_effects=True, vmem_limit_bytes=36 << 20
        ),
        name="mixture",
    )(features, *init)


def final_kernel(sizes, *refs):
    *sums, post_in, mean_ref, var_ref, weight_ref = refs[:-5]
    mean_out, var_out, weight_out, post_out, sems = refs[-5:]
    count = sizes[1]
    parts = sems.shape[0]
    depth = post_in.shape[0] // parts

    def copy(part):
        span = pl.ds(part * depth, depth)
        return pltpu.make_async_copy(post_in.at[span], post_out.at[span], sems.at[part])

    for part in range(parts):
        copy(part).start()
    params, shift_row = first_params(mean_ref, var_ref, weight_ref)
    for summed in sums:
        params = next_params(summed[...], params, sizes)
    means, spreads, weights = params
    comps = means.shape[0]
    blank = jnp.zeros((LANES - comps, LANES), f32)
    turned = [
        jnp.transpose(jnp.concatenate([value, blank], axis=0))[:, :comps]
        for value in (means + shift_row, spreads, weights)
    ]
    mean_out[...] = turned[0][:count]
    var_out[...] = turned[1][:count]
    weight_out[...] = turned[2][:1]
    for part in range(parts):
        copy(part).wait()


def finish(sums, posterior, init, sizes):
    count, comps = init[0].shape
    inputs = sums + [posterior] + list(init)
    return pl.pallas_call(
        functools.partial(final_kernel, sizes),
        out_shape=[
            jax.ShapeDtypeStruct((count, comps), f32),
            jax.ShapeDtypeStruct((count, comps), f32),
            jax.ShapeDtypeStruct((1, comps), f32),
            jax.ShapeDtypeStruct(posterior.shape, posterior.dtype),
        ],
        in_specs=[pl.BlockSpec(memory_space=VMEM)] * len(inputs),
        out_specs=[pl.BlockSpec(memory_space=VMEM)] * 3 + [pl.BlockSpec(memory_space=HBM)],
        scratch_shapes=[pltpu.SemaphoreType.DMA((math.gcd(8, posterior.shape[0]),))],
        compiler_params=pltpu.CompilerParams(vmem_limit_bytes=4 << 20),
        name="finish",
    )(*inputs)


def per_device(traces, directions, init_means, init_variances, init_weights):
    rows, cols, samples = traces.shape
    assert samples == LANES and rows >= HALF and rows % 8 == 0 and cols % 4 == 0
    count = 2 * directions.shape[0]
    pad = round_up(count + 1, 8)
    comps = init_weights.shape[0]
    cells = lax.axis_size("inline") * rows * lax.axis_size("xline") * cols * samples
    init = (init_means.T, init_variances.T, init_weights.reshape(1, comps))
    features = make_features(traces, directions, pad)
    *sums, posterior = mixture(features, init, count, rows, cells)
    means, spreads, weights, posterior = finish(sums, posterior, init, (pad, count, cells))
    return posterior, means.T, spreads.T, weights.reshape(comps)


def solution(mesh):
    in_specs = (P(("slab", "inline"), "xline", None), P(), P(), P(), P())
    out_specs = (
        P(("slab", "inline"), None, "xline", None),
        P("slab", None),
        P("slab", None),
        P("slab"),
    )
    return jax.shard_map(
        per_device, mesh=mesh, in_specs=in_specs, out_specs=out_specs, check_vma=False
    )
```

```python
import functools
import math

import jax
import jax.numpy as jnp
from jax import lax
from jax.experimental import pallas as pl
from jax.experimental.pallas import tpu as pltpu
from jax.sharding import PartitionSpec as P

TAPS = 31
HALF = 15
AZIMUTHS = 8
DIPS = 4
LANES = 128

eps_mag = 0.01
wavenumber = math.pi / 4.0
width_scale = HALF / 3.0
norm = math.sqrt(
    sum(math.exp(-n * n / (width_scale * width_scale)) for n in range(-HALF, HALF + 1))
)
MESH = pl.DeviceIdType.MESH
LOG2E = math.log2(math.e)
f32 = jnp.float32
bf16 = jnp.bfloat16
VMEM = pltpu.MemorySpace.VMEM
SMEM = pltpu.MemorySpace.SMEM
HBM = pltpu.MemorySpace.HBM


def round_up(value, step):
    return -(-value // step) * step


def iotas(shape):
    return (
        lax.broadcasted_iota(jnp.int32, shape, 0),
        lax.broadcasted_iota(jnp.int32, shape, 1),
    )


def roll(value, amount):
    return value if amount == 0 else pltpu.roll(value, amount, 1)


def taps(wave, difference):
    offset = (difference - HALF).astype(f32)
    phase = offset * jnp.concatenate([wave] * (difference.shape[1] // LANES), axis=1)
    envelope = jnp.exp(-offset * offset / (2.0 * width_scale * width_scale)) / norm
    hit = jnp.logical_and(difference >= 0, difference < TAPS)
    real = jnp.where(hit, envelope * jnp.cos(phase), 0.0)
    imag = jnp.where(hit, envelope * jnp.sin(phase), 0.0)
    return real, imag


def time_table(dip, time_ref):
    dip_angle = jnp.full((8, LANES), (dip + 1).astype(f32)) * (math.pi / (2 * DIPS + 2))
    wave = wavenumber * jnp.cos(dip_angle)
    sub, lane = iotas((8, LANES))
    bases = taps(wave, jnp.bitwise_and(sub - lane + HALF, LANES - 1))
    for s in range(0, LANES, 16):
        pieces = []
        for start in (s, s + 8):
            near = jnp.abs(sub + start - lane) <= HALF
            pieces.append(
                jnp.concatenate([jnp.where(near, roll(base, start), 0.0) for base in bases], axis=1)
            )
        time_ref[dip, s : s + 16, :] = jnp.concatenate(pieces, axis=0).astype(bf16)


def space_taps(orients, dir_ref, sizes, col, xtap_ref, itap_ref):
    rows, cols, width, group = sizes
    lanes = 2 * LANES
    per = 8 // group
    height = xtap_ref.shape[1]
    sub, lane = iotas((height, LANES))
    azimuth, dip = jnp.zeros((height, LANES), f32), jnp.zeros((height, LANES), f32)
    for orient in range(orients):
        direction = dir_ref[orient]
        here = sub == orient
        azimuth = jnp.where(here, (direction % AZIMUTHS).astype(f32), azimuth)
        dip = jnp.where(here, (direction // AZIMUTHS + 1).astype(f32), dip)
    azimuth = azimuth * (math.pi / AZIMUTHS)
    dip_angle = dip * (math.pi / (2 * DIPS + 2))
    inline_wave = wavenumber * (jnp.sin(dip_angle) * jnp.cos(azimuth))
    xline_wave = wavenumber * (jnp.sin(dip_angle) * jnp.sin(azimuth))
    for index, part in enumerate(
        taps(inline_wave, jnp.where(lane % per == 0, lane // per, -1))
    ):
        itap_ref[index] = part
    lane = lax.broadcasted_iota(jnp.int32, (height, lanes), 1)
    place = jnp.where(lane >= group * width, lane - lanes, lane)
    for index, part in enumerate(taps(xline_wave, place - col * cols + HALF)):
        xtap_ref[index] = part


def space_tables(orient, sizes, xtap_ref, itap_ref, x_ref, i_ref):
    rows, cols, width, group = sizes
    lanes = 2 * LANES
    per = 8 // group
    sub, lane = iotas((8, lanes))
    row, step = sub // per, sub % per
    mine = jnp.logical_and(lane >= row * width, lane < (row + 1) * width)
    for part in range(2):
        line = jnp.broadcast_to(xtap_ref[part, pl.ds(orient, 1), :], (8, lanes))
        both = line
        for dy in range(1, per):
            both = jnp.where(step == dy, roll(line, dy), both)
        base = both
        for r in range(1, group):
            base = jnp.where(row == r, roll(both, r * width), base)
        for y in range(0, cols, 2 * per):
            pair = jnp.concatenate(
                [jnp.where(mine, roll(base, y + dy), 0.0) for dy in (0, per)], axis=0
            )
            start = (part * cols + y) * group
            x_ref[orient, start : start + 16, :] = pair[:, : group * width].astype(bf16)

    half = per * 3 * rows
    blank = jnp.zeros((rows, LANES), f32)
    real, imag = [
        pltpu.roll(
            jnp.broadcast_to(itap_ref[part, pl.ds(orient, 1), :], (rows, LANES)),
            per * (rows - HALF),
            1,
            stride=per,
            stride_axis=0,
        )
        for part in range(2)
    ]
    for dy in range(per):
        wide = [jnp.concatenate([roll(part, dy), blank], axis=1) for part in (real, imag)]
        for index, value in enumerate(
            (wide[0] - roll(wide[1], half), wide[1] + roll(wide[0], half))
        ):
            start = (dy * 2 + index) * rows
            i_ref[orient, start : start + rows, :] = value[:, : 2 * half].astype(bf16)


def feature_kernel(inlines, xlines, sizes, *refs):
    rows, cols, width, pad, orients, group = sizes
    dir_in, own_ref, out_ref, dir_ref, halo, time_ref, xtap_ref, itap_ref, *refs = refs
    x_ref, i_ref, band, cross, *sems = refs
    send_sem, recv_sem, local_sem = sems
    per = 8 // group
    deep = 3 * rows
    half = per * deep
    span = group * width
    pairs = cols // per
    block = rows * width
    steps = deep // (2 * group)
    row = lax.axis_index("inline")
    col = lax.axis_index("xline")
    mine = pl.ds(pl.multiple_of(col * cols, 8), cols)

    def there(side):
        return row > 0 if side < 0 else row < inlines - 1

    barrier = pltpu.get_barrier_semaphore()
    for side in (-1, 1):
        @pl.when(there(side))
        def _(side=side):
            pl.semaphore_signal(
                barrier, inc=1, device_id={"inline": row + side}, device_id_type=MESH
            )
    for shift in range(1, xlines):
        pl.semaphore_signal(
            barrier,
            inc=1,
            device_id={"xline": lax.rem(col + shift, xlines)},
            device_id_type=MESH,
        )
    own = pltpu.make_async_copy(own_ref, halo.at[1, :, mine], local_sem.at[0])
    own.start()
    named = pltpu.make_async_copy(dir_in, dir_ref, local_sem.at[1])
    named.start()
    sides = (row > 0).astype(jnp.int32) + (row < inlines - 1).astype(jnp.int32)
    pl.semaphore_wait(barrier, sides + xlines - 1)

    def along_line(side):
        return pltpu.make_async_remote_copy(
            src_ref=own_ref,
            dst_ref=halo.at[1 - side, :, mine],
            send_sem=send_sem.at[1 - side, 0],
            recv_sem=recv_sem.at[1 - side, 0],
            device_id={"inline": row + side},
            device_id_type=MESH,
        )

    def to_partner(part, shift):
        return pltpu.make_async_remote_copy(
            src_ref=own_ref if part == 1 else halo.at[part, :, mine],
            dst_ref=halo.at[part, :, mine],
            send_sem=send_sem.at[part, shift],
            recv_sem=recv_sem.at[part, shift],
            device_id={"xline": lax.rem(col + shift, xlines)},
            device_id_type=MESH,
        )

    for side in (-1, 1):
        @pl.when(there(side))
        def _(side=side):
            along_line(side).start()
    for shift in range(1, xlines):
        to_partner(1, shift).start()

    for side in (-1, 1):
        @pl.when(jnp.logical_not(there(side)))
        def _(side=side):
            halo[1 + side] = jnp.zeros(halo.shape[1:], halo.dtype)

    @pl.loop(0, DIPS)
    def _(dip):
        time_table(dip, time_ref)

    named.wait()

    shape = (rows, cols, width, group)
    space_taps(orients, dir_ref, shape, col, xtap_ref, itap_ref)

    @pl.loop(0, orients)
    def _(orient):
        space_tables(orient, shape, xtap_ref, itap_ref, x_ref, i_ref)

    def make_band(part):
        for dip in range(DIPS):
            band[dip, part * block : (part + 1) * block, :] = jnp.dot(
                halo[part].reshape(block, LANES), time_ref[dip], preferred_element_type=f32
            ).astype(bf16)

    def across(orient, dip, step):
        mixed = [
            jnp.dot(
                x_ref[orient],
                band[dip, (2 * step + h) * span : (2 * step + h + 1) * span, :],
                preferred_element_type=f32,
            )
            for h in range(2)
        ]
        for yp in range(pairs):
            slots = [[], [], [], []]
            for h in range(2):
                with_cos = mixed[h][yp * 8 : (yp + 1) * 8]
                with_sin = mixed[h][(pairs + yp) * 8 : (pairs + yp + 1) * 8]
                cu, cv = with_cos[:, :LANES], with_cos[:, LANES:]
                su, sv = with_sin[:, :LANES], with_sin[:, LANES:]
                for slot, value in zip(slots, (cu - sv, su + cv, cu + sv, su - cv)):
                    slot.append(value)
            for index, slot in enumerate(slots):
                q, r = index // 2, index % 2
                start = ((q * pairs + yp) * 2 + r) * half + step * 16
                cross[orient, start : start + 16, :] = jnp.concatenate(slot, axis=0).astype(bf16)

    def along(orient, q, j):
        start = (q * pairs + 2 * j) * 2 * half
        operand = jnp.concatenate(
            [
                cross[orient, start : start + 2 * half, :],
                cross[orient, start + 2 * half : start + 4 * half, :],
            ],
            axis=1,
        )
        total = jnp.dot(i_ref[orient], operand, preferred_element_type=f32)
        for dy in range(per):
            re = total[(2 * dy) * rows : (2 * dy + 1) * rows]
            im = total[(2 * dy + 1) * rows : (2 * dy + 2) * rows]
            square = re * re + im * im + eps_mag
            size = square * lax.rsqrt(square)
            for h in range(2):
                out_ref[
                    (2 * j + h) * per + dy, pl.ds(2 * orient + q, rows, stride=pad), :
                ] = size[:, h * LANES : (h + 1) * LANES]

    inner = range(steps // 3, 2 * steps // 3)
    outer = [step for step in range(steps) if step not in inner]

    def dip_of(orient):
        return dir_ref[orient] // AZIMUTHS

    def own_rows(first, last, stride):
        @pl.loop(first, last, step=stride)
        def _(start):
            for orient in [start + index for index in range(stride)]:
                for step in inner:
                    across(orient, dip_of(orient), step)

    own.wait()
    for shift in range(1, xlines):
        to_partner(1, shift).wait_recv()
    make_band(1)
    pair = 2 if orients % 2 == 0 else 1
    early = round_up(orients // 2, pair)
    own_rows(0, early, pair)
    for side in (-1, 1):
        @pl.when(there(side))
        def _(side=side):
            along_line(-side).wait_recv()
            for shift in range(1, xlines):
                to_partner(1 + side, shift).start()
    own_rows(early, orients, pair)
    for y in range(cols):
        for extra in range(pad - 2 * orients):
            out_ref[y, pl.ds(2 * orients + extra, rows, stride=pad), :] = jnp.full(
                (rows, LANES), 1.0 if extra == 0 else 0.0, f32
            )
    for shift in range(1, xlines):
        to_partner(1, shift).wait_send()
    for side in (-1, 1):
        @pl.when(there(side))
        def _(side=side):
            along_line(side).wait_send()
            for shift in range(1, xlines):
                to_partner(1 + side, shift).wait()
    make_band(0)
    make_band(2)

    for step in outer:
        across(0, dip_of(0), step)

    pieces = [(q, j) for q in range(2) for j in range(pairs // 2)]
    share = -(-len(pieces) // len(outer))

    stride = math.gcd(orients - 1, 3)

    @pl.loop(1, orients, step=stride)
    def _(first):
        for orient in [first + index for index in range(stride)]:
            dip = dip_of(orient)
            for index, step in enumerate(outer):
                across(orient, dip, step)
                for q, j in pieces[index * share : (index + 1) * share]:
                    along(orient - 1, q, j)

    for q, j in pieces:
        along(orients - 1, q, j)


def make_features(traces, directions, pad):
    inlines, xlines = lax.axis_size("inline"), lax.axis_size("xline")
    rows, cols, samples = traces.shape
    orients = directions.shape[0]
    width = xlines * cols
    group = 4
    assert group * width + cols <= 2 * LANES
    per = 8 // group
    sizes = (rows, cols, width, pad, orients, group)
    return pl.pallas_call(
        functools.partial(feature_kernel, inlines, xlines, sizes),
        out_shape=jax.ShapeDtypeStruct((cols, rows * pad, samples), f32),
        in_specs=[pl.BlockSpec(memory_space=HBM)] * 2,
        out_specs=pl.BlockSpec(memory_space=VMEM),
        scratch_shapes=[
            pltpu.SMEM((orients,), jnp.int32),
            pltpu.VMEM((3, rows, width, samples), bf16),
            pltpu.VMEM((DIPS, samples, 2 * samples), bf16),
            pltpu.VMEM((2, round_up(orients, 8), 2 * LANES), f32),
            pltpu.VMEM((2, round_up(orients, 8), LANES), f32),
            pltpu.VMEM((orients, 2 * cols * group, group * width), bf16),
            pltpu.VMEM((orients, 2 * per * rows, 2 * per * 3 * rows), bf16),
            pltpu.VMEM((DIPS, 3 * rows * width, 2 * samples), bf16),
            pltpu.VMEM((orients, 4 * cols * 3 * rows, samples), bf16),
            pltpu.SemaphoreType.DMA((3, xlines)),
            pltpu.SemaphoreType.DMA((3, xlines)),
            pltpu.SemaphoreType.DMA((2,)),
        ],
        compiler_params=pltpu.CompilerParams(
            collective_id=0, has_side_effects=True, vmem_limit_bytes=40 << 20
        ),
        name="features",
    )(
        pltpu.with_memory_space_constraint(directions, HBM),
        pltpu.with_memory_space_constraint(traces, HBM),
    )


def split3(value):
    high = value.astype(bf16)
    rest = value - high.astype(f32)
    mid = rest.astype(bf16)
    low = (rest - mid.astype(f32)).astype(bf16)
    return high, mid, low


def column(row):
    return jnp.transpose(jnp.broadcast_to(row, (row.shape[1], row.shape[1])))


def padded(value, fill):
    rows, lanes = value.shape
    wide = jnp.concatenate([value, jnp.full((rows, LANES - lanes), fill, f32)], axis=1)
    full = jnp.concatenate([wide, jnp.full((LANES - rows, LANES), fill, f32)], axis=0)
    return jnp.transpose(full)


def first_params(mean_ref, var_ref, weight_ref):
    comps = mean_ref.shape[1]
    means = padded(mean_ref[...], 0.0)[:comps]
    shift_row = jnp.mean(means, axis=0, keepdims=True)
    weights = jnp.broadcast_to(padded(weight_ref[...], 1.0)[:comps, :1], (comps, LANES))
    return (means - shift_row, padded(var_ref[...], 1.0)[:comps], weights), shift_row


def packing(comps, count):
    wide = 2 * count + 1
    groups = LANES // wide
    return wide, -(-comps // groups)


def packed(summed, count, pad):
    comps = summed.shape[0]
    wide, height = packing(comps, count)
    lane = lax.broadcasted_iota(jnp.int32, summed.shape, 1)
    close = jnp.where(lane <= count, summed, pltpu.roll(summed, LANES - (pad - count - 1), 1))
    close = jnp.where(lane < wide, close, 0.0)
    out = close[:height]
    for first in range(height, comps, height):
        part = close[first : min(first + height, comps)]
        if part.shape[0] < height:
            blank = jnp.zeros((height - part.shape[0], LANES), f32)
            part = jnp.concatenate([part, blank], axis=0)
        out = out + pltpu.roll(part, (first // height) * wide, 1)
    return out


def unpacked(folded, comps, count, pad):
    wide, height = packing(comps, count)
    parts = []
    for first in range(0, comps, height):
        shift = (first // height) * wide
        part = pltpu.roll(folded, LANES - shift, 1) if shift else folded
        parts.append(part[: min(height, comps - first)])
    close = jnp.concatenate(parts, axis=0)
    lane = lax.broadcasted_iota(jnp.int32, close.shape, 1)
    return jnp.where(lane <= count, close, pltpu.roll(close, pad - count - 1, 1))


def next_params(folded, params, sizes):
    pad, count, cells = sizes
    means, spreads, _ = params
    comps = means.shape[0]
    total = unpacked(folded, comps, count, pad)
    used = lax.broadcasted_iota(jnp.int32, (comps, LANES), 1) < count
    mass = total[:, count : count + 1]
    first = jnp.where(used, total, 0.0)
    second = jnp.where(used, pltpu.roll(total, LANES - pad, 1), 0.0)
    below = mass + 1.0
    new_means = (first + means) / below
    centred = second - 2.0 * new_means * first + new_means * new_means * mass
    new_spreads = jnp.where(used, (centred + spreads) / below, 1.0)
    return new_means, new_spreads, jnp.broadcast_to(below / (cells + comps), (comps, LANES))


def peers(inlines, xlines):
    row = lax.axis_index("inline")
    col = lax.axis_index("xline")

    def turned(index, shift, size):
        moved = index + shift
        return jnp.where(moved >= size, moved - size, moved) if shift else index

    return [
        {"inline": turned(row, down, inlines), "xline": turned(col, side, xlines)}
        for down in range(inlines)
        for side in range(xlines)
        if down or side
    ]


def gather_sum(others, me, payload, slots, send_sem, recv_sem):
    def copy(index):
        return pltpu.make_async_remote_copy(
            src_ref=payload,
            dst_ref=slots.at[me],
            send_sem=send_sem.at[index],
            recv_sem=recv_sem.at[index],
            device_id=others[index],
            device_id_type=MESH,
        )

    for index in range(len(others)):
        copy(index).start()
    slots[me] = payload[...]
    for index in range(len(others)):
        copy(index).wait()
    total = slots[0]
    for member in range(1, len(others) + 1):
        total = total + slots[member]
    return total


def em_kernel(sizes, *refs):
    cols, pad, count, chunk, together, cells, inlines, xlines = sizes
    feat_ref, mean_ref, var_ref, weight_ref, sum_ref, last_ref, post_ref, *refs = refs
    split_ref, table, total, shift_ref, wide, payload, slots, send_sem, recv_sem = refs
    comps = mean_ref.shape[1]
    rows = post_ref.shape[0]
    me = lax.axis_index("inline") * xlines + lax.axis_index("xline")
    others = peers(inlines, xlines)
    barrier = pltpu.get_barrier_semaphore()
    for other in others:
        pl.semaphore_signal(barrier, inc=1, device_id=other, device_id_type=MESH)

    def prepare(params):
        lane = lax.broadcasted_iota(jnp.int32, (comps, 2 * LANES), 1)
        means = jnp.concatenate([params[0], jnp.zeros((comps, LANES), f32)], axis=1)
        spreads = jnp.concatenate([params[1], jnp.ones((comps, LANES), f32)], axis=1)
        used = lane < count
        inverse = jnp.where(used, 1.0 / spreads, 0.0)
        scaled = means * inverse
        terms = jnp.where(used, jnp.log(2.0 * math.pi * spreads) + means * scaled, 0.0)
        constant = jnp.log(params[2][:, :1]) - 0.5 * jnp.sum(terms, axis=1, keepdims=True)
        row = jnp.where(used, scaled, 0.0) + jnp.where(lane == count, constant, 0.0)
        row = row + pltpu.roll(-0.5 * inverse, pad, 1)
        parts = split3(row * LOG2E)
        for index, part in enumerate(parts):
            part = part.astype(f32)
            tiled = part + pltpu.roll(part, 2 * pad, 1) + pltpu.roll(part, 4 * pad, 1)
            table[index * comps : (index + 1) * comps, :] = tiled.astype(bf16)
        total[...] = jnp.zeros_like(total)

    def sweep(step, last):
        weights = table[:, : 6 * pad]

        def scores(j, first):
            span = slice(first * LANES, (first + chunk) * LANES)
            line = step * together + j
            if last:
                operand = split_ref[line, :, span]
            else:
                base = pl.multiple_of(line * pad, 8)
                values = jnp.concatenate(
                    [
                        feat_ref[first + y, pl.ds(base, pad), :] - shift_ref[...]
                        for y in range(chunk)
                    ],
                    axis=1,
                )
                both = jnp.concatenate([values, values * values], axis=0)
                operand = jnp.concatenate(split3(both), axis=0)
                split_ref[line, :, span] = operand
            wide_score = jnp.dot(weights, operand, preferred_element_type=f32)
            score = wide_score[:comps] + (
                wide_score[comps : 2 * comps] + wide_score[2 * comps : 3 * comps]
            )
            return operand, score

        pieces = [(j, first) for j in range(together) for first in range(0, cols, chunk)]
        ahead = scores(*pieces[0])
        moment = total[...]
        for index, (j, first) in enumerate(pieces):
            operand, score = ahead
            if index + 1 < len(pieces):
                ahead = scores(*pieces[index + 1])
            exponent = jnp.exp2(score - jnp.max(score, axis=0, keepdims=True))
            share = exponent * (1.0 / jnp.sum(exponent, axis=0, keepdims=True))
            high = share.astype(bf16)
            low = (share - high.astype(f32)).astype(bf16)
            moment = moment + lax.dot_general(
                jnp.concatenate([high, low], axis=0),
                operand[: 4 * pad],
                (((1,), (1,)), ((), ())),
                preferred_element_type=f32,
            )
            if last:
                for y in range(chunk):
                    wide[pl.ds((j * comps) * cols + first + y, comps, stride=cols), :] = share[
                        :, y * LANES : (y + 1) * LANES
                    ]
        total[...] = moment
        if last:
            for j in range(together):
                for k in range(comps):
                    start = (j * comps + k) * cols
                    post_ref[step * together + j, k] = wide[start : start + cols, :].astype(bf16)

    def fold():
        both = total[:comps] + total[comps:]
        both = jnp.concatenate([both, jnp.zeros((comps, LANES - 4 * pad), f32)], axis=1)
        summed = both + pltpu.roll(both, LANES - 2 * pad, 1)
        return packed(summed, count, pad)

    params, shift_row = first_params(mean_ref, var_ref, weight_ref)
    shift_ref[...] = column(shift_row)[:pad]
    prepare(params)
    pl.loop(0, rows // together)(lambda step: sweep(step, False))
    payload[0] = fold()
    pl.semaphore_wait(barrier, len(others))
    sum_ref[...] = gather_sum(
        others, me, payload.at[0], slots.at[0], send_sem.at[0], recv_sem.at[0]
    )
    prepare(next_params(sum_ref[...], params, (pad, count, cells)))
    pl.loop(0, rows // together)(lambda step: sweep(step, True))
    payload[1] = fold()
    last_ref[...] = gather_sum(
        others, me, payload.at[1], slots.at[1], send_sem.at[1], recv_sem.at[1]
    )


def mixture(features, init, count, rows, cells):
    inlines, xlines = lax.axis_size("inline"), lax.axis_size("xline")
    members = inlines * xlines
    comps = init[0].shape[1]
    cols, flat, samples = features.shape
    pad = flat // rows
    assert 4 * pad <= LANES and comps % 16 == 0
    chunk = 4
    together = math.gcd(rows, 8)
    assert rows % together == 0 and cols % chunk == 0
    folded = (packing(comps, count)[1], LANES)
    sizes = (cols, pad, count, chunk, together, cells, inlines, xlines)
    return pl.pallas_call(
        functools.partial(em_kernel, sizes),
        out_shape=[
            jax.ShapeDtypeStruct(folded, f32),
            jax.ShapeDtypeStruct(folded, f32),
            jax.ShapeDtypeStruct((rows, comps, cols, samples), bf16),
        ],
        in_specs=[pl.BlockSpec(memory_space=VMEM)] * 4,
        out_specs=[pl.BlockSpec(memory_space=VMEM)] * 3,
        scratch_shapes=[
            pltpu.VMEM((rows, 6 * pad, cols * samples), bf16),
            pltpu.VMEM((3 * comps, 2 * LANES), bf16),
            pltpu.VMEM((2 * comps, 4 * pad), f32),
            pltpu.VMEM((pad, LANES), f32),
            pltpu.VMEM((together * comps * cols, samples), f32),
            pltpu.VMEM((2,) + folded, f32),
            pltpu.VMEM((2, members) + folded, f32),
            pltpu.SemaphoreType.DMA((2, members - 1)),
            pltpu.SemaphoreType.DMA((2, members - 1)),
        ],
        compiler_params=pltpu.CompilerParams(
            collective_id=1, has_side_effects=True, vmem_limit_bytes=36 << 20
        ),
        name="mixture",
    )(features, *init)


def final_kernel(sizes, *refs):
    *sums, post_in, mean_ref, var_ref, weight_ref = refs[:-5]
    mean_out, var_out, weight_out, post_out, sems = refs[-5:]
    count = sizes[1]
    parts = sems.shape[0]
    depth = post_in.shape[0] // parts

    def copy(part):
        span = pl.ds(part * depth, depth)
        return pltpu.make_async_copy(post_in.at[span], post_out.at[span], sems.at[part])

    for part in range(parts):
        copy(part).start()
    params, shift_row = first_params(mean_ref, var_ref, weight_ref)
    for summed in sums:
        params = next_params(summed[...], params, sizes)
    means, spreads, weights = params
    comps = means.shape[0]
    blank = jnp.zeros((LANES - comps, LANES), f32)
    turned = [
        jnp.transpose(jnp.concatenate([value, blank], axis=0))[:, :comps]
        for value in (means + shift_row, spreads, weights)
    ]
    mean_out[...] = turned[0][:count]
    var_out[...] = turned[1][:count]
    weight_out[...] = turned[2][:1]
    for part in range(parts):
        copy(part).wait()


def finish(sums, posterior, init, sizes):
    count, comps = init[0].shape
    inputs = sums + [posterior] + list(init)
    return pl.pallas_call(
        functools.partial(final_kernel, sizes),
        out_shape=[
            jax.ShapeDtypeStruct((count, comps), f32),
            jax.ShapeDtypeStruct((count, comps), f32),
            jax.ShapeDtypeStruct((1, comps), f32),
            jax.ShapeDtypeStruct(posterior.shape, posterior.dtype),
        ],
        in_specs=[pl.BlockSpec(memory_space=VMEM)] * len(inputs),
        out_specs=[pl.BlockSpec(memory_space=VMEM)] * 3 + [pl.BlockSpec(memory_space=HBM)],
        scratch_shapes=[pltpu.SemaphoreType.DMA((math.gcd(8, posterior.shape[0]),))],
        compiler_params=pltpu.CompilerParams(vmem_limit_bytes=4 << 20),
        name="finish",
    )(*inputs)


def per_device(traces, directions, init_means, init_variances, init_weights):
    rows, cols, samples = traces.shape
    assert samples == LANES and rows >= HALF and rows % 8 == 0 and cols % 4 == 0
    count = 2 * directions.shape[0]
    pad = round_up(count + 1, 8)
    comps = init_weights.shape[0]
    cells = lax.axis_size("inline") * rows * lax.axis_size("xline") * cols * samples
    init = (init_means.T, init_variances.T, init_weights.reshape(1, comps))
    features = make_features(traces, directions, pad)
    *sums, posterior = mixture(features, init, count, rows, cells)
    means, spreads, weights, posterior = finish(sums, posterior, init, (pad, count, cells))
    return posterior, means.T, spreads.T, weights.reshape(comps)


def solution(mesh):
    in_specs = (P(("slab", "inline"), "xline", None), P(), P(), P(), P())
    out_specs = (
        P(("slab", "inline"), None, "xline", None),
        P("slab", None),
        P("slab", None),
        P("slab"),
    )
    return jax.shard_map(
        per_device, mesh=mesh, in_specs=in_specs, out_specs=out_specs, check_vma=False
    )
```

```python
import functools
import math

import jax
import jax.numpy as jnp
from jax import lax
from jax.experimental import pallas as pl
from jax.experimental.pallas import tpu as pltpu
from jax.sharding import PartitionSpec as P

TAPS = 31
HALF = 15
AZIMUTHS = 8
DIPS = 4
LANES = 128

eps_mag = 0.01
wavenumber = math.pi / 4.0
width_scale = HALF / 3.0
norm = math.sqrt(
    sum(math.exp(-n * n / (width_scale * width_scale)) for n in range(-HALF, HALF + 1))
)
MESH = pl.DeviceIdType.MESH
LOG2E = math.log2(math.e)
f32 = jnp.float32
bf16 = jnp.bfloat16
VMEM = pltpu.MemorySpace.VMEM
SMEM = pltpu.MemorySpace.SMEM
HBM = pltpu.MemorySpace.HBM


def round_up(value, step):
    return -(-value // step) * step


def iotas(shape):
    return (
        lax.broadcasted_iota(jnp.int32, shape, 0),
        lax.broadcasted_iota(jnp.int32, shape, 1),
    )


def roll(value, amount):
    return value if amount == 0 else pltpu.roll(value, amount, 1)


def taps(wave, difference):
    offset = (difference - HALF).astype(f32)
    phase = offset * jnp.concatenate([wave] * (difference.shape[1] // LANES), axis=1)
    envelope = jnp.exp(-offset * offset / (2.0 * width_scale * width_scale)) / norm
    hit = jnp.logical_and(difference >= 0, difference < TAPS)
    real = jnp.where(hit, envelope * jnp.cos(phase), 0.0)
    imag = jnp.where(hit, envelope * jnp.sin(phase), 0.0)
    return real, imag


def time_table(dip, time_ref):
    dip_angle = jnp.full((8, LANES), (dip + 1).astype(f32)) * (math.pi / (2 * DIPS + 2))
    wave = wavenumber * jnp.cos(dip_angle)
    sub, lane = iotas((8, LANES))
    bases = taps(wave, jnp.bitwise_and(sub - lane + HALF, LANES - 1))
    for s in range(0, LANES, 16):
        pieces = []
        for start in (s, s + 8):
            near = jnp.abs(sub + start - lane) <= HALF
            pieces.append(
                jnp.concatenate([jnp.where(near, roll(base, start), 0.0) for base in bases], axis=1)
            )
        time_ref[dip, s : s + 16, :] = jnp.concatenate(pieces, axis=0).astype(bf16)


def space_taps(orients, dir_ref, sizes, col, xtap_ref, itap_ref):
    rows, cols, width, group = sizes
    lanes = 2 * LANES
    per = 8 // group
    height = xtap_ref.shape[1]
    sub, lane = iotas((height, LANES))
    azimuth, dip = jnp.zeros((height, LANES), f32), jnp.zeros((height, LANES), f32)
    for orient in range(orients):
        direction = dir_ref[orient]
        here = sub == orient
        azimuth = jnp.where(here, (direction % AZIMUTHS).astype(f32), azimuth)
        dip = jnp.where(here, (direction // AZIMUTHS + 1).astype(f32), dip)
    azimuth = azimuth * (math.pi / AZIMUTHS)
    dip_angle = dip * (math.pi / (2 * DIPS + 2))
    inline_wave = wavenumber * (jnp.sin(dip_angle) * jnp.cos(azimuth))
    xline_wave = wavenumber * (jnp.sin(dip_angle) * jnp.sin(azimuth))
    for index, part in enumerate(
        taps(inline_wave, jnp.where(lane % per == 0, lane // per, -1))
    ):
        itap_ref[index] = part
    lane = lax.broadcasted_iota(jnp.int32, (height, lanes), 1)
    place = jnp.where(lane >= group * width, lane - lanes, lane)
    for index, part in enumerate(taps(xline_wave, place - col * cols + HALF)):
        xtap_ref[index] = part


def space_tables(orient, sizes, xtap_ref, itap_ref, x_ref, i_ref):
    rows, cols, width, group = sizes
    lanes = 2 * LANES
    per = 8 // group
    sub, lane = iotas((8, lanes))
    row, step = sub // per, sub % per
    mine = jnp.logical_and(lane >= row * width, lane < (row + 1) * width)
    for part in range(2):
        line = jnp.broadcast_to(xtap_ref[part, pl.ds(orient, 1), :], (8, lanes))
        both = line
        for dy in range(1, per):
            both = jnp.where(step == dy, roll(line, dy), both)
        base = both
        for r in range(1, group):
            base = jnp.where(row == r, roll(both, r * width), base)
        for y in range(0, cols, 2 * per):
            pair = jnp.concatenate(
                [jnp.where(mine, roll(base, y + dy), 0.0) for dy in (0, per)], axis=0
            )
            start = (part * cols + y) * group
            x_ref[orient, start : start + 16, :] = pair[:, : group * width].astype(bf16)

    half = per * 3 * rows
    blank = jnp.zeros((rows, LANES), f32)
    real, imag = [
        pltpu.roll(
            jnp.broadcast_to(itap_ref[part, pl.ds(orient, 1), :], (rows, LANES)),
            per * (rows - HALF),
            1,
            stride=per,
            stride_axis=0,
        )
        for part in range(2)
    ]
    for dy in range(per):
        wide = [jnp.concatenate([roll(part, dy), blank], axis=1) for part in (real, imag)]
        for index, value in enumerate(
            (wide[0] - roll(wide[1], half), wide[1] + roll(wide[0], half))
        ):
            start = (dy * 2 + index) * rows
            i_ref[orient, start : start + rows, :] = value[:, : 2 * half].astype(bf16)


def feature_kernel(inlines, xlines, sizes, *refs):
    rows, cols, width, pad, orients, group = sizes
    dir_in, own_ref, out_ref, dir_ref, halo, time_ref, xtap_ref, itap_ref, *refs = refs
    x_ref, i_ref, band, cross, *sems = refs
    send_sem, recv_sem, local_sem = sems
    per = 8 // group
    deep = 3 * rows
    half = per * deep
    span = group * width
    pairs = cols // per
    block = rows * width
    steps = deep // (2 * group)
    row = lax.axis_index("inline")
    col = lax.axis_index("xline")
    mine = pl.ds(pl.multiple_of(col * cols, 8), cols)

    def there(side):
        return row > 0 if side < 0 else row < inlines - 1

    barrier = pltpu.get_barrier_semaphore()
    for side in (-1, 1):
        @pl.when(there(side))
        def _(side=side):
            pl.semaphore_signal(
                barrier, inc=1, device_id={"inline": row + side}, device_id_type=MESH
            )
    for shift in range(1, xlines):
        pl.semaphore_signal(
            barrier,
            inc=1,
            device_id={"xline": lax.rem(col + shift, xlines)},
            device_id_type=MESH,
        )
    own = pltpu.make_async_copy(own_ref, halo.at[1, :, mine], local_sem.at[0])
    own.start()
    named = pltpu.make_async_copy(dir_in, dir_ref, local_sem.at[1])
    named.start()
    sides = (row > 0).astype(jnp.int32) + (row < inlines - 1).astype(jnp.int32)
    pl.semaphore_wait(barrier, sides + xlines - 1)

    def along_line(side):
        return pltpu.make_async_remote_copy(
            src_ref=own_ref,
            dst_ref=halo.at[1 - side, :, mine],
            send_sem=send_sem.at[1 - side, 0],
            recv_sem=recv_sem.at[1 - side, 0],
            device_id={"inline": row + side},
            device_id_type=MESH,
        )

    def to_partner(part, shift):
        return pltpu.make_async_remote_copy(
            src_ref=own_ref if part == 1 else halo.at[part, :, mine],
            dst_ref=halo.at[part, :, mine],
            send_sem=send_sem.at[part, shift],
            recv_sem=recv_sem.at[part, shift],
            device_id={"xline": lax.rem(col + shift, xlines)},
            device_id_type=MESH,
        )

    for side in (-1, 1):
        @pl.when(there(side))
        def _(side=side):
            along_line(side).start()
    for shift in range(1, xlines):
        to_partner(1, shift).start()

    for side in (-1, 1):
        @pl.when(jnp.logical_not(there(side)))
        def _(side=side):
            halo[1 + side] = jnp.zeros(halo.shape[1:], halo.dtype)

    @pl.loop(0, DIPS)
    def _(dip):
        time_table(dip, time_ref)

    named.wait()

    shape = (rows, cols, width, group)
    space_taps(orients, dir_ref, shape, col, xtap_ref, itap_ref)

    @pl.loop(0, orients)
    def _(orient):
        space_tables(orient, shape, xtap_ref, itap_ref, x_ref, i_ref)

    def make_band(part):
        for dip in range(DIPS):
            band[dip, part * block : (part + 1) * block, :] = jnp.dot(
                halo[part].reshape(block, LANES), time_ref[dip], preferred_element_type=f32
            ).astype(bf16)

    def across(orient, dip, step):
        mixed = [
            jnp.dot(
                x_ref[orient],
                band[dip, (2 * step + h) * span : (2 * step + h + 1) * span, :],
                preferred_element_type=f32,
            )
            for h in range(2)
        ]
        for yp in range(pairs):
            slots = [[], [], [], []]
            for h in range(2):
                with_cos = mixed[h][yp * 8 : (yp + 1) * 8]
                with_sin = mixed[h][(pairs + yp) * 8 : (pairs + yp + 1) * 8]
                cu, cv = with_cos[:, :LANES], with_cos[:, LANES:]
                su, sv = with_sin[:, :LANES], with_sin[:, LANES:]
                for slot, value in zip(slots, (cu - sv, su + cv, cu + sv, su - cv)):
                    slot.append(value)
            for index, slot in enumerate(slots):
                q, r = index // 2, index % 2
                start = ((q * pairs + yp) * 2 + r) * half + step * 16
                cross[orient, start : start + 16, :] = jnp.concatenate(slot, axis=0).astype(bf16)

    def along(orient, q, j):
        start = (q * pairs + 2 * j) * 2 * half
        operand = jnp.concatenate(
            [
                cross[orient, start : start + 2 * half, :],
                cross[orient, start + 2 * half : start + 4 * half, :],
            ],
            axis=1,
        )
        total = jnp.dot(i_ref[orient], operand, preferred_element_type=f32)
        for dy in range(per):
            re = total[(2 * dy) * rows : (2 * dy + 1) * rows]
            im = total[(2 * dy + 1) * rows : (2 * dy + 2) * rows]
            square = re * re + im * im + eps_mag
            size = square * lax.rsqrt(square)
            for h in range(2):
                out_ref[
                    (2 * j + h) * per + dy, pl.ds(2 * orient + q, rows, stride=pad), :
                ] = size[:, h * LANES : (h + 1) * LANES]

    inner = range(steps // 3, 2 * steps // 3)
    outer = [step for step in range(steps) if step not in inner]

    def dip_of(orient):
        return dir_ref[orient] // AZIMUTHS

    def own_rows(first, last, stride):
        @pl.loop(first, last, step=stride)
        def _(start):
            for orient in [start + index for index in range(stride)]:
                for step in inner:
                    across(orient, dip_of(orient), step)

    own.wait()
    for shift in range(1, xlines):
        to_partner(1, shift).wait_recv()
    make_band(1)
    pair = math.gcd(orients, 5)
    early = round_up(orients // 2, pair)
    own_rows(0, early, pair)
    for side in (-1, 1):
        @pl.when(there(side))
        def _(side=side):
            along_line(-side).wait_recv()
            for shift in range(1, xlines):
                to_partner(1 + side, shift).start()
    own_rows(early, orients, pair)
    for y in range(cols):
        for extra in range(pad - 2 * orients):
            out_ref[y, pl.ds(2 * orients + extra, rows, stride=pad), :] = jnp.full(
                (rows, LANES), 1.0 if extra == 0 else 0.0, f32
            )
    for shift in range(1, xlines):
        to_partner(1, shift).wait_send()
    for side in (-1, 1):
        @pl.when(there(side))
        def _(side=side):
            along_line(side).wait_send()
            for shift in range(1, xlines):
                to_partner(1 + side, shift).wait()
    make_band(0)
    make_band(2)

    for step in outer:
        across(0, dip_of(0), step)

    pieces = [(q, j) for q in range(2) for j in range(pairs // 2)]
    share = -(-len(pieces) // len(outer))

    stride = math.gcd(orients - 1, 3)

    @pl.loop(1, orients, step=stride)
    def _(first):
        for orient in [first + index for index in range(stride)]:
            dip = dip_of(orient)
            for index, step in enumerate(outer):
                across(orient, dip, step)
                for q, j in pieces[index * share : (index + 1) * share]:
                    along(orient - 1, q, j)

    for q, j in pieces:
        along(orients - 1, q, j)


def make_features(traces, directions, pad):
    inlines, xlines = lax.axis_size("inline"), lax.axis_size("xline")
    rows, cols, samples = traces.shape
    orients = directions.shape[0]
    width = xlines * cols
    group = 4
    assert group * width + cols <= 2 * LANES
    per = 8 // group
    sizes = (rows, cols, width, pad, orients, group)
    return pl.pallas_call(
        functools.partial(feature_kernel, inlines, xlines, sizes),
        out_shape=jax.ShapeDtypeStruct((cols, rows * pad, samples), f32),
        in_specs=[pl.BlockSpec(memory_space=HBM)] * 2,
        out_specs=pl.BlockSpec(memory_space=VMEM),
        scratch_shapes=[
            pltpu.SMEM((orients,), jnp.int32),
            pltpu.VMEM((3, rows, width, samples), bf16),
            pltpu.VMEM((DIPS, samples, 2 * samples), bf16),
            pltpu.VMEM((2, round_up(orients, 8), 2 * LANES), f32),
            pltpu.VMEM((2, round_up(orients, 8), LANES), f32),
            pltpu.VMEM((orients, 2 * cols * group, group * width), bf16),
            pltpu.VMEM((orients, 2 * per * rows, 2 * per * 3 * rows), bf16),
            pltpu.VMEM((DIPS, 3 * rows * width, 2 * samples), bf16),
            pltpu.VMEM((orients, 4 * cols * 3 * rows, samples), bf16),
            pltpu.SemaphoreType.DMA((3, xlines)),
            pltpu.SemaphoreType.DMA((3, xlines)),
            pltpu.SemaphoreType.DMA((2,)),
        ],
        compiler_params=pltpu.CompilerParams(
            collective_id=0, has_side_effects=True, vmem_limit_bytes=40 << 20
        ),
        name="features",
    )(
        pltpu.with_memory_space_constraint(directions, HBM),
        pltpu.with_memory_space_constraint(traces, HBM),
    )


def split3(value):
    high = value.astype(bf16)
    rest = value - high.astype(f32)
    mid = rest.astype(bf16)
    low = (rest - mid.astype(f32)).astype(bf16)
    return high, mid, low


def column(row):
    return jnp.transpose(jnp.broadcast_to(row, (row.shape[1], row.shape[1])))


def padded(value, fill):
    rows, lanes = value.shape
    wide = jnp.concatenate([value, jnp.full((rows, LANES - lanes), fill, f32)], axis=1)
    full = jnp.concatenate([wide, jnp.full((LANES - rows, LANES), fill, f32)], axis=0)
    return jnp.transpose(full)


def first_params(mean_ref, var_ref, weight_ref):
    comps = mean_ref.shape[1]
    means = padded(mean_ref[...], 0.0)[:comps]
    shift_row = jnp.mean(means, axis=0, keepdims=True)
    weights = jnp.broadcast_to(padded(weight_ref[...], 1.0)[:comps, :1], (comps, LANES))
    return (means - shift_row, padded(var_ref[...], 1.0)[:comps], weights), shift_row


def packing(comps, count):
    wide = 2 * count + 1
    groups = LANES // wide
    return wide, -(-comps // groups)


def packed(summed, count, pad):
    comps = summed.shape[0]
    wide, height = packing(comps, count)
    lane = lax.broadcasted_iota(jnp.int32, summed.shape, 1)
    close = jnp.where(lane <= count, summed, pltpu.roll(summed, LANES - (pad - count - 1), 1))
    close = jnp.where(lane < wide, close, 0.0)
    out = close[:height]
    for first in range(height, comps, height):
        part = close[first : min(first + height, comps)]
        if part.shape[0] < height:
            blank = jnp.zeros((height - part.shape[0], LANES), f32)
            part = jnp.concatenate([part, blank], axis=0)
        out = out + pltpu.roll(part, (first // height) * wide, 1)
    return out


def unpacked(folded, comps, count, pad):
    wide, height = packing(comps, count)
    parts = []
    for first in range(0, comps, height):
        shift = (first // height) * wide
        part = pltpu.roll(folded, LANES - shift, 1) if shift else folded
        parts.append(part[: min(height, comps - first)])
    close = jnp.concatenate(parts, axis=0)
    lane = lax.broadcasted_iota(jnp.int32, close.shape, 1)
    return jnp.where(lane <= count, close, pltpu.roll(close, pad - count - 1, 1))


def next_params(folded, params, sizes):
    pad, count, cells = sizes
    means, spreads, _ = params
    comps = means.shape[0]
    total = unpacked(folded, comps, count, pad)
    used = lax.broadcasted_iota(jnp.int32, (comps, LANES), 1) < count
    mass = total[:, count : count + 1]
    first = jnp.where(used, total, 0.0)
    second = jnp.where(used, pltpu.roll(total, LANES - pad, 1), 0.0)
    below = mass + 1.0
    new_means = (first + means) / below
    centred = second - 2.0 * new_means * first + new_means * new_means * mass
    new_spreads = jnp.where(used, (centred + spreads) / below, 1.0)
    return new_means, new_spreads, jnp.broadcast_to(below / (cells + comps), (comps, LANES))


def peers(inlines, xlines):
    row = lax.axis_index("inline")
    col = lax.axis_index("xline")

    def turned(index, shift, size):
        moved = index + shift
        return jnp.where(moved >= size, moved - size, moved) if shift else index

    return [
        {"inline": turned(row, down, inlines), "xline": turned(col, side, xlines)}
        for down in range(inlines)
        for side in range(xlines)
        if down or side
    ]


def gather_sum(others, me, payload, slots, send_sem, recv_sem):
    def copy(index):
        return pltpu.make_async_remote_copy(
            src_ref=payload,
            dst_ref=slots.at[me],
            send_sem=send_sem.at[index],
            recv_sem=recv_sem.at[index],
            device_id=others[index],
            device_id_type=MESH,
        )

    for index in range(len(others)):
        copy(index).start()
    slots[me] = payload[...]
    for index in range(len(others)):
        copy(index).wait()
    total = slots[0]
    for member in range(1, len(others) + 1):
        total = total + slots[member]
    return total


def em_kernel(sizes, *refs):
    cols, pad, count, chunk, together, cells, inlines, xlines = sizes
    feat_ref, mean_ref, var_ref, weight_ref, sum_ref, last_ref, post_ref, *refs = refs
    split_ref, table, total, shift_ref, wide, payload, slots, send_sem, recv_sem = refs
    comps = mean_ref.shape[1]
    rows = post_ref.shape[0]
    me = lax.axis_index("inline") * xlines + lax.axis_index("xline")
    others = peers(inlines, xlines)
    barrier = pltpu.get_barrier_semaphore()
    for other in others:
        pl.semaphore_signal(barrier, inc=1, device_id=other, device_id_type=MESH)

    def prepare(params):
        lane = lax.broadcasted_iota(jnp.int32, (comps, 2 * LANES), 1)
        means = jnp.concatenate([params[0], jnp.zeros((comps, LANES), f32)], axis=1)
        spreads = jnp.concatenate([params[1], jnp.ones((comps, LANES), f32)], axis=1)
        used = lane < count
        inverse = jnp.where(used, 1.0 / spreads, 0.0)
        scaled = means * inverse
        terms = jnp.where(used, jnp.log(2.0 * math.pi * spreads) + means * scaled, 0.0)
        constant = jnp.log(params[2][:, :1]) - 0.5 * jnp.sum(terms, axis=1, keepdims=True)
        row = jnp.where(used, scaled, 0.0) + jnp.where(lane == count, constant, 0.0)
        row = row + pltpu.roll(-0.5 * inverse, pad, 1)
        parts = split3(row * LOG2E)
        for index, part in enumerate(parts):
            part = part.astype(f32)
            tiled = part + pltpu.roll(part, 2 * pad, 1) + pltpu.roll(part, 4 * pad, 1)
            table[index * comps : (index + 1) * comps, :] = tiled.astype(bf16)
        total[...] = jnp.zeros_like(total)

    def sweep(step, last):
        weights = table[:, : 6 * pad]

        def scores(j, first):
            span = slice(first * LANES, (first + chunk) * LANES)
            line = step * together + j
            if last:
                operand = split_ref[line, :, span]
            else:
                base = pl.multiple_of(line * pad, 8)
                values = jnp.concatenate(
                    [
                        feat_ref[first + y, pl.ds(base, pad), :] - shift_ref[...]
                        for y in range(chunk)
                    ],
                    axis=1,
                )
                both = jnp.concatenate([values, values * values], axis=0)
                operand = jnp.concatenate(split3(both), axis=0)
                split_ref[line, :, span] = operand
            wide_score = jnp.dot(weights, operand, preferred_element_type=f32)
            score = wide_score[:comps] + (
                wide_score[comps : 2 * comps] + wide_score[2 * comps : 3 * comps]
            )
            return operand, score

        pieces = [(j, first) for j in range(together) for first in range(0, cols, chunk)]
        ahead = scores(*pieces[0])
        moment = total[...]
        for index, (j, first) in enumerate(pieces):
            operand, score = ahead
            if index + 1 < len(pieces):
                ahead = scores(*pieces[index + 1])
            exponent = jnp.exp2(score - jnp.max(score, axis=0, keepdims=True))
            share = exponent * (1.0 / jnp.sum(exponent, axis=0, keepdims=True))
            high = share.astype(bf16)
            low = (share - high.astype(f32)).astype(bf16)
            moment = moment + lax.dot_general(
                jnp.concatenate([high, low], axis=0),
                operand[: 4 * pad],
                (((1,), (1,)), ((), ())),
                preferred_element_type=f32,
            )
            if last:
                for y in range(chunk):
                    wide[pl.ds((j * comps) * cols + first + y, comps, stride=cols), :] = share[
                        :, y * LANES : (y + 1) * LANES
                    ]
        total[...] = moment
        if last:
            for j in range(together):
                for k in range(comps):
                    start = (j * comps + k) * cols
                    post_ref[step * together + j, k] = wide[start : start + cols, :].astype(bf16)

    def fold():
        both = total[:comps] + total[comps:]
        both = jnp.concatenate([both, jnp.zeros((comps, LANES - 4 * pad), f32)], axis=1)
        summed = both + pltpu.roll(both, LANES - 2 * pad, 1)
        return packed(summed, count, pad)

    params, shift_row = first_params(mean_ref, var_ref, weight_ref)
    shift_ref[...] = column(shift_row)[:pad]
    prepare(params)
    pl.loop(0, rows // together)(lambda step: sweep(step, False))
    payload[0] = fold()
    pl.semaphore_wait(barrier, len(others))
    sum_ref[...] = gather_sum(
        others, me, payload.at[0], slots.at[0], send_sem.at[0], recv_sem.at[0]
    )
    prepare(next_params(sum_ref[...], params, (pad, count, cells)))
    pl.loop(0, rows // together)(lambda step: sweep(step, True))
    payload[1] = fold()
    last_ref[...] = gather_sum(
        others, me, payload.at[1], slots.at[1], send_sem.at[1], recv_sem.at[1]
    )


def mixture(features, init, count, rows, cells):
    inlines, xlines = lax.axis_size("inline"), lax.axis_size("xline")
    members = inlines * xlines
    comps = init[0].shape[1]
    cols, flat, samples = features.shape
    pad = flat // rows
    assert 4 * pad <= LANES and comps % 16 == 0
    chunk = 6
    together = math.gcd(rows, 8)
    assert rows % together == 0 and cols % chunk == 0
    folded = (packing(comps, count)[1], LANES)
    sizes = (cols, pad, count, chunk, together, cells, inlines, xlines)
    return pl.pallas_call(
        functools.partial(em_kernel, sizes),
        out_shape=[
            jax.ShapeDtypeStruct(folded, f32),
            jax.ShapeDtypeStruct(folded, f32),
            jax.ShapeDtypeStruct((rows, comps, cols, samples), bf16),
        ],
        in_specs=[pl.BlockSpec(memory_space=VMEM)] * 4,
        out_specs=[pl.BlockSpec(memory_space=VMEM)] * 3,
        scratch_shapes=[
            pltpu.VMEM((rows, 6 * pad, cols * samples), bf16),
            pltpu.VMEM((3 * comps, 2 * LANES), bf16),
            pltpu.VMEM((2 * comps, 4 * pad), f32),
            pltpu.VMEM((pad, LANES), f32),
            pltpu.VMEM((together * comps * cols, samples), f32),
            pltpu.VMEM((2,) + folded, f32),
            pltpu.VMEM((2, members) + folded, f32),
            pltpu.SemaphoreType.DMA((2, members - 1)),
            pltpu.SemaphoreType.DMA((2, members - 1)),
        ],
        compiler_params=pltpu.CompilerParams(
            collective_id=1, has_side_effects=True, vmem_limit_bytes=36 << 20
        ),
        name="mixture",
    )(features, *init)


def final_kernel(sizes, *refs):
    *sums, post_in, mean_ref, var_ref, weight_ref = refs[:-5]
    mean_out, var_out, weight_out, post_out, sems = refs[-5:]
    count = sizes[1]
    parts = sems.shape[0]
    depth = post_in.shape[0] // parts

    def copy(part):
        span = pl.ds(part * depth, depth)
        return pltpu.make_async_copy(post_in.at[span], post_out.at[span], sems.at[part])

    for part in range(parts):
        copy(part).start()
    params, shift_row = first_params(mean_ref, var_ref, weight_ref)
    for summed in sums:
        params = next_params(summed[...], params, sizes)
    means, spreads, weights = params
    comps = means.shape[0]
    blank = jnp.zeros((LANES - comps, LANES), f32)
    turned = [
        jnp.transpose(jnp.concatenate([value, blank], axis=0))[:, :comps]
        for value in (means + shift_row, spreads, weights)
    ]
    mean_out[...] = turned[0][:count]
    var_out[...] = turned[1][:count]
    weight_out[...] = turned[2][:1]
    for part in range(parts):
        copy(part).wait()


def finish(sums, posterior, init, sizes):
    count, comps = init[0].shape
    inputs = sums + [posterior] + list(init)
    return pl.pallas_call(
        functools.partial(final_kernel, sizes),
        out_shape=[
            jax.ShapeDtypeStruct((count, comps), f32),
            jax.ShapeDtypeStruct((count, comps), f32),
            jax.ShapeDtypeStruct((1, comps), f32),
            jax.ShapeDtypeStruct(posterior.shape, posterior.dtype),
        ],
        in_specs=[pl.BlockSpec(memory_space=VMEM)] * len(inputs),
        out_specs=[pl.BlockSpec(memory_space=VMEM)] * 3 + [pl.BlockSpec(memory_space=HBM)],
        scratch_shapes=[pltpu.SemaphoreType.DMA((math.gcd(8, posterior.shape[0]),))],
        compiler_params=pltpu.CompilerParams(vmem_limit_bytes=4 << 20),
        name="finish",
    )(*inputs)


def per_device(traces, directions, init_means, init_variances, init_weights):
    rows, cols, samples = traces.shape
    assert samples == LANES and rows >= HALF and rows % 8 == 0 and cols % 4 == 0
    count = 2 * directions.shape[0]
    pad = round_up(count + 1, 8)
    comps = init_weights.shape[0]
    cells = lax.axis_size("inline") * rows * lax.axis_size("xline") * cols * samples
    init = (init_means.T, init_variances.T, init_weights.reshape(1, comps))
    features = make_features(traces, directions, pad)
    *sums, posterior = mixture(features, init, count, rows, cells)
    means, spreads, weights, posterior = finish(sums, posterior, init, (pad, count, cells))
    return posterior, means.T, spreads.T, weights.reshape(comps)


def solution(mesh):
    in_specs = (P(("slab", "inline"), "xline", None), P(), P(), P(), P())
    out_specs = (
        P(("slab", "inline"), None, "xline", None),
        P("slab", None),
        P("slab", None),
        P("slab"),
    )
    return jax.shard_map(
        per_device, mesh=mesh, in_specs=in_specs, out_specs=out_specs, check_vma=False
    )
```
